32 devices in a mesh: scan: 8 (over z, x), col: 4 (over y, core).
Axes of the slice: x: 2, y: 2, z: 4, core: 2. Of those that a mesh axis runs over, the one named last changes fastest.
Arguments:
- object_field: float32 [2, 2048, 1024], P(None, 'scan', 'col'), may hold values from -6 to 6
- amplitudes: bfloat16 [64, 256, 256], P(('scan', 'col')), may hold values from 0.099609375 to 3
- positions: int32 [64, 2], P(('scan', 'col')), may hold values from 0 to 1792, as said below
- frame_count: int32 [32], P(('scan', 'col')), may hold values from 1 to 2, as said below
- coefficients: float32 [64, 4], P(('scan', 'col')), may hold values from -6 to 6
- probe_modes: float32 [4, 2, 256, 256], replicated, may hold values from -6 to 6
Outputs:
- refined_object: float32 [2, 2048, 1024], P(None, 'scan', 'col')
- refined_modes: float32 [4, 2, 256, 256], replicated
- refined_coefficients: float32 [64, 4], P(('scan', 'col'))
The draws below stay inside these ranges and needn't reach their ends.
Inputs may be any that keep to these rules, and one draw needn't show every extreme that they name: `positions`: frame g belongs to the device of index g // 2 along scan+col (scan slowest). Its top-left pixel lies in that device's block of 256 x 256 pixels, and its 256 x 256 patch lies inside the object. Entry d counts the live frames of the device of index d along scan+col: its first frame_count[d] slots are live, the rest are ignored. Some device has 2.
All inputs are finite; a program needn't handle non-finite values.
Results may differ from the reference program's by a relative error of at most 0.0058.
Values sent between devices are 32-bit elements; how exact they have to be, the bound alone decides.
A program may use at most 128 MiB of HBM per device.

```python
import math
import jax
import jax.numpy as jnp
from jax import lax

FS = 256
MODES = 4
ITERS = 2
F_DEV = 2
BH = 256
BW = 256
FRAMES = 64
OH = 2048
OW = 1024
N_SCAN = 8
N_COL = 4


def draw_positions(key, part):
    devices = N_SCAN * N_COL
    frames = F_DEV * devices
    slot_index = jnp.arange(frames, dtype=jnp.int32)
    device = slot_index // F_DEV
    scan_index = device // N_COL
    col_index = device % N_COL
    row_key, col_key = jax.random.split(jax.random.fold_in(key, 11))
    row_limit = jnp.where(scan_index < N_SCAN - 1, BH, BH - FS + 1).astype(jnp.int32)
    col_limit = jnp.where(col_index < N_COL - 1, BW, BW - FS + 1).astype(jnp.int32)
    row_offset = jax.random.randint(row_key, (frames,), 0, row_limit, dtype=jnp.int32)
    col_offset = jax.random.randint(col_key, (frames,), 0, col_limit, dtype=jnp.int32)
    return jnp.stack([scan_index * BH + row_offset, col_index * BW + col_offset], 1).astype(jnp.int32)


def draw_frame_count(key, part):
    devices = N_SCAN * N_COL
    pick_key, count_key = jax.random.split(jax.random.fold_in(key, 23))
    raw_draw = jax.random.randint(count_key, (devices,), 0, F_DEV, dtype=jnp.int32)
    counts = jnp.maximum(1, raw_draw * raw_draw // F_DEV)
    chosen = jax.random.randint(pick_key, (), 0, devices, dtype=jnp.int32)
    return jnp.where(jnp.arange(devices, dtype=jnp.int32) == chosen, F_DEV, counts).astype(jnp.int32)


def block_scale(stream_key, extent, shards, least, top_value):
    gain = 1.0
    for position, shards_of in shards:
        draws = jax.random.uniform(jax.random.fold_in(jax.random.fold_in(stream_key, 6), position), (shards_of,), jnp.float32, least / len(shards), top_value / len(shards))
        gain = gain * jnp.repeat(jnp.exp(draws), extent[position] // shards_of).reshape((-1,) + (1,) * (len(extent) - 1 - position))
    return gain


def scatter_about(stream_key, shape, deviation, most, pieces=(), kind=jnp.bfloat16):
    drawn = jax.random.normal(stream_key, shape, jnp.float32) * deviation
    if len(pieces) > 0:
        drawn = block_scale(stream_key, shape, pieces, -0.22, 0.18) * drawn
    return jnp.clip(drawn, min=-most, max=most).astype(kind)


def setup_inputs(seed: int = 0) -> dict:
    splits = jax.random.split(jax.random.key(seed), 7)
    object_field = scatter_about(splits[0], (2, OH, OW), 1.0, 6.0, ((1, 8), (2, 4)), jnp.float32)
    amplitudes = jnp.clip(jnp.exp(math.log(3.0) - 3.4051113 * jax.random.uniform(splits[1], (FRAMES, FS, FS), jnp.float32) ** block_scale(splits[1], (FRAMES, FS, FS), ((0, 32),), -0.2, 0.2)), 0.099609375, 3.0).astype(jnp.bfloat16)
    positions = draw_positions(jax.random.fold_in(splits[6], 71), 0)
    frame_count = draw_frame_count(jax.random.fold_in(splits[6], 71), 0)
    coefficients = scatter_about(splits[4], (FRAMES, MODES), 1.0, 6.0, ((0, 32),), jnp.float32)
    probe_modes = scatter_about(splits[5], (MODES, 2, FS, FS), 1.0, 6.0, (), jnp.float32)
    return dict(object_field=object_field, amplitudes=amplitudes, positions=positions, frame_count=frame_count, coefficients=coefficients, probe_modes=probe_modes)


highest = lax.Precision.HIGHEST

def make_tables(length):
    indices = jnp.arange(length, dtype=jnp.int32)
    phases = indices[:, None] * indices[None, :] % length
    angles = phases.astype(jnp.float32) * (2.0 * math.pi / length)
    factor = 1.0 / math.sqrt(length)
    cosine = jnp.cos(angles) * factor
    sine_table = jnp.sin(angles) * factor
    rows_table = jnp.concatenate([jnp.concatenate([cosine, sine_table], 1), jnp.concatenate([-sine_table, cosine], 1)], 0)
    cols_table = jnp.concatenate([jnp.concatenate([cosine, -sine_table], 1), jnp.concatenate([sine_table, cosine], 1)], 0)
    return (rows_table.astype(jnp.bfloat16), cols_table.astype(jnp.bfloat16))

def apply_transform(real_part, imag_part, first_table, second_table):
    length = real_part.shape[0]
    stacked = jnp.concatenate([real_part, imag_part], 0)
    halfway = jnp.dot(first_table, stacked, preferred_element_type=jnp.float32).astype(jnp.bfloat16)
    beside = jnp.concatenate([halfway[:length], halfway[length:]], 1)
    result = jnp.dot(beside, second_table, preferred_element_type=jnp.float32)
    return (result[:, :length], result[:, length:])

def frame_update(object_patch, probe_field, amplitude, rows_table, cols_table):
    probe_real = probe_field[0]
    probe_imag = probe_field[1]
    object_real = object_patch[0]
    object_imag = object_patch[1]
    exit_real = probe_real * object_real - probe_imag * object_imag
    exit_imag = probe_real * object_imag + probe_imag * object_real
    far_real, far_imag = apply_transform(exit_real.astype(jnp.bfloat16), exit_imag.astype(jnp.bfloat16), rows_table, cols_table)
    magnitude = jnp.sqrt(far_real * far_real + far_imag * far_imag)
    factor = amplitude.astype(jnp.float32) / jnp.maximum(magnitude, 0.5)
    new_real, new_imag = apply_transform((far_real * factor).astype(jnp.bfloat16), (far_imag * factor).astype(jnp.bfloat16), cols_table, rows_table)
    diff_real = new_real - exit_real
    diff_imag = new_imag - exit_imag
    update = jnp.stack([probe_real * diff_real + probe_imag * diff_imag, probe_real * diff_imag - probe_imag * diff_real, probe_real * probe_real + probe_imag * probe_imag])
    probe_step = jnp.stack([object_real * diff_real + object_imag * diff_imag, object_real * diff_imag - object_imag * diff_real])
    return (update, probe_step)

def gram_parts(flat_modes):
    real_plane = flat_modes[:, 0]
    imag_plane = flat_modes[:, 1]
    gram_real = jnp.dot(real_plane, real_plane.T, precision=highest, preferred_element_type=jnp.float32) + jnp.dot(imag_plane, imag_plane.T, precision=highest, preferred_element_type=jnp.float32)
    gram_imag = jnp.dot(real_plane, imag_plane.T, precision=highest, preferred_element_type=jnp.float32) - jnp.dot(imag_plane, real_plane.T, precision=highest, preferred_element_type=jnp.float32)
    return (gram_real, gram_imag)

def orthonormal(flat_modes, gram_real, gram_imag):
    mode_count = flat_modes.shape[0]
    upper_real = [[None] * mode_count for other in range(mode_count)]
    upper_imag = [[None] * mode_count for other in range(mode_count)]
    for right_index in range(mode_count):
        for left_index in range(right_index):
            sum_real = gram_real[left_index, right_index]
            sum_imag = gram_imag[left_index, right_index]
            for inner_index in range(left_index):
                first_real = upper_real[inner_index][left_index]
                first_imag = upper_imag[inner_index][left_index]
                second_real = upper_real[inner_index][right_index]
                second_imag = upper_imag[inner_index][right_index]
                sum_real = sum_real - (first_real * second_real + first_imag * second_imag)
                sum_imag = sum_imag - (first_real * second_imag - first_imag * second_real)
            upper_real[left_index][right_index] = sum_real / upper_real[left_index][left_index]
            upper_imag[left_index][right_index] = sum_imag / upper_real[left_index][left_index]
        diagonal = gram_real[right_index, right_index]
        for inner_index in range(right_index):
            entry_real = upper_real[inner_index][right_index]
            entry_imag = upper_imag[inner_index][right_index]
            diagonal = diagonal - (entry_real * entry_real + entry_imag * entry_imag)
        upper_real[right_index][right_index] = jnp.sqrt(diagonal)
    columns = []
    for right_index in range(mode_count):
        vector_real = flat_modes[right_index, 0]
        vector_imag = flat_modes[right_index, 1]
        for left_index in range(right_index):
            basis_real, basis_imag = columns[left_index]
            entry_real = upper_real[left_index][right_index]
            entry_imag = upper_imag[left_index][right_index]
            vector_real = vector_real - (entry_real * basis_real - entry_imag * basis_imag)
            vector_imag = vector_imag - (entry_real * basis_imag + entry_imag * basis_real)
        pivot = upper_real[right_index][right_index]
        columns.append((vector_real / pivot, vector_imag / pivot))
    return jnp.stack([jnp.stack([pair[0], pair[1]]) for pair in columns])

def reference(object_field, amplitudes, positions, frame_count, coefficients, probe_modes):
    frames = amplitudes.shape[0]
    length = amplitudes.shape[1]
    mode_count = probe_modes.shape[0]
    pixels = length * length
    root_total = math.sqrt(frames)
    rows_table, cols_table = make_tables(length)
    slot_index = jnp.arange(frames, dtype=jnp.int32)
    owner = (slot_index // F_DEV).astype(jnp.int32)
    live_mask = slot_index % F_DEV < frame_count[owner]
    anchor = jnp.zeros((), jnp.int32)
    for iteration in range(ITERS):
        current_object = object_field
        current_modes = probe_modes

        def visit(state, item):
            amplitude, offset, weights, alive = item

            def work(inner):
                totals, mode_terms = inner
                object_patch = lax.dynamic_slice(current_object, (anchor, offset[0], offset[1]), (2, length, length))
                probe_field = jnp.tensordot(weights, current_modes, axes=1, precision=highest)
                update, probe_step = frame_update(object_patch, probe_field, amplitude, rows_table, cols_table)
                window = lax.dynamic_slice(totals, (anchor, offset[0], offset[1]), (3, length, length))
                totals = lax.dynamic_update_slice(totals, window + update, (anchor, offset[0], offset[1]))
                mode_terms = mode_terms + weights[:, None, None, None] * probe_step[None]
                return ((totals, mode_terms), probe_step)

            def skip(inner):
                return (inner, jnp.zeros((2, length, length), jnp.float32))
            return lax.cond(alive, work, skip, state)
        initial = (jnp.zeros((3,) + object_field.shape[1:], jnp.float32), jnp.zeros((mode_count, 2, length, length), jnp.float32))
        (totals, mode_terms), stashed = lax.scan(visit, initial, (amplitudes, positions, coefficients, live_mask))
        object_field = object_field + totals[:2] / (totals[2] + 1.0)
        raised = (probe_modes + mode_terms / root_total).reshape(mode_count, 2, pixels)
        gram_real, gram_imag = gram_parts(raised)
        orthogonal = orthonormal(raised, gram_real / pixels, gram_imag / pixels)
        ortho_flat = orthogonal.reshape(mode_count, 2 * pixels)
        mixing = jnp.dot(probe_modes.reshape(mode_count, 2 * pixels), ortho_flat.T, precision=highest, preferred_element_type=jnp.float32) / pixels
        projected = jnp.dot(stashed.reshape(frames, 2 * pixels), ortho_flat.T, precision=highest, preferred_element_type=jnp.float32) / pixels
        refit = jnp.dot(coefficients, mixing, precision=highest, preferred_element_type=jnp.float32) + 0.5 * projected
        coefficients = jnp.where(live_mask[:, None], refit, coefficients)
        probe_modes = orthogonal.reshape(mode_count, 2, length, length)
    return (object_field, probe_modes, coefficients)
```

```python
import functools
import math

import jax
import jax.numpy as jnp
import ml_dtypes
import numpy as np
from jax import lax
from jax.experimental import pallas as pl
from jax.experimental.pallas import tpu as pltpu
from jax.sharding import PartitionSpec as P

ITERS = 2
CHUNKS = 4

VMEM = pl.BlockSpec(memory_space=pltpu.VMEM)
SMEM = pl.BlockSpec(memory_space=pltpu.SMEM)


def make_tables(length):
    indices = np.arange(length, dtype=np.int32)
    phases = indices[:, None] * indices[None, :] % length
    angles = phases.astype(np.float32) * np.float32(2.0 * math.pi / length)
    factor = np.float32(1.0 / math.sqrt(length))
    cosine = np.cos(angles) * factor
    sine = np.sin(angles) * factor
    rows_table = np.block([[cosine, sine], [-sine, cosine]])
    cols_table = np.block([[cosine, -sine], [sine, cosine]])
    return (rows_table.astype(ml_dtypes.bfloat16), cols_table.astype(ml_dtypes.bfloat16))


def apply_transform(stacked, first_table, second_table):
    length = stacked.shape[1]
    halfway = jnp.dot(first_table, stacked, preferred_element_type=jnp.float32).astype(jnp.bfloat16)
    beside = jnp.concatenate([halfway[:length], halfway[length:]], 1)
    return jnp.dot(beside, second_table, preferred_element_type=jnp.float32)


def bits_of(axis, count):
    return [(axis, 1 << b) for b in range(count.bit_length() - 1)]


def stream_orders(scan_count, col_count, units, again):
    scan, col = bits_of("scan", scan_count), bits_of("col", col_count)
    core, y, x, z, w = col[:1], col[1:], scan[:1], scan[1:3], scan[3:]
    if again:
        orders = [[core, z, y, x, w], [core, x, y, z, w], [core, y, z, x, w], [core, y, x, z, w]]
    else:
        orders = [[core, x, y, z, w], [core, y, x, z, w], [core, x, y, z, w], [core, y, x, z, w]]
    if units // (scan_count * col_count) < len(orders):
        orders = orders[1:3]
    return [[group for group in order if group] for order in orders]


def reach(device, source, target, send_sem, recv_sem):
    return pltpu.make_async_remote_copy(
        src_ref=source,
        dst_ref=target,
        send_sem=send_sem,
        recv_sem=recv_sem,
        device_id=device,
        device_id_type=pl.DeviceIdType.MESH,
    )


class Shift:
    def __init__(self, copy, sends, receives):
        self.copy, self.sends, self.receives = copy, sends, receives

    def start(self):
        pl.when(self.sends)(self.copy.start)

    def arrive(self):
        pl.when(self.receives)(self.copy.wait_recv)

    def leave(self):
        pl.when(self.sends)(self.copy.wait_send)


class Place:
    def __init__(self, scan_count, col_count):
        self.scan, self.col = lax.axis_index("scan"), lax.axis_index("col")
        self.right = (self.scan, lax.rem(self.col + 1, col_count))
        self.left = (self.scan, lax.rem(self.col + col_count - 1, col_count))
        self.down = (lax.rem(self.scan + 1, scan_count), self.col)
        self.up = (lax.rem(self.scan + scan_count - 1, scan_count), self.col)
        self.has_right, self.has_left = self.col < col_count - 1, self.col > 0
        self.has_down, self.has_up = self.scan < scan_count - 1, self.scan > 0

    def sides(self):
        return (
            (self.right, self.has_right), (self.left, self.has_left),
            (self.down, self.has_down), (self.up, self.has_up),
        )

    def bit(self, axis, bit):
        at = self.scan if axis == "scan" else self.col
        return at // bit % 2

    def index(self, group, flips):
        total = 0
        for b, (axis, bit) in enumerate(group):
            mine = self.bit(axis, bit)
            total = total + (1 - mine if flips >> b & 1 else mine) * (1 << b)
        return total

    def partner(self, group, flips):
        scan, col = self.scan, self.col
        for b, (axis, bit) in enumerate(group):
            if flips >> b & 1:
                step = bit - 2 * bit * self.bit(axis, bit)
                if axis == "scan":
                    scan = scan + step
                else:
                    col = col + step
        return (scan, col)

    def greet(self, groups):
        barrier = pltpu.get_barrier_semaphore()
        partners = [self.partner(group, flips) for group in groups for flips in range(1, 1 << len(group))]

        def signal(device):
            pl.semaphore_signal(barrier, inc=1, device_id=device, device_id_type=pl.DeviceIdType.MESH)

        for device in partners:
            signal(device)
        for device, there in self.sides():
            pl.when(there)(functools.partial(signal, device))
        present = [there.astype(jnp.int32) for _, there in self.sides()]
        pl.semaphore_wait(barrier, len(partners) + sum(present))


class Stream:
    def __init__(self, place, order, base, count, terms, landed, send_sems, recv_sems):
        self.place, self.order = place, order
        self.terms, self.landed = terms, landed
        self.send_sems, self.recv_sems = send_sems, recv_sems
        self.bases, self.counts, self.slots, self.marks = [base], [count], [], []
        self.copies = {}
        slot, mark = base, 0
        for group in order:
            members = 1 << len(group)
            part = self.counts[-1] // members
            self.bases.append(self.bases[-1] + place.index(group, 0) * part)
            self.counts.append(part)
            self.slots.append(slot)
            self.marks.append(mark)
            slot += part * (members - 1)
            mark += members - 1
        self.total = mark

    def flips(self, s):
        return range(1, 1 << len(self.order[s]))

    def scatter(self, s):
        part = self.counts[s + 1]
        for flips in self.flips(s):
            group = self.order[s]
            source = self.terms.at[pl.ds(self.bases[s] + self.place.index(group, flips) * part, part)]
            target = self.landed.at[pl.ds(self.slots[s] + (flips - 1) * part, part)]
            at = self.marks[s] + flips - 1
            copy = reach(
                self.place.partner(group, flips), source, target, self.send_sems.at[at], self.recv_sems.at[at]
            )
            copy.start()
            self.copies["scatter", s, flips] = copy

    def gathered(self, s):
        part = self.counts[s + 1]
        at = pl.ds(self.bases[s + 1], part)
        value = self.terms[at]
        for flips in self.flips(s):
            self.copies["scatter", s, flips].wait_recv()
            value = value + self.landed[pl.ds(self.slots[s] + (flips - 1) * part, part)]
        return at, value

    def spread(self, s, raised):
        piece = raised.at[pl.ds(self.bases[s + 1], self.counts[s + 1])]
        for flips in self.flips(s):
            at = self.total + self.marks[s] + flips - 1
            copy = reach(
                self.place.partner(self.order[s], flips), piece, piece,
                self.send_sems.at[at], self.recv_sems.at[at],
            )
            copy.start()
            self.copies["gather", s, flips] = copy

    def arrived(self, s):
        for flips in self.flips(s):
            self.copies["gather", s, flips].wait_recv()

    def leave(self):
        for copy in self.copies.values():
            copy.wait_send()


class Halo:
    def __init__(self, place, wide, tiles, width, send_sems, recv_sems):
        rows = tiles // CHUNKS
        near, far = pl.ds(0, width), pl.ds(width, width)
        self.up, self.side, self.corner = [], [], []
        for q in range(CHUNKS):
            top, low = pl.ds(q * rows, rows), pl.ds(tiles + q * rows, rows)
            self.up.append(Shift(
                reach(place.up, wide.at[:, top, :, near], wide.at[:, low, :, near], send_sems.at[0, q], recv_sems.at[0, q]),
                place.has_up, place.has_down,
            ))
            self.side.append(Shift(
                reach(place.left, wide.at[:, top, :, near], wide.at[:, top, :, far], send_sems.at[1, q], recv_sems.at[1, q]),
                place.has_left, place.has_right,
            ))
            self.corner.append(Shift(
                reach(place.left, wide.at[:, low, :, near], wide.at[:, low, :, far], send_sems.at[2, q], recv_sems.at[2, q]),
                place.has_left, place.has_right,
            ))

    def begin(self, q):
        self.up[q].start()
        self.side[q].start()

    def turn(self, q):
        self.up[q].arrive()
        self.corner[q].start()

    def end(self):
        for shift in self.side + self.corner:
            shift.arrive()

    def leave(self):
        for shift in self.up + self.side + self.corner:
            shift.leave()


def step_kernel(
    scan_count, col_count, mode_count, root_total,
    count, positions, first_weights, field, amplitudes, first_modes, rows_table, cols_table,
    new_object, new_modes, new_weights,
    wide, totals, shelf, probes, grads, terms, landed, raised, middle_modes, middle_weights,
    sideways, fallen, bottom,
    stream_send, stream_recv, halo_send, halo_recv, side_send, side_recv,
):
    tiles, _, width = field.shape[1:]
    height = 8 * tiles
    frames, length = amplitudes.shape[:2]
    planes = 2 * mode_count
    blocks = length // 8
    units = blocks * planes
    pixels = float(length * length)
    full_width = width + length
    rows_of_chunk = tiles // CHUNKS
    place = Place(scan_count, col_count)
    near, far = pl.ds(0, width), pl.ds(width, width)
    top, low = pl.ds(0, tiles), pl.ds(tiles, tiles)
    pairs = [(i, j) for j in range(mode_count) for i in range(j + 1)]
    strict = [(i, j) for i, j in pairs if i < j]
    leaving = []

    def chunk(q, offset=0):
        return pl.ds(offset + q * rows_of_chunk, rows_of_chunk)

    def block_rows(block):
        return pl.ds(pl.multiple_of(block * 8, 8), 8)

    wide[0, :, :tiles, :, :width] = field[...]

    @pl.when(jnp.logical_not(place.has_left))
    def _():
        sideways[...] = jnp.zeros_like(sideways)

    @pl.when(jnp.logical_not(place.has_up))
    def _():
        fallen[...] = jnp.zeros_like(fallen)

    every_order = [stream_orders(scan_count, col_count, units, i < ITERS - 1) for i in range(ITERS)]
    place.greet(every_order[0][0])
    halos = [
        Halo(place, wide.at[i], tiles, width, halo_send.at[i], halo_recv.at[i]) for i in range(ITERS)
    ]
    for q in range(CHUNKS):
        halos[0].begin(q)
    blank = jnp.zeros((blocks, 8, full_width), jnp.float32)
    shelf[:blocks] = blank
    shelf[blocks + 1:2 * blocks + 1] = blank
    shelf[2 * blocks:] = blank

    def live(slot):
        return slot < count[0]

    def inside(value, limit):
        return jnp.minimum(jnp.maximum(value, 0), limit - 1)

    corners = [
        (
            inside(positions[g, 0] - place.scan * height, height),
            inside(positions[g, 1] - place.col * width, width),
        )
        for g in range(frames)
    ]

    def spot(slot):
        row, col = corners[slot]
        start = lax.div(row, 8)
        return start, row - 8 * start, col

    def lay(slot, piece):
        start, rest, col = spot(slot)
        band = jnp.concatenate([piece, jnp.zeros((8, length), jnp.float32)], 0)
        band = pltpu.roll(band, rest, 0)
        band = jnp.concatenate([band, jnp.zeros((length + 8, width), jnp.float32)], 1)
        band = pltpu.roll(band, col, 1)
        shelf[blocks:2 * blocks + 1] = band.reshape(blocks + 1, 8, full_width)
        return blocks - start

    def put(i, plane, slot, piece):
        start = lay(slot, piece)

        def move(n, carry):
            value = shelf[start + n]
            totals[i, plane, n] = value if slot == 0 else totals[i, plane, n] + value
            return carry

        lax.fori_loop(0, tiles + blocks, move, 0, unroll=8)

    def cut(i, plane, slot):
        start, rest, col = spot(slot)
        band = jnp.concatenate([wide[i, plane, start + n] for n in range(blocks + 1)], 0)
        band = pltpu.roll(band, lax.rem(full_width - col, full_width), 1)[:, :length]
        return pltpu.roll(band, lax.rem(length + 8 - rest, length + 8), 0)[:length]

    def masked(weights):
        table = [[weights[g:g + 1, k:k + 1] for k in range(mode_count)] for g in range(frames)]
        return [[jnp.where(live(g), w, 0.0) for w in row] for g, row in enumerate(table)]

    def wave(weights, tiles):
        out = []
        for g in range(frames):
            for part in range(2):
                value = weights[g][0] * tiles[part]
                for k in range(1, mode_count):
                    value = value + weights[g][k] * tiles[2 * k + part]
                out.append(value)
        return out

    def fold(value):
        total = value[:, :128]
        for at in range(128, length, 128):
            total = total + value[:, at:at + 128]
        return total

    def whole(value):
        return jnp.sum(jnp.sum(value, 0, keepdims=True), 1, keepdims=True)

    def run_frame(i, g):
        object_real = cut(i, 0, g)
        object_imag = cut(i, 1, g)
        probe_real, probe_imag = probes[g, 0], probes[g, 1]
        exit_real = probe_real * object_real - probe_imag * object_imag
        exit_imag = probe_real * object_imag + probe_imag * object_real
        stacked = jnp.concatenate([exit_real, exit_imag], 0).astype(jnp.bfloat16)
        far_field = apply_transform(stacked, rows_table[...], cols_table[...])
        far_real, far_imag = far_field[:, :length], far_field[:, length:]
        magnitude = jnp.sqrt(far_real * far_real + far_imag * far_imag)
        factor = amplitudes[g].astype(jnp.float32) / jnp.maximum(magnitude, 0.5)
        scaled = jnp.concatenate([far_real * factor, far_imag * factor], 0).astype(jnp.bfloat16)
        back = apply_transform(scaled, cols_table[...], rows_table[...])
        diff_real = back[:, :length] - exit_real
        diff_imag = back[:, length:] - exit_imag
        grads[g, 0] = object_real * diff_real + object_imag * diff_imag
        grads[g, 1] = object_real * diff_imag - object_imag * diff_real
        put(i, 0, g, probe_real * diff_real + probe_imag * diff_imag)
        put(i, 1, g, probe_real * diff_imag - probe_imag * diff_real)

    weights = masked(first_weights)

    def first_wave(block, carry):
        rows = block_rows(block)
        values = wave(weights, [first_modes[p, rows, :] for p in range(planes)])
        for at, value in enumerate(values):
            probes[at // 2, at % 2, rows, :] = value
        return carry

    lax.fori_loop(0, blocks, first_wave, 0)

    for i in range(ITERS):
        again = i < ITERS - 1
        modes = first_modes if i == 0 else middle_modes
        kept_weights = first_weights if i == 0 else middle_weights

        def rightward(at, source, target):
            copy = reach(place.right, source, target, side_send.at[i, at], side_recv.at[i, at])
            return Shift(copy, place.has_right, place.has_left)

        def downward(at, source, target):
            copy = reach(place.down, source, target, side_send.at[i, at], side_recv.at[i, at])
            return Shift(copy, place.has_down, place.has_up)

        pair = pl.ds(0, 2)
        low_rights = [
            rightward(q, totals.at[i, pair, chunk(q, tiles), :, far], sideways.at[i, pair, chunk(q, tiles)])
            for q in range(CHUNKS)
        ]
        top_rights = [
            rightward(CHUNKS + q, totals.at[i, pair, chunk(q), :, far], sideways.at[i, pair, chunk(q)])
            for q in range(CHUNKS)
        ]
        downs = [
            downward(2 * CHUNKS + q, bottom.at[i, pair, chunk(q)], fallen.at[i, pair, chunk(q)])
            for q in range(CHUNKS)
        ]
        low_den = rightward(3 * CHUNKS, totals.at[i, 2, low, :, far], sideways.at[i, 2, low])
        top_den = rightward(3 * CHUNKS + 1, totals.at[i, 2, top, :, far], sideways.at[i, 2, top])
        down_den = downward(3 * CHUNKS + 2, bottom.at[i, 2], fallen.at[i, 2])
        leaving += low_rights + top_rights + downs + [low_den, top_den, down_den]

        for g in range(frames):
            put(i, 2, g, probes[g, 0] * probes[g, 0] + probes[g, 1] * probes[g, 1])
        low_den.start()
        top_den.start()
        if i == 0:
            for q in range(CHUNKS):
                halos[0].turn(q)
        halos[i].end()
        for g in range(frames):
            run_frame(i, g)
            if g == 0:
                low_den.arrive()
                bottom[i, 2] = totals[i, 2, tiles:, :, :width] + sideways[i, 2, tiles:]
                down_den.start()
        for q in range(CHUNKS):
            low_rights[q].start()

        orders = every_order[i]
        stages = len(orders[0])
        share = units // len(orders)
        streams = [
            Stream(
                place, order, t * share, share, terms.at[i], landed.at[i],
                stream_send.at[i, t], stream_recv.at[i, t],
            )
            for t, order in enumerate(orders)
        ]
        leaving += streams

        def term_step(block, carry):
            rows = block_rows(block)
            tiles = [grads[g, part, rows, :] for g in range(frames) for part in range(2)]
            for k in range(mode_count):
                for part in range(2):
                    value = weights[0][k] * tiles[part]
                    for g in range(1, frames):
                        value = value + weights[g][k] * tiles[2 * g + part]
                    terms[i, block * planes + 2 * k + part] = value
            return carry

        for t, stream in enumerate(streams):
            per = share // planes
            lax.fori_loop(t * per, (t + 1) * per, term_step, 0)
            stream.scatter(0)
        for q in range(CHUNKS):
            top_rights[q].start()

        def finish_scatter(t, s):
            stream = streams[t]
            at, value = stream.gathered(s)
            if s < stages - 1:
                terms[i, at] = value
                stream.scatter(s + 1)
                return
            first = stream.bases[s + 1]
            for n in range(stream.counts[s + 1]):
                unit = first + n
                kept = modes[unit % planes, block_rows(unit // planes), :]
                raised[i, unit] = kept + value[n] / root_total
            stream.spread(s, raised.at[i])

        sums = [jnp.zeros((8, 128), jnp.float32)] * (len(pairs) + len(strict) + 2 * mode_count * frames)

        def fit_step(block, sums):
            rows = block_rows(block)
            tiles = [raised[i, block * planes + p] for p in range(planes)]
            real, imag = tiles[0::2], tiles[1::2]
            terms_ = [fold(real[a] * real[b] + imag[a] * imag[b]) for a, b in pairs]
            terms_ += [fold(real[a] * imag[b] - imag[a] * real[b]) for a, b in strict]
            for g in range(frames):
                held_real = probes[g, 0, rows, :] + 0.5 * grads[g, 0, rows, :]
                held_imag = probes[g, 1, rows, :] + 0.5 * grads[g, 1, rows, :]
                for a in range(mode_count):
                    terms_.append(fold(real[a] * held_real + imag[a] * held_imag))
                    terms_.append(fold(real[a] * held_imag - imag[a] * held_real))
            return tuple(a + b for a, b in zip(sums, terms_))

        def finish_gather(t, s):
            nonlocal sums
            streams[t].arrived(s)
            if s > 0:
                streams[t].spread(s - 1, raised.at[i])
            else:
                per = share // planes
                sums = lax.fori_loop(t * per, (t + 1) * per, fit_step, tuple(sums))

        def drop(q):
            low_rights[q].arrive()
            bottom[i, :2, chunk(q)] = totals[i, :2, chunk(q, tiles), :, near] + sideways[i, :2, chunk(q, tiles)]
            downs[q].start()

        def renew(q):
            if q == 0:
                top_den.arrive()
                down_den.arrive()
            top_rights[q].arrive()
            downs[q].arrive()
            update = [
                totals[i, p, chunk(q), :, near] + sideways[i, p, chunk(q)] + fallen[i, p, chunk(q)]
                for p in range(3)
            ]
            scale = 1.0 / (update[2] + 1.0)
            for p in range(2):
                value = wide[i, p, chunk(q), :, near] + update[p] * scale
                if again:
                    wide[i + 1, p, chunk(q), :, near] = value
                else:
                    new_object[p, chunk(q)] = value
            if again:
                halos[i + 1].begin(q)

        def turn(q):
            if again:
                halos[i + 1].turn(q)

        steps = [functools.partial(finish_scatter, t, s) for s in range(stages) for t in range(len(streams))]
        steps += [
            functools.partial(finish_gather, t, s)
            for s in range(stages - 1, -1, -1) for t in range(len(streams))
        ]
        if again:
            marks = [(drop, (4, 4, 6, 6)), (renew, (9, 11, 13, 15)), (turn, (18, 21, 24, 27))]
        else:
            marks = [(drop, (4, 4, 6, 6)), (renew, (13, 16, 19, 22)), (turn, (32, 32, 32, 32))]
        for n, step in enumerate(steps):
            for task, whens in marks:
                for q, when in enumerate(whens):
                    if when * len(steps) // 32 == n:
                        task(q)
            step()
        for task, whens in marks:
            for q, when in enumerate(whens):
                if when * len(steps) // 32 >= len(steps):
                    task(q)

        totals_of = [whole(s) / pixels for s in sums]
        gram_real = dict(zip(pairs, totals_of))
        gram_imag = dict(zip(strict, totals_of[len(pairs):]))
        upper_real, upper_imag = {}, {}
        for b in range(mode_count):
            for a in range(b):
                sum_real, sum_imag = gram_real[a, b], gram_imag[a, b]
                for k in range(a):
                    r, s, u, v = upper_real[k, a], upper_imag[k, a], upper_real[k, b], upper_imag[k, b]
                    sum_real = sum_real - (r * u + s * v)
                    sum_imag = sum_imag - (r * v - s * u)
                upper_real[a, b] = sum_real / upper_real[a, a]
                upper_imag[a, b] = sum_imag / upper_real[a, a]
            diagonal = gram_real[b, b]
            for k in range(b):
                diagonal = diagonal - (upper_real[k, b] * upper_real[k, b] + upper_imag[k, b] * upper_imag[k, b])
            upper_real[b, b] = jnp.sqrt(diagonal)
        inverse = {b: 1.0 / upper_real[b, b] for b in range(mode_count)}

        refit_weights = []
        at = len(pairs) + len(strict)
        for g in range(frames):
            inner = []
            for k in range(mode_count):
                real, imag = totals_of[at], totals_of[at + 1]
                at += 2
                for a in range(k):
                    r, s, u, v = upper_real[a, k], upper_imag[a, k], inner[a][0], inner[a][1]
                    real = real - (r * u + s * v)
                    imag = imag - (r * v - s * u)
                inner.append((real * inverse[k], imag * inverse[k]))
            refit_weights.append([
                jnp.where(live(g), inner[k][0], kept_weights[g:g + 1, k:k + 1]) for k in range(mode_count)
            ])
        target_weights = middle_weights if again else new_weights
        for g in range(frames):
            for k in range(mode_count):
                target_weights[g:g + 1, k:k + 1] = refit_weights[g][k]
        weights = [[jnp.where(live(g), w, 0.0) for w in row] for g, row in enumerate(refit_weights)]
        target_modes = middle_modes if again else new_modes

        def spread_out(value):
            return jnp.broadcast_to(value, (8, length))

        upper_real = {p: spread_out(v) for p, v in upper_real.items() if p[0] < p[1]}
        upper_imag = {p: spread_out(v) for p, v in upper_imag.items()}
        inverse = {p: spread_out(v) for p, v in inverse.items()}
        wave_weights = [[spread_out(w) for w in row] for row in weights]

        def basis_step(block, carry):
            rows = block_rows(block)
            basis = []
            for b in range(mode_count):
                real, imag = raised[i, block * planes + 2 * b], raised[i, block * planes + 2 * b + 1]
                for a in range(b):
                    r, s = upper_real[a, b], upper_imag[a, b]
                    u, v = basis[2 * a], basis[2 * a + 1]
                    real = real - (r * u - s * v)
                    imag = imag - (r * v + s * u)
                basis += [real * inverse[b], imag * inverse[b]]
            for p in range(planes):
                target_modes[p, rows, :] = basis[p]
            if again:
                for n, value in enumerate(wave(wave_weights, basis)):
                    probes[n // 2, n % 2, rows, :] = value
            return carry

        lax.fori_loop(0, blocks, basis_step, 0)

    for item in leaving + halos:
        item.leave()


def shape(*dims):
    return jax.ShapeDtypeStruct(dims, jnp.float32)


def on_device(object_field, amplitudes, positions, frame_count, coefficients, probe_modes):
    frames, length = amplitudes.shape[:2]
    mode_count = probe_modes.shape[0]
    planes = 2 * mode_count
    height, width = object_field.shape[1:]
    scan_count = lax.axis_size("scan")
    col_count = lax.axis_size("col")
    root_total = math.sqrt(frames * scan_count * col_count)
    rows_table, cols_table = make_tables(length)
    tiles, blocks = height // 8, length // 8
    full_width = width + length
    units = planes * blocks
    order = stream_orders(scan_count, col_count, units, True)[0]
    partners = 2 * sum((1 << len(group)) - 1 for group in order)

    def vmem(*dims):
        return pltpu.VMEM(dims, jnp.float32)

    stream_sems = pltpu.SemaphoreType.DMA((ITERS, 4, partners))
    halo_sems = pltpu.SemaphoreType.DMA((ITERS, 3, CHUNKS))
    side_sems = pltpu.SemaphoreType.DMA((ITERS, 3 * CHUNKS + 3))
    new_object, modes, weights = pl.pallas_call(
        functools.partial(step_kernel, scan_count, col_count, mode_count, root_total),
        name="reconstruct",
        out_shape=(shape(2, tiles, 8, width), shape(planes, length, length), shape(frames, mode_count)),
        in_specs=[SMEM] * 2 + [VMEM] * 6,
        out_specs=(VMEM,) * 3,
        scratch_shapes=[
            vmem(ITERS, 2, tiles + blocks, 8, full_width),
            vmem(ITERS, 3, tiles + blocks, 8, full_width),
            vmem(3 * blocks, 8, full_width),
            vmem(frames, 2, length, length),
            vmem(frames, 2, length, length),
            vmem(ITERS, units, 8, length),
            vmem(ITERS, units, 8, length),
            vmem(ITERS, units, 8, length),
            vmem(planes, length, length),
            vmem(frames, mode_count),
            vmem(ITERS, 3, tiles + blocks, 8, width),
            vmem(ITERS, 3, tiles, 8, width),
            vmem(ITERS, 3, tiles, 8, width),
            stream_sems, stream_sems, halo_sems, halo_sems, side_sems, side_sems,
        ],
        compiler_params=pltpu.CompilerParams(
            collective_id=0, has_side_effects=True, vmem_limit_bytes=60 * 2**20
        ),
        cost_estimate=pl.CostEstimate(flops=5 * 10**9, bytes_accessed=10**7, transcendentals=0),
    )(
        frame_count, positions, coefficients, object_field.reshape(2, tiles, 8, width), amplitudes,
        probe_modes.reshape(planes, length, length), rows_table, cols_table,
    )
    return (new_object.reshape(object_field.shape), modes.reshape(probe_modes.shape), weights)


def solution(mesh):
    placed = (
        P(None, "scan", "col"),
        P(("scan", "col"), None, None),
        P(("scan", "col"), None),
        P(("scan", "col")),
        P(("scan", "col"), None),
        P(),
    )
    return jax.shard_map(
        on_device,
        mesh=mesh,
        in_specs=placed,
        out_specs=(P(None, "scan", "col"), P(), P(("scan", "col"), None)),
        check_vma=False,
    )
```

```python
import functools
import math

import jax
import jax.numpy as jnp
import ml_dtypes
import numpy as np
from jax import lax
from jax.experimental import pallas as pl
from jax.experimental.pallas import tpu as pltpu
from jax.sharding import PartitionSpec as P

ITERS = 2
CHUNKS = 4

VMEM = pl.BlockSpec(memory_space=pltpu.VMEM)
SMEM = pl.BlockSpec(memory_space=pltpu.SMEM)
ANY = pl.BlockSpec(memory_space=pl.ANY)


def make_tables(length):
    indices = np.arange(length, dtype=np.int32)
    phases = indices[:, None] * indices[None, :] % length
    angles = phases.astype(np.float32) * np.float32(2.0 * math.pi / length)
    factor = np.float32(1.0 / math.sqrt(length))
    cosine = np.cos(angles) * factor
    sine = np.sin(angles) * factor
    rows_table = np.block([[cosine, sine], [-sine, cosine]])
    cols_table = np.block([[cosine, -sine], [sine, cosine]])
    return (rows_table.astype(ml_dtypes.bfloat16), cols_table.astype(ml_dtypes.bfloat16))


def apply_transform(stacked, first_table, second_table):
    length = stacked.shape[1]
    halfway = jnp.dot(first_table, stacked, preferred_element_type=jnp.float32).astype(jnp.bfloat16)
    beside = jnp.concatenate([halfway[:length], halfway[length:]], 1)
    return jnp.dot(beside, second_table, preferred_element_type=jnp.float32)


def bits_of(axis, count):
    return [(axis, 1 << b) for b in range(count.bit_length() - 1)]


def stream_orders(scan_count, col_count, units, again):
    scan, col = bits_of("scan", scan_count), bits_of("col", col_count)
    core, y, x, z, w = col[:1], col[1:], scan[:1], scan[1:3], scan[3:]
    if again:
        orders = [[core, z, y, x, w], [core, x, y, z, w], [core, y, z, x, w], [core, y, x, z, w]]
    else:
        orders = [[core, x, y, z, w], [core, y, x, z, w], [core, x, y, z, w], [core, y, x, z, w]]
    if units // (scan_count * col_count) < len(orders):
        orders = orders[1:3]
    return [[group for group in order if group] for order in orders]


def reach(device, source, target, send_sem, recv_sem):
    return pltpu.make_async_remote_copy(
        src_ref=source,
        dst_ref=target,
        send_sem=send_sem,
        recv_sem=recv_sem,
        device_id=device,
        device_id_type=pl.DeviceIdType.MESH,
    )


class Shift:
    def __init__(self, copy, sends, receives):
        self.copy, self.sends, self.receives = copy, sends, receives

    def start(self):
        pl.when(self.sends)(self.copy.start)

    def arrive(self):
        pl.when(self.receives)(self.copy.wait_recv)

    def leave(self):
        pl.when(self.sends)(self.copy.wait_send)


class Place:
    def __init__(self, scan_count, col_count):
        self.scan, self.col = lax.axis_index("scan"), lax.axis_index("col")
        self.right = (self.scan, lax.rem(self.col + 1, col_count))
        self.left = (self.scan, lax.rem(self.col + col_count - 1, col_count))
        self.down = (lax.rem(self.scan + 1, scan_count), self.col)
        self.up = (lax.rem(self.scan + scan_count - 1, scan_count), self.col)
        self.has_right, self.has_left = self.col < col_count - 1, self.col > 0
        self.has_down, self.has_up = self.scan < scan_count - 1, self.scan > 0

    def sides(self):
        return (
            (self.right, self.has_right), (self.left, self.has_left),
            (self.down, self.has_down), (self.up, self.has_up),
        )

    def bit(self, axis, bit):
        at = self.scan if axis == "scan" else self.col
        return at // bit % 2

    def index(self, group, flips):
        total = 0
        for b, (axis, bit) in enumerate(group):
            mine = self.bit(axis, bit)
            total = total + (1 - mine if flips >> b & 1 else mine) * (1 << b)
        return total

    def partner(self, group, flips):
        scan, col = self.scan, self.col
        for b, (axis, bit) in enumerate(group):
            if flips >> b & 1:
                step = bit - 2 * bit * self.bit(axis, bit)
                if axis == "scan":
                    scan = scan + step
                else:
                    col = col + step
        return (scan, col)

    def greet(self, groups):
        barrier = pltpu.get_barrier_semaphore()
        partners = [self.partner(group, flips) for group in groups for flips in range(1, 1 << len(group))]

        def signal(device):
            pl.semaphore_signal(barrier, inc=1, device_id=device, device_id_type=pl.DeviceIdType.MESH)

        for device in partners:
            signal(device)
        for device, there in self.sides():
            pl.when(there)(functools.partial(signal, device))
        present = [there.astype(jnp.int32) for _, there in self.sides()]
        pl.semaphore_wait(barrier, len(partners) + sum(present))


class Stream:
    def __init__(self, place, order, base, count, terms, landed, send_sems, recv_sems):
        self.place, self.order = place, order
        self.terms, self.landed = terms, landed
        self.send_sems, self.recv_sems = send_sems, recv_sems
        self.bases, self.counts, self.slots, self.marks = [base], [count], [], []
        self.copies = {}
        slot, mark = base, 0
        for group in order:
            members = 1 << len(group)
            part = self.counts[-1] // members
            self.bases.append(self.bases[-1] + place.index(group, 0) * part)
            self.counts.append(part)
            self.slots.append(slot)
            self.marks.append(mark)
            slot += part * (members - 1)
            mark += members - 1
        self.total = mark

    def flips(self, s):
        return range(1, 1 << len(self.order[s]))

    def scatter(self, s):
        part = self.counts[s + 1]
        for flips in self.flips(s):
            group = self.order[s]
            source = self.terms.at[pl.ds(self.bases[s] + self.place.index(group, flips) * part, part)]
            target = self.landed.at[pl.ds(self.slots[s] + (flips - 1) * part, part)]
            at = self.marks[s] + flips - 1
            copy = reach(
                self.place.partner(group, flips), source, target, self.send_sems.at[at], self.recv_sems.at[at]
            )
            copy.start()
            self.copies["scatter", s, flips] = copy

    def offer(self, grads, mates, first, half):
        group = self.order[0]
        start = (first + self.place.index(group, 1) * half) * 8
        rows = pl.ds(pl.multiple_of(start, 8), half * 8)
        copy = reach(
            self.place.partner(group, 1), grads.at[:, :, rows, :], mates.at[:, :, rows, :],
            self.send_sems.at[0], self.recv_sems.at[0],
        )
        copy.start()
        self.copies["scatter", 0, 1] = copy

    def gathered(self, s):
        part = self.counts[s + 1]
        at = pl.ds(self.bases[s + 1], part)
        value = self.terms[at]
        for flips in self.flips(s):
            self.copies["scatter", s, flips].wait_recv()
            value = value + self.landed[pl.ds(self.slots[s] + (flips - 1) * part, part)]
        return at, value

    def spread(self, s, raised):
        piece = raised.at[pl.ds(self.bases[s + 1], self.counts[s + 1])]
        for flips in self.flips(s):
            at = self.total + self.marks[s] + flips - 1
            copy = reach(
                self.place.partner(self.order[s], flips), piece, piece,
                self.send_sems.at[at], self.recv_sems.at[at],
            )
            copy.start()
            self.copies["gather", s, flips] = copy

    def arrived(self, s):
        for flips in self.flips(s):
            self.copies["gather", s, flips].wait_recv()

    def leave(self):
        for copy in self.copies.values():
            copy.wait_send()


class Halo:
    def __init__(self, place, wide, tiles, width, send_sems, recv_sems):
        rows = tiles // CHUNKS
        near, far = pl.ds(0, width), pl.ds(width, width)
        self.up, self.side, self.corner = [], [], []
        for q in range(CHUNKS):
            top, low = pl.ds(q * rows, rows), pl.ds(tiles + q * rows, rows)
            self.up.append(Shift(
                reach(place.up, wide.at[:, top, :, near], wide.at[:, low, :, near], send_sems.at[0, q], recv_sems.at[0, q]),
                place.has_up, place.has_down,
            ))
            self.side.append(Shift(
                reach(place.left, wide.at[:, top, :, near], wide.at[:, top, :, far], send_sems.at[1, q], recv_sems.at[1, q]),
                place.has_left, place.has_right,
            ))
            self.corner.append(Shift(
                reach(place.left, wide.at[:, low, :, near], wide.at[:, low, :, far], send_sems.at[2, q], recv_sems.at[2, q]),
                place.has_left, place.has_right,
            ))

    def begin(self, q):
        self.up[q].start()
        self.side[q].start()

    def turn(self, q):
        self.up[q].arrive()
        self.corner[q].start()

    def end(self):
        for shift in self.side + self.corner:
            shift.arrive()

    def leave(self):
        for shift in self.up + self.side + self.corner:
            shift.leave()


def step_kernel(
    scan_count, col_count, mode_count, root_total,
    count, positions, first_weights, field, far_amplitudes, far_modes, far_rows, far_cols,
    new_object, last_raised, factors, new_weights,
    amplitudes, first_modes, rows_table, cols_table, input_sems,
    wide, totals, held, probes, grads, mates, given, taken, terms, landed, raised, middle_modes, middle_weights,
    sideways, fallen, bottom,
    stream_send, stream_recv, halo_send, halo_recv, side_send, side_recv,
):
    tiles, _, width = field.shape[1:]
    height = 8 * tiles
    frames, length = amplitudes.shape[:2]
    planes = 2 * mode_count
    blocks = length // 8
    units = blocks * planes
    pixels = float(length * length)
    full_width = width + length
    rows_of_chunk = tiles // CHUNKS
    place = Place(scan_count, col_count)
    near, far = pl.ds(0, width), pl.ds(width, width)
    top, low = pl.ds(0, tiles), pl.ds(tiles, tiles)
    pairs = [(i, j) for j in range(mode_count) for i in range(j + 1)]
    strict = [(i, j) for i, j in pairs if i < j]
    leaving = []
    ups = [raised.at[i] for i in range(ITERS - 1)] + [last_raised]

    def chunk(q, offset=0):
        return pl.ds(offset + q * rows_of_chunk, rows_of_chunk)

    def block_rows(block):
        return pl.ds(pl.multiple_of(block * 8, 8), 8)

    loads = [
        pltpu.make_async_copy(source, target, input_sems.at[n])
        for n, (source, target) in enumerate((
            (far_modes, first_modes), (far_rows, rows_table), (far_cols, cols_table), (far_amplitudes, amplitudes),
        ))
    ]
    for load in loads:
        load.start()

    wide[0, :, :tiles, :, :width] = field[...]

    @pl.when(jnp.logical_not(place.has_left))
    def _():
        sideways[...] = jnp.zeros_like(sideways)

    @pl.when(jnp.logical_not(place.has_up))
    def _():
        fallen[...] = jnp.zeros_like(fallen)

    every_order = [stream_orders(scan_count, col_count, units, i < ITERS - 1) for i in range(ITERS)]
    place.greet(every_order[0][0])
    halos = [
        Halo(place, wide.at[i], tiles, width, halo_send.at[i], halo_recv.at[i]) for i in range(ITERS)
    ]
    for q in range(CHUNKS):
        halos[0].begin(q)
    def live(slot):
        return slot < count[0]

    def inside(value, limit):
        return jnp.minimum(jnp.maximum(value, 0), limit - 1)

    corners = [
        (
            inside(positions[g, 0] - place.scan * height, height),
            inside(positions[g, 1] - place.col * width, width),
        )
        for g in range(frames)
    ]

    def turned(piece, row, col):
        return pltpu.roll(pltpu.roll(piece, row, 0), col, 1)

    def hold(plane, slot, piece):
        row, col = corners[slot]
        held[plane, slot] = turned(piece, row, col).reshape(tiles, 8, width)

    lanes = lax.broadcasted_iota(jnp.int32, (8, width), 1)
    sublanes = lax.broadcasted_iota(jnp.int32, (8, width), 0)

    def settle(i, planes_):
        def move(n, carry):
            for plane in planes_:
                quarters = [0.0] * 4
                for g in range(frames):
                    row, col = corners[g]
                    value = held[plane, g, n]
                    below, beyond = sublanes + 8 * n < row, lanes < col
                    upper, lower = jnp.where(below, 0.0, value), jnp.where(below, value, 0.0)
                    for at, half in ((0, upper), (2, lower)):
                        quarters[at] += jnp.where(beyond, 0.0, half)
                        quarters[at + 1] += jnp.where(beyond, half, 0.0)
                totals[i, plane, n, :, :width] = quarters[0]
                totals[i, plane, n, :, width:] = quarters[1]
                totals[i, plane, tiles + n, :, :width] = quarters[2]
                totals[i, plane, tiles + n, :, width:] = quarters[3]
            return carry

        lax.fori_loop(0, tiles, move, 0, unroll=4)

    def cut(i, plane, slot):
        row, col = corners[slot]
        picked = []
        for n in range(tiles):
            below, beyond = sublanes + 8 * n < row, lanes < col
            upper, lower = wide[i, plane, n], wide[i, plane, tiles + n]
            left = jnp.where(below, lower[:, :width], upper[:, :width])
            right = jnp.where(below, lower[:, width:], upper[:, width:])
            picked.append(jnp.where(beyond, right, left))
        return turned(
            jnp.concatenate(picked, 0), lax.rem(height - row, height), lax.rem(width - col, width)
        )

    def masked(weights):
        table = [[weights[g:g + 1, k:k + 1] for k in range(mode_count)] for g in range(frames)]
        return [[jnp.where(live(g), w, 0.0) for w in row] for g, row in enumerate(table)]

    def wave(weights, tiles):
        out = []
        for g in range(frames):
            for part in range(2):
                value = weights[g][0] * tiles[part]
                for k in range(1, mode_count):
                    value = value + weights[g][k] * tiles[2 * k + part]
                out.append(value)
        return out

    def fold(value):
        total = value[:, :128]
        for at in range(128, length, 128):
            total = total + value[:, at:at + 128]
        return total

    def whole(value):
        return jnp.sum(jnp.sum(value, 0, keepdims=True), 1, keepdims=True)

    def run_frame(i, g):
        object_real = cut(i, 0, g)
        object_imag = cut(i, 1, g)
        probe_real, probe_imag = probes[g, 0], probes[g, 1]
        exit_real = probe_real * object_real - probe_imag * object_imag
        exit_imag = probe_real * object_imag + probe_imag * object_real
        stacked = jnp.concatenate([exit_real, exit_imag], 0).astype(jnp.bfloat16)
        far_field = apply_transform(stacked, rows_table[...], cols_table[...])
        far_real, far_imag = far_field[:, :length], far_field[:, length:]
        magnitude = jnp.sqrt(far_real * far_real + far_imag * far_imag)
        factor = amplitudes[g].astype(jnp.float32) / jnp.maximum(magnitude, 0.5)
        scaled = jnp.concatenate([far_real * factor, far_imag * factor], 0).astype(jnp.bfloat16)
        back = apply_transform(scaled, cols_table[...], rows_table[...])
        diff_real = back[:, :length] - exit_real
        diff_imag = back[:, length:] - exit_imag
        grads[i, g, 0] = object_real * diff_real + object_imag * diff_imag
        grads[i, g, 1] = object_real * diff_imag - object_imag * diff_real
        hold(0, g, probe_real * diff_real + probe_imag * diff_imag)
        hold(1, g, probe_real * diff_imag - probe_imag * diff_real)

    weights = masked(first_weights)
    for g in range(frames):
        for k in range(mode_count):
            given[0, g:g + 1, k:k + 1] = weights[g][k]
    mate = place.partner(every_order[0][0][0], 1)
    tellings = [
        reach(
            mate, given.at[i], taken.at[i], side_send.at[i, 3 * CHUNKS + 3], side_recv.at[i, 3 * CHUNKS + 3]
        )
        for i in range(ITERS)
    ]
    tellings[0].start()

    def first_wave(block, carry):
        rows = block_rows(block)
        values = wave(weights, [first_modes[p, rows, :] for p in range(planes)])
        for at, value in enumerate(values):
            probes[at // 2, at % 2, rows, :] = value
        return carry

    loads[0].wait()
    lax.fori_loop(0, blocks, first_wave, 0, unroll=4)
    for load in loads[1:]:
        load.wait()

    for i in range(ITERS):
        again = i < ITERS - 1
        modes = first_modes if i == 0 else middle_modes
        kept_weights = first_weights if i == 0 else middle_weights

        def rightward(at, source, target):
            copy = reach(place.right, source, target, side_send.at[i, at], side_recv.at[i, at])
            return Shift(copy, place.has_right, place.has_left)

        def downward(at, source, target):
            copy = reach(place.down, source, target, side_send.at[i, at], side_recv.at[i, at])
            return Shift(copy, place.has_down, place.has_up)

        pair = pl.ds(0, 2)
        low_rights = [
            rightward(q, totals.at[i, pair, chunk(q, tiles), :, far], sideways.at[i, pair, chunk(q, tiles)])
            for q in range(CHUNKS)
        ]
        top_rights = [
            rightward(CHUNKS + q, totals.at[i, pair, chunk(q), :, far], sideways.at[i, pair, chunk(q)])
            for q in range(CHUNKS)
        ]
        downs = [
            downward(2 * CHUNKS + q, bottom.at[i, pair, chunk(q)], fallen.at[i, pair, chunk(q)])
            for q in range(CHUNKS)
        ]
        low_den = rightward(3 * CHUNKS, totals.at[i, 2, low, :, far], sideways.at[i, 2, low])
        top_den = rightward(3 * CHUNKS + 1, totals.at[i, 2, top, :, far], sideways.at[i, 2, top])
        down_den = downward(3 * CHUNKS + 2, bottom.at[i, 2], fallen.at[i, 2])
        leaving += low_rights + top_rights + downs + [low_den, top_den, down_den]

        for g in range(frames):
            hold(2, g, probes[g, 0] * probes[g, 0] + probes[g, 1] * probes[g, 1])
        settle(i, [2])
        low_den.start()
        top_den.start()
        if i == 0:
            for q in range(CHUNKS):
                halos[0].turn(q)
        halos[i].end()
        for g in range(frames):
            run_frame(i, g)
            if g == 0:
                low_den.arrive()
                bottom[i, 2] = totals[i, 2, tiles:, :, :width] + sideways[i, 2, tiles:]
                down_den.start()
        settle(i, [0, 1])
        for q in range(CHUNKS):
            low_rights[q].start()

        orders = every_order[i]
        stages = len(orders[0])
        share = units // len(orders)
        streams = [
            Stream(
                place, order, t * share, share, terms.at[i], landed.at[i],
                stream_send.at[i, t], stream_recv.at[i, t],
            )
            for t, order in enumerate(orders)
        ]
        leaving += streams

        def term_step(block, carry):
            rows = block_rows(block)
            tiles_ = [ref[i, g, part, rows, :] for ref in (grads, mates) for g in range(frames) for part in range(2)]
            for k in range(mode_count):
                for part in range(2):
                    value = joint[0][k] * tiles_[part]
                    for g in range(1, 2 * frames):
                        value = value + joint[g][k] * tiles_[2 * g + part]
                    terms[i, block * planes + 2 * k + part] = value
            return carry

        half = share // planes // 2
        for t, stream in enumerate(streams):
            stream.offer(grads.at[i], mates.at[i], t * 2 * half, half)
        for q in range(CHUNKS):
            top_rights[q].start()

        tellings[i].wait_recv()
        joint = weights + [[taken[i, g:g + 1, k:k + 1] for k in range(mode_count)] for g in range(frames)]
        joint = [[jnp.broadcast_to(w, (8, length)) for w in row] for row in joint]

        def finish_scatter(t, s):
            stream = streams[t]
            if s == 0:
                stream.copies["scatter", 0, 1].wait_recv()
                first = stream.bases[1] // planes
                lax.fori_loop(
                    0, half // 4, lambda n, carry: [term_step(first + 4 * n + m, carry) for m in range(4)][-1], 0
                )
                stream.scatter(1)
                return
            at, value = stream.gathered(s)
            if s < stages - 1:
                terms[i, at] = value
                stream.scatter(s + 1)
                return
            first, target = stream.bases[s + 1], ups[i]
            for n in range(stream.counts[s + 1]):
                unit = first + n
                kept = modes[unit % planes, block_rows(unit // planes), :]
                target[unit] = kept + value[n] / root_total
            stream.spread(s, ups[i])

        sums = [jnp.zeros((8, 128), jnp.float32)] * (len(pairs) + len(strict) + 2 * mode_count * frames)

        def fit_step(block, sums):
            rows = block_rows(block)
            tiles = [ups[i][block * planes + p] for p in range(planes)]
            real, imag = tiles[0::2], tiles[1::2]
            terms_ = [fold(real[a] * real[b] + imag[a] * imag[b]) for a, b in pairs]
            terms_ += [fold(real[a] * imag[b] - imag[a] * real[b]) for a, b in strict]
            for g in range(frames):
                held_real = probes[g, 0, rows, :] + 0.5 * grads[i, g, 0, rows, :]
                held_imag = probes[g, 1, rows, :] + 0.5 * grads[i, g, 1, rows, :]
                for a in range(mode_count):
                    terms_.append(fold(real[a] * held_real + imag[a] * held_imag))
                    terms_.append(fold(real[a] * held_imag - imag[a] * held_real))
            return tuple(a + b for a, b in zip(sums, terms_))

        def finish_gather(t, s):
            nonlocal sums
            streams[t].arrived(s)
            if s > 0:
                streams[t].spread(s - 1, ups[i])
            else:
                per = share // planes
                sums = lax.fori_loop(t * per, (t + 1) * per, fit_step, tuple(sums), unroll=2)

        def drop(q):
            low_rights[q].arrive()
            bottom[i, :2, chunk(q)] = totals[i, :2, chunk(q, tiles), :, near] + sideways[i, :2, chunk(q, tiles)]
            downs[q].start()

        def renew(q):
            if q == 0:
                top_den.arrive()
                down_den.arrive()
            top_rights[q].arrive()
            downs[q].arrive()
            update = [
                totals[i, p, chunk(q), :, near] + sideways[i, p, chunk(q)] + fallen[i, p, chunk(q)]
                for p in range(3)
            ]
            scale = 1.0 / (update[2] + 1.0)
            for p in range(2):
                value = wide[i, p, chunk(q), :, near] + update[p] * scale
                if again:
                    wide[i + 1, p, chunk(q), :, near] = value
                else:
                    new_object[p, chunk(q)] = value
            if again:
                halos[i + 1].begin(q)

        def turn(q):
            if again:
                halos[i + 1].turn(q)

        steps = [functools.partial(finish_scatter, t, s) for s in range(stages) for t in range(len(streams))]
        steps += [
            functools.partial(finish_gather, t, s)
            for s in range(stages - 1, -1, -1) for t in range(len(streams))
        ]
        if again:
            marks = [(drop, (4, 4, 6, 6)), (renew, (9, 11, 13, 15)), (turn, (18, 21, 24, 27))]
        else:
            marks = [(drop, (4, 4, 6, 6)), (renew, (13, 16, 19, 22)), (turn, (32, 32, 32, 32))]
        for n, step in enumerate(steps):
            for task, whens in marks:
                for q, when in enumerate(whens):
                    if when * len(steps) // 32 == n:
                        task(q)
            step()
        for task, whens in marks:
            for q, when in enumerate(whens):
                if when * len(steps) // 32 >= len(steps):
                    task(q)

        totals_of = [whole(s) / pixels for s in sums]
        gram_real = dict(zip(pairs, totals_of))
        gram_imag = dict(zip(strict, totals_of[len(pairs):]))
        upper_real, upper_imag = {}, {}
        for b in range(mode_count):
            for a in range(b):
                sum_real, sum_imag = gram_real[a, b], gram_imag[a, b]
                for k in range(a):
                    r, s, u, v = upper_real[k, a], upper_imag[k, a], upper_real[k, b], upper_imag[k, b]
                    sum_real = sum_real - (r * u + s * v)
                    sum_imag = sum_imag - (r * v - s * u)
                upper_real[a, b] = sum_real / upper_real[a, a]
                upper_imag[a, b] = sum_imag / upper_real[a, a]
            diagonal = gram_real[b, b]
            for k in range(b):
                diagonal = diagonal - (upper_real[k, b] * upper_real[k, b] + upper_imag[k, b] * upper_imag[k, b])
            upper_real[b, b] = jnp.sqrt(diagonal)
        inverse = {b: 1.0 / upper_real[b, b] for b in range(mode_count)}

        refit_weights = []
        at = len(pairs) + len(strict)
        for g in range(frames):
            inner = []
            for k in range(mode_count):
                real, imag = totals_of[at], totals_of[at + 1]
                at += 2
                for a in range(k):
                    r, s, u, v = upper_real[a, k], upper_imag[a, k], inner[a][0], inner[a][1]
                    real = real - (r * u + s * v)
                    imag = imag - (r * v - s * u)
                inner.append((real * inverse[k], imag * inverse[k]))
            refit_weights.append([
                jnp.where(live(g), inner[k][0], kept_weights[g:g + 1, k:k + 1]) for k in range(mode_count)
            ])
        target_weights = middle_weights if again else new_weights
        for g in range(frames):
            for k in range(mode_count):
                target_weights[g:g + 1, k:k + 1] = refit_weights[g][k]
        weights = [[jnp.where(live(g), w, 0.0) for w in row] for g, row in enumerate(refit_weights)]
        if again:
            for g in range(frames):
                for k in range(mode_count):
                    given[i + 1, g:g + 1, k:k + 1] = weights[g][k]
            tellings[i + 1].start()

        def spread_out(value):
            return jnp.broadcast_to(value, (8, length))

        upper_real = {p: spread_out(v) for p, v in upper_real.items() if p[0] < p[1]}
        upper_imag = {p: spread_out(v) for p, v in upper_imag.items()}
        inverse = {p: spread_out(v) for p, v in inverse.items()}
        wave_weights = [[spread_out(w) for w in row] for row in weights]

        def basis_step(block, carry):
            rows = block_rows(block)
            basis = []
            for b in range(mode_count):
                real, imag = ups[i][block * planes + 2 * b], ups[i][block * planes + 2 * b + 1]
                for a in range(b):
                    r, s = upper_real[a, b], upper_imag[a, b]
                    u, v = basis[2 * a], basis[2 * a + 1]
                    real = real - (r * u - s * v)
                    imag = imag - (r * v + s * u)
                basis += [real * inverse[b], imag * inverse[b]]
            for p in range(planes):
                middle_modes[p, rows, :] = basis[p]
            for n, value in enumerate(wave(wave_weights, basis)):
                probes[n // 2, n % 2, rows, :] = value
            return carry

        if again:
            lax.fori_loop(0, blocks, basis_step, 0, unroll=4)
        else:
            rows_ = [inverse[b] for b in range(mode_count)]
            rows_ += [upper_real[p] for p in strict] + [upper_imag[p] for p in strict]
            for n, row in enumerate(rows_):
                factors[n] = row

    for item in leaving + halos:
        item.leave()
    for telling in tellings:
        telling.wait_send()


def finish_kernel(mode_count, settled, rotated, factors, kept_weights, new_object, new_modes, new_weights):
    planes = 2 * mode_count
    pairs = [(i, j) for j in range(mode_count) for i in range(j)]
    new_object[...] = settled[...]
    new_weights[...] = kept_weights[...]
    inverse = [factors[b] for b in range(mode_count)]
    upper_real = {p: factors[mode_count + n] for n, p in enumerate(pairs)}
    upper_imag = {p: factors[mode_count + len(pairs) + n] for n, p in enumerate(pairs)}
    for block in range(rotated.shape[0] // planes):
        basis = []
        for b in range(mode_count):
            real, imag = rotated[block * planes + 2 * b], rotated[block * planes + 2 * b + 1]
            for a in range(b):
                r, s = upper_real[a, b], upper_imag[a, b]
                u, v = basis[2 * a], basis[2 * a + 1]
                real = real - (r * u - s * v)
                imag = imag - (r * v + s * u)
            basis += [real * inverse[b], imag * inverse[b]]
        for p in range(planes):
            new_modes[p, block * 8:block * 8 + 8, :] = basis[p]


def shape(*dims):
    return jax.ShapeDtypeStruct(dims, jnp.float32)


def on_device(object_field, amplitudes, positions, frame_count, coefficients, probe_modes):
    frames, length = amplitudes.shape[:2]
    mode_count = probe_modes.shape[0]
    planes = 2 * mode_count
    height, width = object_field.shape[1:]
    scan_count = lax.axis_size("scan")
    col_count = lax.axis_size("col")
    root_total = math.sqrt(frames * scan_count * col_count)
    rows_table, cols_table = make_tables(length)
    tiles, blocks = height // 8, length // 8
    full_width = width + length
    units = planes * blocks
    order = stream_orders(scan_count, col_count, units, True)[0]
    partners = 2 * sum((1 << len(group)) - 1 for group in order)

    def vmem(*dims):
        return pltpu.VMEM(dims, jnp.float32)

    stream_sems = pltpu.SemaphoreType.DMA((ITERS, 4, partners))
    halo_sems = pltpu.SemaphoreType.DMA((ITERS, 3, CHUNKS))
    side_sems = pltpu.SemaphoreType.DMA((ITERS, 3 * CHUNKS + 4))
    settled, rotated, factors, kept = pl.pallas_call(
        functools.partial(step_kernel, scan_count, col_count, mode_count, root_total),
        name="reconstruct",
        out_shape=(
            shape(2, tiles, 8, width), shape(units, 8, length), shape(mode_count * mode_count, 8, length),
            shape(frames, mode_count),
        ),
        in_specs=[SMEM] * 2 + [VMEM] * 2 + [ANY] * 4,
        out_specs=(VMEM,) * 4,
        scratch_shapes=[
            pltpu.VMEM(amplitudes.shape, amplitudes.dtype),
            vmem(planes, length, length),
            pltpu.VMEM(rows_table.shape, rows_table.dtype),
            pltpu.VMEM(cols_table.shape, cols_table.dtype),
            pltpu.SemaphoreType.DMA((4,)),
            vmem(ITERS, 2, tiles + blocks, 8, full_width),
            vmem(ITERS, 3, tiles + blocks, 8, full_width),
            vmem(3, frames, tiles, 8, width),
            vmem(frames, 2, length, length),
            vmem(ITERS, frames, 2, length, length),
            vmem(ITERS, frames, 2, length, length),
            vmem(ITERS, frames, mode_count),
            vmem(ITERS, frames, mode_count),
            vmem(ITERS, units, 8, length),
            vmem(ITERS, units, 8, length),
            vmem(ITERS - 1, units, 8, length),
            vmem(planes, length, length),
            vmem(frames, mode_count),
            vmem(ITERS, 3, tiles + blocks, 8, width),
            vmem(ITERS, 3, tiles, 8, width),
            vmem(ITERS, 3, tiles, 8, width),
            stream_sems, stream_sems, halo_sems, halo_sems, side_sems, side_sems,
        ],
        compiler_params=pltpu.CompilerParams(
            collective_id=0, has_side_effects=True, vmem_limit_bytes=60 * 2**20
        ),
        cost_estimate=pl.CostEstimate(flops=5 * 10**9, bytes_accessed=10**7, transcendentals=0),
    )(
        frame_count, positions, coefficients, object_field.reshape(2, tiles, 8, width), amplitudes,
        probe_modes.reshape(planes, length, length), rows_table, cols_table,
    )
    parts = 4
    new_object, modes, weights = pl.pallas_call(
        functools.partial(finish_kernel, mode_count),
        name="finish",
        grid=(parts,),
        out_shape=(shape(2, tiles, 8, width), shape(planes, length, length), shape(frames, mode_count)),
        in_specs=[
            pl.BlockSpec((2, tiles // parts, 8, width), lambda n: (0, n, 0, 0)),
            pl.BlockSpec((units // parts, 8, length), lambda n: (n, 0, 0)),
            pl.BlockSpec(factors.shape, lambda n: (0, 0, 0)),
            pl.BlockSpec(kept.shape, lambda n: (0, 0)),
        ],
        out_specs=(
            pl.BlockSpec((2, tiles // parts, 8, width), lambda n: (0, n, 0, 0)),
            pl.BlockSpec((planes, length // parts, length), lambda n: (0, n, 0)),
            pl.BlockSpec(kept.shape, lambda n: (0, 0)),
        ),
    )(settled, rotated, factors, kept)
    return (new_object.reshape(object_field.shape), modes.reshape(probe_modes.shape), weights)


def solution(mesh):
    placed = (
        P(None, "scan", "col"),
        P(("scan", "col"), None, None),
        P(("scan", "col"), None),
        P(("scan", "col")),
        P(("scan", "col"), None),
        P(),
    )
    return jax.shard_map(
        on_device,
        mesh=mesh,
        in_specs=placed,
        out_specs=(P(None, "scan", "col"), P(), P(("scan", "col"), None)),
        check_vma=False,
    )
```

```python
import functools
import math

import jax
import jax.numpy as jnp
import ml_dtypes
import numpy as np
from jax import lax
from jax.experimental import pallas as pl
from jax.experimental.pallas import tpu as pltpu
from jax.sharding import PartitionSpec as P

ITERS = 2
CHUNKS = 4

VMEM = pl.BlockSpec(memory_space=pltpu.VMEM)
SMEM = pl.BlockSpec(memory_space=pltpu.SMEM)
ANY = pl.BlockSpec(memory_space=pl.ANY)


def make_tables(length):
    indices = np.arange(length, dtype=np.int32)
    phases = indices[:, None] * indices[None, :] % length
    angles = phases.astype(np.float32) * np.float32(2.0 * math.pi / length)
    factor = np.float32(1.0 / math.sqrt(length))
    cosine = np.cos(angles) * factor
    sine = np.sin(angles) * factor
    rows_table = np.block([[cosine, sine], [-sine, cosine]])
    cols_table = np.block([[cosine, -sine], [sine, cosine]])
    return (rows_table.astype(ml_dtypes.bfloat16), cols_table.astype(ml_dtypes.bfloat16))


def apply_transform(stacked, first_table, second_table):
    length = stacked.shape[1]
    halfway = jnp.dot(first_table, stacked, preferred_element_type=jnp.float32).astype(jnp.bfloat16)
    beside = jnp.concatenate([halfway[:length], halfway[length:]], 1)
    return jnp.dot(beside, second_table, preferred_element_type=jnp.float32)


def bits_of(axis, count):
    return [(axis, 1 << b) for b in range(count.bit_length() - 1)]


def stream_orders(scan_count, col_count, units, again):
    scan, col = bits_of("scan", scan_count), bits_of("col", col_count)
    core, y, x, z, w = col[:1], col[1:], scan[:1], scan[1:3], scan[3:]
    if again:
        orders = [[core, x, y, z, w], [core, y, z, x, w], [core, y, x, z, w], [core, y, z, x, w]]
    else:
        orders = [[core, x, y, z, w], [core, y, x, z, w], [core, x, y, z, w], [core, y, x, z, w]]
    if units // (scan_count * col_count) < len(orders):
        orders = orders[1:3]
    return [[group for group in order if group] for order in orders]


def reach(device, source, target, send_sem, recv_sem):
    return pltpu.make_async_remote_copy(
        src_ref=source,
        dst_ref=target,
        send_sem=send_sem,
        recv_sem=recv_sem,
        device_id=device,
        device_id_type=pl.DeviceIdType.MESH,
    )


class Shift:
    def __init__(self, copy, sends, receives):
        self.copy, self.sends, self.receives = copy, sends, receives

    def start(self):
        pl.when(self.sends)(self.copy.start)

    def arrive(self):
        pl.when(self.receives)(self.copy.wait_recv)

    def leave(self):
        pl.when(self.sends)(self.copy.wait_send)


class Place:
    def __init__(self, scan_count, col_count):
        self.scan, self.col = lax.axis_index("scan"), lax.axis_index("col")
        self.right = (self.scan, lax.rem(self.col + 1, col_count))
        self.left = (self.scan, lax.rem(self.col + col_count - 1, col_count))
        self.down = (lax.rem(self.scan + 1, scan_count), self.col)
        self.up = (lax.rem(self.scan + scan_count - 1, scan_count), self.col)
        self.has_right, self.has_left = self.col < col_count - 1, self.col > 0
        self.has_down, self.has_up = self.scan < scan_count - 1, self.scan > 0
        self.beyond = (self.down[0], self.right[1])
        self.before = (self.up[0], self.left[1])
        self.has_beyond = jnp.logical_and(self.has_down, self.has_right)
        self.has_before = jnp.logical_and(self.has_up, self.has_left)

    def sides(self):
        return (
            (self.right, self.has_right), (self.left, self.has_left),
            (self.down, self.has_down), (self.up, self.has_up),
            (self.beyond, self.has_beyond), (self.before, self.has_before),
        )

    def bit(self, axis, bit):
        at = self.scan if axis == "scan" else self.col
        return at // bit % 2

    def index(self, group, flips):
        total = 0
        for b, (axis, bit) in enumerate(group):
            mine = self.bit(axis, bit)
            total = total + (1 - mine if flips >> b & 1 else mine) * (1 << b)
        return total

    def partner(self, group, flips):
        scan, col = self.scan, self.col
        for b, (axis, bit) in enumerate(group):
            if flips >> b & 1:
                step = bit - 2 * bit * self.bit(axis, bit)
                if axis == "scan":
                    scan = scan + step
                else:
                    col = col + step
        return (scan, col)

    def greet(self, groups):
        barrier = pltpu.get_barrier_semaphore()
        partners = [self.partner(group, flips) for group in groups for flips in range(1, 1 << len(group))]

        def signal(device):
            pl.semaphore_signal(barrier, inc=1, device_id=device, device_id_type=pl.DeviceIdType.MESH)

        for device in partners:
            signal(device)
        for device, there in self.sides():
            pl.when(there)(functools.partial(signal, device))
        present = [there.astype(jnp.int32) for _, there in self.sides()]
        pl.semaphore_wait(barrier, len(partners) + sum(present))


class Stream:
    def __init__(self, place, order, base, count, terms, landed, send_sems, recv_sems):
        self.place, self.order = place, order
        self.terms, self.landed = terms, landed
        self.send_sems, self.recv_sems = send_sems, recv_sems
        self.bases, self.counts, self.slots, self.marks = [base], [count], [], []
        self.copies = {}
        slot, mark = base, 0
        for group in order:
            members = 1 << len(group)
            part = self.counts[-1] // members
            self.bases.append(self.bases[-1] + place.index(group, 0) * part)
            self.counts.append(part)
            self.slots.append(slot)
            self.marks.append(mark)
            slot += part * (members - 1)
            mark += members - 1
        self.total = mark

    def flips(self, s):
        return range(1, 1 << len(self.order[s]))

    def scatter(self, s):
        part = self.counts[s + 1]
        for flips in self.flips(s):
            group = self.order[s]
            source = self.terms.at[pl.ds(self.bases[s] + self.place.index(group, flips) * part, part)]
            target = self.landed.at[pl.ds(self.slots[s] + (flips - 1) * part, part)]
            at = self.marks[s] + flips - 1
            copy = reach(
                self.place.partner(group, flips), source, target, self.send_sems.at[at], self.recv_sems.at[at]
            )
            copy.start()
            self.copies["scatter", s, flips] = copy

    def offer(self, grads, mates, first, half):
        group = self.order[0]
        start = (first + self.place.index(group, 1) * half) * 8
        rows = pl.ds(pl.multiple_of(start, 8), half * 8)
        copy = reach(
            self.place.partner(group, 1), grads.at[:, :, rows, :], mates.at[:, :, rows, :],
            self.send_sems.at[0], self.recv_sems.at[0],
        )
        copy.start()
        self.copies["scatter", 0, 1] = copy

    def gathered(self, s):
        part = self.counts[s + 1]
        at = pl.ds(self.bases[s + 1], part)
        value = self.terms[at]
        for flips in self.flips(s):
            self.copies["scatter", s, flips].wait_recv()
            value = value + self.landed[pl.ds(self.slots[s] + (flips - 1) * part, part)]
        return at, value

    def spread(self, s, raised):
        piece = raised.at[pl.ds(self.bases[s + 1], self.counts[s + 1])]
        for flips in self.flips(s):
            at = self.total + self.marks[s] + flips - 1
            copy = reach(
                self.place.partner(self.order[s], flips), piece, piece,
                self.send_sems.at[at], self.recv_sems.at[at],
            )
            copy.start()
            self.copies["gather", s, flips] = copy

    def arrived(self, s):
        for flips in self.flips(s):
            self.copies["gather", s, flips].wait_recv()

    def leave(self):
        for copy in self.copies.values():
            copy.wait_send()


class Halo:
    def __init__(self, place, wide, tiles, width, send_sems, recv_sems):
        rows = tiles // CHUNKS
        near, far = pl.ds(0, width), pl.ds(width, width)
        self.up, self.side, self.corner = [], [], []
        for q in range(CHUNKS):
            top, low = pl.ds(q * rows, rows), pl.ds(tiles + q * rows, rows)
            self.up.append(Shift(
                reach(place.up, wide.at[:, top, :, near], wide.at[:, low, :, near], send_sems.at[0, q], recv_sems.at[0, q]),
                place.has_up, place.has_down,
            ))
            self.side.append(Shift(
                reach(place.left, wide.at[:, top, :, near], wide.at[:, top, :, far], send_sems.at[1, q], recv_sems.at[1, q]),
                place.has_left, place.has_right,
            ))
            self.corner.append(Shift(
                reach(place.left, wide.at[:, low, :, near], wide.at[:, low, :, far], send_sems.at[2, q], recv_sems.at[2, q]),
                place.has_left, place.has_right,
            ))

    def begin(self, q):
        self.up[q].start()
        self.side[q].start()

    def turn(self, q):
        self.up[q].arrive()
        self.corner[q].start()

    def end(self):
        for shift in self.side + self.corner:
            shift.arrive()

    def leave(self):
        for shift in self.up + self.side + self.corner:
            shift.leave()


def step_kernel(
    scan_count, col_count, mode_count, root_total,
    count, positions, first_weights, field, far_amplitudes, far_modes, far_rows, far_cols,
    new_object, last_raised, factors, new_weights,
    amplitudes, first_modes, rows_table, cols_table, input_sems,
    wide, totals, held, den, powers, probes, grads, mates, given, taken, terms, landed, raised, middle_modes, middle_weights,
    sideways, fallen, bottom,
    stream_send, stream_recv, halo_send, halo_recv, side_send, side_recv,
):
    tiles, _, width = field.shape[1:]
    height = 8 * tiles
    frames, length = amplitudes.shape[:2]
    planes = 2 * mode_count
    blocks = length // 8
    units = blocks * planes
    pixels = float(length * length)
    full_width = width + length
    rows_of_chunk = tiles // CHUNKS
    place = Place(scan_count, col_count)
    near, far = pl.ds(0, width), pl.ds(width, width)
    top, low = pl.ds(0, tiles), pl.ds(tiles, tiles)
    pairs = [(i, j) for j in range(mode_count) for i in range(j + 1)]
    strict = [(i, j) for i, j in pairs if i < j]
    leaving = []
    ups = [raised.at[i] for i in range(ITERS - 1)] + [last_raised]

    def chunk(q, offset=0):
        return pl.ds(offset + q * rows_of_chunk, rows_of_chunk)

    def block_rows(block):
        return pl.ds(pl.multiple_of(block * 8, 8), 8)

    loads = [
        pltpu.make_async_copy(source, target, input_sems.at[n])
        for n, (source, target) in enumerate((
            (far_modes, first_modes), (far_rows, rows_table), (far_cols, cols_table), (far_amplitudes, amplitudes),
        ))
    ]
    for load in loads:
        load.start()

    wide[0, :, :tiles, :, :width] = field[...]

    @pl.when(jnp.logical_not(place.has_left))
    def _():
        sideways[...] = jnp.zeros_like(sideways)

    @pl.when(jnp.logical_not(place.has_up))
    def _():
        fallen[...] = jnp.zeros_like(fallen)

    for slot, there in ((1, place.has_left), (2, place.has_up), (3, place.has_before)):

        @pl.when(jnp.logical_not(there))
        def _():
            for i in range(ITERS):
                taken[i, slot] = jnp.zeros(taken.shape[2:], jnp.float32)

    every_order = [stream_orders(scan_count, col_count, units, i < ITERS - 1) for i in range(ITERS)]
    place.greet(every_order[0][0])
    halos = [
        Halo(place, wide.at[i], tiles, width, halo_send.at[i], halo_recv.at[i]) for i in range(ITERS)
    ]
    for q in range(CHUNKS):
        halos[0].begin(q)
    def live(slot):
        return slot < count[0]

    def inside(value, limit):
        return jnp.minimum(jnp.maximum(value, 0), limit - 1)

    corners = [
        (
            inside(positions[g, 0] - place.scan * height, height),
            inside(positions[g, 1] - place.col * width, width),
        )
        for g in range(frames)
    ]

    def turned(piece, row, col):
        return pltpu.roll(pltpu.roll(piece, row, 0), col, 1)

    def hold(plane, slot, piece):
        row, col = corners[slot]
        held[plane, slot] = turned(piece, row, col).reshape(tiles, 8, width)

    lanes = lax.broadcasted_iota(jnp.int32, (8, width), 1)
    sublanes = lax.broadcasted_iota(jnp.int32, (8, width), 0)

    def settle(i):
        def move(n, carry):
            for plane in range(2):
                quarters = [0.0] * 4
                for g in range(frames):
                    row, col = corners[g]
                    value = held[plane, g, n]
                    below, beyond = sublanes + 8 * n < row, lanes < col
                    upper, lower = jnp.where(below, 0.0, value), jnp.where(below, value, 0.0)
                    for at, half in ((0, upper), (2, lower)):
                        quarters[at] += jnp.where(beyond, 0.0, half)
                        quarters[at + 1] += jnp.where(beyond, half, 0.0)
                totals[i, plane, n, :, :width] = quarters[0]
                totals[i, plane, n, :, width:] = quarters[1]
                totals[i, plane, tiles + n, :, :width] = quarters[2]
                totals[i, plane, tiles + n, :, width:] = quarters[3]
            return carry

        lax.fori_loop(0, tiles, move, 0, unroll=4)

    def cut(i, plane, slot):
        row, col = corners[slot]
        picked = []
        for n in range(tiles):
            below, beyond = sublanes + 8 * n < row, lanes < col
            upper, lower = wide[i, plane, n], wide[i, plane, tiles + n]
            left = jnp.where(below, lower[:, :width], upper[:, :width])
            right = jnp.where(below, lower[:, width:], upper[:, width:])
            picked.append(jnp.where(beyond, right, left))
        return turned(
            jnp.concatenate(picked, 0), lax.rem(height - row, height), lax.rem(width - col, width)
        )

    def masked(weights):
        table = [[weights[g:g + 1, k:k + 1] for k in range(mode_count)] for g in range(frames)]
        return [[jnp.where(live(g), w, 0.0) for w in row] for g, row in enumerate(table)]

    def wave(weights, tiles):
        out = []
        for g in range(frames):
            for part in range(2):
                value = weights[g][0] * tiles[part]
                for k in range(1, mode_count):
                    value = value + weights[g][k] * tiles[2 * k + part]
                out.append(value)
        return out

    def fold(value):
        total = value[:, :128]
        for at in range(128, length, 128):
            total = total + value[:, at:at + 128]
        return total

    def whole(value):
        return jnp.sum(jnp.sum(value, 0, keepdims=True), 1, keepdims=True)

    def run_frame(i, g):
        object_real = cut(i, 0, g)
        object_imag = cut(i, 1, g)
        probe_real, probe_imag = probes[g, 0], probes[g, 1]
        exit_real = probe_real * object_real - probe_imag * object_imag
        exit_imag = probe_real * object_imag + probe_imag * object_real
        stacked = jnp.concatenate([exit_real, exit_imag], 0).astype(jnp.bfloat16)
        far_field = apply_transform(stacked, rows_table[...], cols_table[...])
        far_real, far_imag = far_field[:, :length], far_field[:, length:]
        magnitude = jnp.sqrt(far_real * far_real + far_imag * far_imag)
        factor = amplitudes[g].astype(jnp.float32) / jnp.maximum(magnitude, 0.5)
        scaled = jnp.concatenate([far_real * factor, far_imag * factor], 0).astype(jnp.bfloat16)
        back = apply_transform(scaled, cols_table[...], rows_table[...])
        diff_real = back[:, :length] - exit_real
        diff_imag = back[:, length:] - exit_imag
        grads[i, g, 0] = object_real * diff_real + object_imag * diff_imag
        grads[i, g, 1] = object_real * diff_imag - object_imag * diff_real
        hold(0, g, probe_real * diff_real + probe_imag * diff_imag)
        hold(1, g, probe_real * diff_imag - probe_imag * diff_real)

    weights = masked(first_weights)
    mate = place.partner(every_order[0][0][0], 1)

    def tell(i):
        for g in range(frames):
            for k in range(mode_count):
                given[i, g:g + 1, k:k + 1] = weights[g][k]
            for at, value in enumerate(corners[g]):
                given[i, g:g + 1, mode_count + at:mode_count + at + 1] = jnp.full((1, 1), value, jnp.int32).astype(jnp.float32)
        for telling in tellings[i]:
            telling.start()

    def telling_to(i, slot, device, sends, receives):
        at = 3 * CHUNKS + slot
        return Shift(
            reach(device, given.at[i], taken.at[i, slot], side_send.at[i, at], side_recv.at[i, at]), sends, receives
        )

    always = place.col >= 0
    tellings = [
        [
            telling_to(i, 0, mate, always, always),
            telling_to(i, 1, place.right, place.has_right, place.has_left),
            telling_to(i, 2, place.down, place.has_down, place.has_up),
            telling_to(i, 3, place.beyond, place.has_beyond, place.has_before),
        ]
        for i in range(ITERS)
    ]
    tell(0)

    def first_wave(block, carry):
        rows = block_rows(block)
        values = wave(weights, [first_modes[p, rows, :] for p in range(planes)])
        for at, value in enumerate(values):
            probes[at // 2, at % 2, rows, :] = value
        return carry

    loads[0].wait()
    lax.fori_loop(0, blocks, first_wave, 0, unroll=4)
    for load in loads[1:]:
        load.wait()

    for i in range(ITERS):
        again = i < ITERS - 1
        modes = first_modes if i == 0 else middle_modes
        kept_weights = first_weights if i == 0 else middle_weights

        def rightward(at, source, target):
            copy = reach(place.right, source, target, side_send.at[i, at], side_recv.at[i, at])
            return Shift(copy, place.has_right, place.has_left)

        def downward(at, source, target):
            copy = reach(place.down, source, target, side_send.at[i, at], side_recv.at[i, at])
            return Shift(copy, place.has_down, place.has_up)

        pair = pl.ds(0, 2)
        low_rights = [
            rightward(q, totals.at[i, pair, chunk(q, tiles), :, far], sideways.at[i, pair, chunk(q, tiles)])
            for q in range(CHUNKS)
        ]
        top_rights = [
            rightward(CHUNKS + q, totals.at[i, pair, chunk(q), :, far], sideways.at[i, pair, chunk(q)])
            for q in range(CHUNKS)
        ]
        downs = [
            downward(2 * CHUNKS + q, bottom.at[i, pair, chunk(q)], fallen.at[i, pair, chunk(q)])
            for q in range(CHUNKS)
        ]
        leaving += low_rights + top_rights + downs

        if i == 0:
            for q in range(CHUNKS):
                halos[0].turn(q)
        halos[i].end()
        for g in range(frames):
            run_frame(i, g)
        settle(i)
        for q in range(CHUNKS):
            low_rights[q].start()

        orders = every_order[i]
        stages = len(orders[0])
        share = units // len(orders)
        streams = [
            Stream(
                place, order, t * share, share, terms.at[i], landed.at[i],
                stream_send.at[i, t], stream_recv.at[i, t],
            )
            for t, order in enumerate(orders)
        ]
        leaving += streams

        def term_step(block, carry):
            rows = block_rows(block)
            tiles_ = [ref[i, g, part, rows, :] for ref in (grads, mates) for g in range(frames) for part in range(2)]
            for k in range(mode_count):
                for part in range(2):
                    value = joint[0][k] * tiles_[part]
                    for g in range(1, 2 * frames):
                        value = value + joint[g][k] * tiles_[2 * g + part]
                    terms[i, block * planes + 2 * k + part] = value
            return carry

        half = share // planes // 2
        for t, stream in enumerate(streams):
            stream.offer(grads.at[i], mates.at[i], t * 2 * half, half)
        for q in range(CHUNKS):
            top_rights[q].start()

        for telling in tellings[i]:
            telling.arrive()
        joint = weights + [[taken[i, 0, g:g + 1, k:k + 1] for k in range(mode_count)] for g in range(frames)]
        joint = [[jnp.broadcast_to(w, (8, length)) for w in row] for row in joint]

        def finish_scatter(t, s):
            stream = streams[t]
            if s == 0:
                stream.copies["scatter", 0, 1].wait_recv()
                first = stream.bases[1] // planes
                lax.fori_loop(
                    0, half // 4, lambda n, carry: [term_step(first + 4 * n + m, carry) for m in range(4)][-1], 0
                )
                stream.scatter(1)
                return
            at, value = stream.gathered(s)
            if s < stages - 1:
                terms[i, at] = value
                stream.scatter(s + 1)
                return
            first, target = stream.bases[s + 1], ups[i]
            for n in range(stream.counts[s + 1]):
                unit = first + n
                kept = modes[unit % planes, block_rows(unit // planes), :]
                target[unit] = kept + value[n] / root_total
            stream.spread(s, ups[i])

        sums = [jnp.zeros((8, 128), jnp.float32)] * (len(pairs) + len(strict) + 2 * mode_count * frames)

        def fit_step(block, sums):
            rows = block_rows(block)
            tiles = [ups[i][block * planes + p] for p in range(planes)]
            real, imag = tiles[0::2], tiles[1::2]
            terms_ = [fold(real[a] * real[b] + imag[a] * imag[b]) for a, b in pairs]
            terms_ += [fold(real[a] * imag[b] - imag[a] * real[b]) for a, b in strict]
            for g in range(frames):
                held_real = probes[g, 0, rows, :] + 0.5 * grads[i, g, 0, rows, :]
                held_imag = probes[g, 1, rows, :] + 0.5 * grads[i, g, 1, rows, :]
                for a in range(mode_count):
                    terms_.append(fold(real[a] * held_real + imag[a] * held_imag))
                    terms_.append(fold(real[a] * held_imag - imag[a] * held_real))
            return tuple(a + b for a, b in zip(sums, terms_))

        def finish_gather(t, s):
            nonlocal sums
            streams[t].arrived(s)
            if s > 0:
                streams[t].spread(s - 1, ups[i])
            else:
                per = share // planes
                sums = lax.fori_loop(t * per, (t + 1) * per, fit_step, tuple(sums), unroll=2)

        def drop(q):
            low_rights[q].arrive()
            bottom[i, :2, chunk(q)] = totals[i, :2, chunk(q, tiles), :, near] + sideways[i, :2, chunk(q, tiles)]
            downs[q].start()

        def renew(q):
            top_rights[q].arrive()
            downs[q].arrive()
            update = [
                totals[i, p, chunk(q), :, near] + sideways[i, p, chunk(q)] + fallen[i, p, chunk(q)]
                for p in range(2)
            ]
            scale = 1.0 / (den[chunk(q)] + 1.0)
            for p in range(2):
                value = wide[i, p, chunk(q), :, near] + update[p] * scale
                if again:
                    wide[i + 1, p, chunk(q), :, near] = value
                else:
                    new_object[p, chunk(q)] = value
            if again:
                halos[i + 1].begin(q)

        def weigh():
            near_weights = [
                [
                    [jnp.broadcast_to(taken[i, slot, g:g + 1, k:k + 1], (8, length)) for k in range(mode_count)]
                    for g in range(frames)
                ]
                for slot in range(1, 4)
            ]

            def power_step(block, carry):
                rows = block_rows(block)
                tiles_ = [modes[p, rows, :] for p in range(planes)]
                values = [probes[g, part, rows, :] for g in range(frames) for part in range(2)]
                for weights_ in near_weights:
                    values += wave(weights_, tiles_)
                for n in range(4 * frames):
                    real, imag = values[2 * n], values[2 * n + 1]
                    powers[n // frames, n % frames, rows, :] = real * real + imag * imag
                return carry

            lax.fori_loop(0, blocks, power_step, 0, unroll=2)
            spots = [list(corners)]
            for slot in range(1, 4):
                spots.append([
                    tuple(
                        inside(jnp.sum(taken[i, slot, g:g + 1, at:at + 1]).astype(jnp.int32), limit)
                        for at, limit in ((mode_count, height), (mode_count + 1, width))
                    )
                    for g in range(frames)
                ])
            for slot in range(4):
                for g in range(frames):
                    powers[slot, g] = turned(powers[slot, g], *spots[slot][g])

            def den_step(n, carry):
                rows = block_rows(n)
                total = 0.0
                for slot in range(4):
                    for g in range(frames):
                        row, col = spots[slot][g]
                        below, beyond = sublanes + 8 * n < row, lanes < col
                        if slot < 2:
                            below = jnp.logical_not(below)
                        if slot % 2 == 0:
                            beyond = jnp.logical_not(beyond)
                        total = total + jnp.where(jnp.logical_and(below, beyond), powers[slot, g, rows, :], 0.0)
                den[n] = total
                return carry

            lax.fori_loop(0, tiles, den_step, 0, unroll=2)

        def turn(q):
            if again:
                halos[i + 1].turn(q)

        steps = [functools.partial(finish_scatter, t, s) for s in range(stages) for t in range(len(streams))]
        steps += [
            functools.partial(finish_gather, t, s)
            for s in range(stages - 1, -1, -1) for t in range(len(streams))
        ]
        if again:
            marks = [(drop, (4, 4, 6, 6)), (renew, (9, 11, 13, 15)), (turn, (18, 21, 24, 27))]
        else:
            marks = [(drop, (4, 4, 6, 6)), (renew, (13, 16, 19, 22)), (turn, (32, 32, 32, 32))]
        for n, step in enumerate(steps):
            if n == len(steps) * 6 // 32:
                weigh()
            for task, whens in marks:
                for q, when in enumerate(whens):
                    if when * len(steps) // 32 == n:
                        task(q)
            step()
        for task, whens in marks:
            for q, when in enumerate(whens):
                if when * len(steps) // 32 >= len(steps):
                    task(q)

        totals_of = [whole(s) / pixels for s in sums]
        gram_real = dict(zip(pairs, totals_of))
        gram_imag = dict(zip(strict, totals_of[len(pairs):]))
        upper_real, upper_imag = {}, {}
        for b in range(mode_count):
            for a in range(b):
                sum_real, sum_imag = gram_real[a, b], gram_imag[a, b]
                for k in range(a):
                    r, s, u, v = upper_real[k, a], upper_imag[k, a], upper_real[k, b], upper_imag[k, b]
                    sum_real = sum_real - (r * u + s * v)
                    sum_imag = sum_imag - (r * v - s * u)
                upper_real[a, b] = sum_real / upper_real[a, a]
                upper_imag[a, b] = sum_imag / upper_real[a, a]
            diagonal = gram_real[b, b]
            for k in range(b):
                diagonal = diagonal - (upper_real[k, b] * upper_real[k, b] + upper_imag[k, b] * upper_imag[k, b])
            upper_real[b, b] = jnp.sqrt(diagonal)
        inverse = {b: 1.0 / upper_real[b, b] for b in range(mode_count)}

        refit_weights = []
        at = len(pairs) + len(strict)
        for g in range(frames):
            inner = []
            for k in range(mode_count):
                real, imag = totals_of[at], totals_of[at + 1]
                at += 2
                for a in range(k):
                    r, s, u, v = upper_real[a, k], upper_imag[a, k], inner[a][0], inner[a][1]
                    real = real - (r * u + s * v)
                    imag = imag - (r * v - s * u)
                inner.append((real * inverse[k], imag * inverse[k]))
            refit_weights.append([
                jnp.where(live(g), inner[k][0], kept_weights[g:g + 1, k:k + 1]) for k in range(mode_count)
            ])
        target_weights = middle_weights if again else new_weights
        for g in range(frames):
            for k in range(mode_count):
                target_weights[g:g + 1, k:k + 1] = refit_weights[g][k]
        weights = [[jnp.where(live(g), w, 0.0) for w in row] for g, row in enumerate(refit_weights)]
        if again:
            tell(i + 1)

        def spread_out(value):
            return jnp.broadcast_to(value, (8, length))

        upper_real = {p: spread_out(v) for p, v in upper_real.items() if p[0] < p[1]}
        upper_imag = {p: spread_out(v) for p, v in upper_imag.items()}
        inverse = {p: spread_out(v) for p, v in inverse.items()}
        wave_weights = [[spread_out(w) for w in row] for row in weights]

        def basis_step(block, carry):
            rows = block_rows(block)
            basis = []
            for b in range(mode_count):
                real, imag = ups[i][block * planes + 2 * b], ups[i][block * planes + 2 * b + 1]
                for a in range(b):
                    r, s = upper_real[a, b], upper_imag[a, b]
                    u, v = basis[2 * a], basis[2 * a + 1]
                    real = real - (r * u - s * v)
                    imag = imag - (r * v + s * u)
                basis += [real * inverse[b], imag * inverse[b]]
            for p in range(planes):
                middle_modes[p, rows, :] = basis[p]
            for n, value in enumerate(wave(wave_weights, basis)):
                probes[n // 2, n % 2, rows, :] = value
            return carry

        if again:
            lax.fori_loop(0, blocks, basis_step, 0, unroll=4)
        else:
            rows_ = [inverse[b] for b in range(mode_count)]
            rows_ += [upper_real[p] for p in strict] + [upper_imag[p] for p in strict]
            for n, row in enumerate(rows_):
                factors[n] = row

    for item in leaving + halos:
        item.leave()
    for telling in sum(tellings, []):
        telling.leave()


def finish_kernel(mode_count, settled, rotated, factors, kept_weights, new_object, new_modes, new_weights):
    planes = 2 * mode_count
    pairs = [(i, j) for j in range(mode_count) for i in range(j)]
    new_object[...] = settled[...]
    new_weights[...] = kept_weights[...]
    inverse = [factors[b] for b in range(mode_count)]
    upper_real = {p: factors[mode_count + n] for n, p in enumerate(pairs)}
    upper_imag = {p: factors[mode_count + len(pairs) + n] for n, p in enumerate(pairs)}
    for block in range(rotated.shape[0] // planes):
        basis = []
        for b in range(mode_count):
            real, imag = rotated[block * planes + 2 * b], rotated[block * planes + 2 * b + 1]
            for a in range(b):
                r, s = upper_real[a, b], upper_imag[a, b]
                u, v = basis[2 * a], basis[2 * a + 1]
                real = real - (r * u - s * v)
                imag = imag - (r * v + s * u)
            basis += [real * inverse[b], imag * inverse[b]]
        for p in range(planes):
            new_modes[p, block * 8:block * 8 + 8, :] = basis[p]


def shape(*dims):
    return jax.ShapeDtypeStruct(dims, jnp.float32)


def on_device(object_field, amplitudes, positions, frame_count, coefficients, probe_modes):
    frames, length = amplitudes.shape[:2]
    mode_count = probe_modes.shape[0]
    planes = 2 * mode_count
    height, width = object_field.shape[1:]
    scan_count = lax.axis_size("scan")
    col_count = lax.axis_size("col")
    root_total = math.sqrt(frames * scan_count * col_count)
    rows_table, cols_table = make_tables(length)
    tiles, blocks = height // 8, length // 8
    full_width = width + length
    units = planes * blocks
    order = stream_orders(scan_count, col_count, units, True)[0]
    partners = 2 * sum((1 << len(group)) - 1 for group in order)

    def vmem(*dims):
        return pltpu.VMEM(dims, jnp.float32)

    stream_sems = pltpu.SemaphoreType.DMA((ITERS, 4, partners))
    halo_sems = pltpu.SemaphoreType.DMA((ITERS, 3, CHUNKS))
    side_sems = pltpu.SemaphoreType.DMA((ITERS, 3 * CHUNKS + 4))
    settled, rotated, factors, kept = pl.pallas_call(
        functools.partial(step_kernel, scan_count, col_count, mode_count, root_total),
        name="reconstruct",
        out_shape=(
            shape(2, tiles, 8, width), shape(units, 8, length), shape(mode_count * mode_count, 8, length),
            shape(frames, mode_count),
        ),
        in_specs=[SMEM] * 2 + [VMEM] * 2 + [ANY] * 4,
        out_specs=(VMEM,) * 4,
        scratch_shapes=[
            pltpu.VMEM(amplitudes.shape, amplitudes.dtype),
            vmem(planes, length, length),
            pltpu.VMEM(rows_table.shape, rows_table.dtype),
            pltpu.VMEM(cols_table.shape, cols_table.dtype),
            pltpu.SemaphoreType.DMA((4,)),
            vmem(ITERS, 2, tiles + blocks, 8, full_width),
            vmem(ITERS, 2, tiles + blocks, 8, full_width),
            vmem(2, frames, tiles, 8, width),
            vmem(tiles, 8, width),
            vmem(4, frames, length, length),
            vmem(frames, 2, length, length),
            vmem(ITERS, frames, 2, length, length),
            vmem(ITERS, frames, 2, length, length),
            vmem(ITERS, frames, mode_count + 2),
            vmem(ITERS, 4, frames, mode_count + 2),
            vmem(ITERS, units, 8, length),
            vmem(ITERS, units, 8, length),
            vmem(ITERS - 1, units, 8, length),
            vmem(planes, length, length),
            vmem(frames, mode_count),
            vmem(ITERS, 2, tiles + blocks, 8, width),
            vmem(ITERS, 2, tiles, 8, width),
            vmem(ITERS, 2, tiles, 8, width),
            stream_sems, stream_sems, halo_sems, halo_sems, side_sems, side_sems,
        ],
        compiler_params=pltpu.CompilerParams(
            collective_id=0, has_side_effects=True, vmem_limit_bytes=60 * 2**20
        ),
        cost_estimate=pl.CostEstimate(flops=5 * 10**9, bytes_accessed=10**7, transcendentals=0),
    )(
        frame_count, positions, coefficients, object_field.reshape(2, tiles, 8, width), amplitudes,
        probe_modes.reshape(planes, length, length), rows_table, cols_table,
    )
    parts = 4
    new_object, modes, weights = pl.pallas_call(
        functools.partial(finish_kernel, mode_count),
        name="finish",
        grid=(parts,),
        out_shape=(shape(2, tiles, 8, width), shape(planes, length, length), shape(frames, mode_count)),
        in_specs=[
            pl.BlockSpec((2, tiles // parts, 8, width), lambda n: (0, n, 0, 0)),
            pl.BlockSpec((units // parts, 8, length), lambda n: (n, 0, 0)),
            pl.BlockSpec(factors.shape, lambda n: (0, 0, 0)),
            pl.BlockSpec(kept.shape, lambda n: (0, 0)),
        ],
        out_specs=(
            pl.BlockSpec((2, tiles // parts, 8, width), lambda n: (0, n, 0, 0)),
            pl.BlockSpec((planes, length // parts, length), lambda n: (0, n, 0)),
            pl.BlockSpec(kept.shape, lambda n: (0, 0)),
        ),
    )(settled, rotated, factors, kept)
    return (new_object.reshape(object_field.shape), modes.reshape(probe_modes.shape), weights)


def solution(mesh):
    placed = (
        P(None, "scan", "col"),
        P(("scan", "col"), None, None),
        P(("scan", "col"), None),
        P(("scan", "col")),
        P(("scan", "col"), None),
        P(),
    )
    return jax.shard_map(
        on_device,
        mesh=mesh,
        in_specs=placed,
        out_specs=(P(None, "scan", "col"), P(), P(("scan", "col"), None)),
        check_vma=False,
    )
```

```python
import functools
import math

import jax
import jax.numpy as jnp
import ml_dtypes
import numpy as np
from jax import lax
from jax.experimental import pallas as pl
from jax.experimental.pallas import tpu as pltpu
from jax.sharding import PartitionSpec as P

ITERS = 2
CHUNKS = 8

VMEM = pl.BlockSpec(memory_space=pltpu.VMEM)
SMEM = pl.BlockSpec(memory_space=pltpu.SMEM)
ANY = pl.BlockSpec(memory_space=pl.ANY)


def make_tables(length):
    indices = np.arange(length, dtype=np.int32)
    phases = indices[:, None] * indices[None, :] % length
    angles = phases.astype(np.float32) * np.float32(2.0 * math.pi / length)
    factor = np.float32(1.0 / math.sqrt(length))
    cosine = np.cos(angles) * factor
    sine = np.sin(angles) * factor
    rows_table = np.block([[cosine, sine], [-sine, cosine]])
    cols_table = np.block([[cosine, -sine], [sine, cosine]])
    return (rows_table.astype(ml_dtypes.bfloat16), cols_table.astype(ml_dtypes.bfloat16))


def apply_transform(stacked, first_table, second_table):
    length = stacked.shape[1]
    halfway = jnp.dot(first_table, stacked, preferred_element_type=jnp.float32).astype(jnp.bfloat16)
    beside = jnp.concatenate([halfway[:length], halfway[length:]], 1)
    return jnp.dot(beside, second_table, preferred_element_type=jnp.float32)


def bits_of(axis, count):
    return [(axis, 1 << b) for b in range(count.bit_length() - 1)]


def stream_orders(scan_count, col_count, units):
    scan, col = bits_of("scan", scan_count), bits_of("col", col_count)
    core, y, x, z, w = col[:1], col[1:], scan[:1], scan[1:3], scan[3:]
    orders = [[core, y, z, x, w], [core, z, y, x, w], [core, x, y, z, w], [core, y, x, z, w]]
    shares = units // (scan_count * col_count)
    if shares < len(orders):
        orders = orders[2:]
    elif shares >= 2 * len(orders):
        orders = 2 * orders
    return [[group for group in order if group] for order in orders]


def reach(device, source, target, send_sem, recv_sem):
    return pltpu.make_async_remote_copy(
        src_ref=source,
        dst_ref=target,
        send_sem=send_sem,
        recv_sem=recv_sem,
        device_id=device,
        device_id_type=pl.DeviceIdType.MESH,
    )


class Shift:
    def __init__(self, copy, sends, receives):
        self.copy, self.sends, self.receives = copy, sends, receives

    def start(self):
        pl.when(self.sends)(self.copy.start)

    def arrive(self):
        pl.when(self.receives)(self.copy.wait_recv)

    def leave(self):
        pl.when(self.sends)(self.copy.wait_send)


class Place:
    def __init__(self, scan_count, col_count):
        self.scan, self.col = lax.axis_index("scan"), lax.axis_index("col")
        self.right = (self.scan, lax.rem(self.col + 1, col_count))
        self.left = (self.scan, lax.rem(self.col + col_count - 1, col_count))
        self.down = (lax.rem(self.scan + 1, scan_count), self.col)
        self.up = (lax.rem(self.scan + scan_count - 1, scan_count), self.col)
        self.has_right, self.has_left = self.col < col_count - 1, self.col > 0
        self.has_down, self.has_up = self.scan < scan_count - 1, self.scan > 0
        self.beyond = (self.down[0], self.right[1])
        self.before = (self.up[0], self.left[1])
        self.has_beyond = jnp.logical_and(self.has_down, self.has_right)
        self.has_before = jnp.logical_and(self.has_up, self.has_left)

    def sides(self):
        return (
            (self.right, self.has_right), (self.left, self.has_left),
            (self.down, self.has_down), (self.up, self.has_up),
            (self.beyond, self.has_beyond), (self.before, self.has_before),
        )

    def bit(self, axis, bit):
        at = self.scan if axis == "scan" else self.col
        return at // bit % 2

    def index(self, group, flips):
        total = 0
        for b, (axis, bit) in enumerate(group):
            mine = self.bit(axis, bit)
            total = total + (1 - mine if flips >> b & 1 else mine) * (1 << b)
        return total

    def partner(self, group, flips):
        scan, col = self.scan, self.col
        for b, (axis, bit) in enumerate(group):
            if flips >> b & 1:
                step = bit - 2 * bit * self.bit(axis, bit)
                if axis == "scan":
                    scan = scan + step
                else:
                    col = col + step
        return (scan, col)

    def greet(self, groups):
        barrier = pltpu.get_barrier_semaphore()
        partners = [self.partner(group, flips) for group in groups for flips in range(1, 1 << len(group))]

        def signal(device):
            pl.semaphore_signal(barrier, inc=1, device_id=device, device_id_type=pl.DeviceIdType.MESH)

        for device in partners:
            signal(device)
        for device, there in self.sides():
            pl.when(there)(functools.partial(signal, device))
        present = [there.astype(jnp.int32) for _, there in self.sides()]
        pl.semaphore_wait(barrier, len(partners) + sum(present))


class Stream:
    def __init__(self, place, order, base, count, terms, landed, send_sems, recv_sems):
        self.place, self.order = place, order
        self.terms, self.landed = terms, landed
        self.send_sems, self.recv_sems = send_sems, recv_sems
        self.bases, self.counts, self.slots, self.marks = [base], [count], [], []
        self.copies = {}
        slot, mark = base, 0
        for group in order:
            members = 1 << len(group)
            part = self.counts[-1] // members
            self.bases.append(self.bases[-1] + place.index(group, 0) * part)
            self.counts.append(part)
            self.slots.append(slot)
            self.marks.append(mark)
            slot += part * (members - 1)
            mark += members - 1
        self.total = mark

    def flips(self, s):
        return range(1, 1 << len(self.order[s]))

    def scatter(self, s):
        part = self.counts[s + 1]
        for flips in self.flips(s):
            group = self.order[s]
            source = self.terms.at[pl.ds(self.bases[s] + self.place.index(group, flips) * part, part)]
            target = self.landed.at[pl.ds(self.slots[s] + (flips - 1) * part, part)]
            at = self.marks[s] + flips - 1
            copy = reach(
                self.place.partner(group, flips), source, target, self.send_sems.at[at], self.recv_sems.at[at]
            )
            copy.start()
            self.copies["scatter", s, flips] = copy

    def offer(self, grads, mates, first, half):
        group = self.order[0]
        start = (first + self.place.index(group, 1) * half) * 8
        rows = pl.ds(pl.multiple_of(start, 8), half * 8)
        copy = reach(
            self.place.partner(group, 1), grads.at[:, :, rows, :], mates.at[:, :, rows, :],
            self.send_sems.at[0], self.recv_sems.at[0],
        )
        copy.start()
        self.copies["scatter", 0, 1] = copy

    def gathered(self, s):
        part = self.counts[s + 1]
        at = pl.ds(self.bases[s + 1], part)
        value = self.terms[at]
        for flips in self.flips(s):
            self.copies["scatter", s, flips].wait_recv()
            value = value + self.landed[pl.ds(self.slots[s] + (flips - 1) * part, part)]
        return at, value

    def spread(self, s, raised):
        piece = raised.at[pl.ds(self.bases[s + 1], self.counts[s + 1])]
        for flips in self.flips(s):
            at = self.total + self.marks[s] + flips - 1
            copy = reach(
                self.place.partner(self.order[s], flips), piece, piece,
                self.send_sems.at[at], self.recv_sems.at[at],
            )
            copy.start()
            self.copies["gather", s, flips] = copy

    def arrived(self, s):
        for flips in self.flips(s):
            self.copies["gather", s, flips].wait_recv()

    def leave(self):
        for copy in self.copies.values():
            copy.wait_send()


class Halo:
    def __init__(self, place, wide, tiles, width, send_sems, recv_sems):
        rows = tiles // CHUNKS
        near, far = pl.ds(0, width), pl.ds(width, width)
        self.up, self.side, self.corner = [], [], []
        for q in range(CHUNKS):
            top, low = pl.ds(q * rows, rows), pl.ds(tiles + q * rows, rows)
            self.up.append(Shift(
                reach(place.up, wide.at[:, top, :, near], wide.at[:, low, :, near], send_sems.at[0, q], recv_sems.at[0, q]),
                place.has_up, place.has_down,
            ))
            self.side.append(Shift(
                reach(place.left, wide.at[:, top, :, near], wide.at[:, top, :, far], send_sems.at[1, q], recv_sems.at[1, q]),
                place.has_left, place.has_right,
            ))
            self.corner.append(Shift(
                reach(place.left, wide.at[:, low, :, near], wide.at[:, low, :, far], send_sems.at[2, q], recv_sems.at[2, q]),
                place.has_left, place.has_right,
            ))

    def begin(self, q):
        self.up[q].start()
        self.side[q].start()

    def turn(self, q):
        self.up[q].arrive()
        self.corner[q].start()

    def end(self):
        for shift in self.side + self.corner:
            shift.arrive()

    def leave(self):
        for shift in self.up + self.side + self.corner:
            shift.leave()


def step_kernel(
    scan_count, col_count, mode_count, root_total,
    count, positions, first_weights, field, far_amplitudes, far_modes, far_rows, far_cols,
    new_object, last_raised, factors, new_weights,
    amplitudes, first_modes, rows_table, cols_table, input_sems,
    wide, totals, held, den, powers, probes, grads, mates, given, taken, terms, landed, raised, middle_modes, middle_weights,
    sideways, fallen, bottom,
    stream_send, stream_recv, halo_send, halo_recv, side_send, side_recv,
):
    tiles, _, width = field.shape[1:]
    height = 8 * tiles
    frames, length = amplitudes.shape[:2]
    planes = 2 * mode_count
    blocks = length // 8
    units = blocks * planes
    pixels = float(length * length)
    full_width = width + length
    rows_of_chunk = tiles // CHUNKS
    place = Place(scan_count, col_count)
    near, far = pl.ds(0, width), pl.ds(width, width)
    top, low = pl.ds(0, tiles), pl.ds(tiles, tiles)
    pairs = [(i, j) for j in range(mode_count) for i in range(j + 1)]
    strict = [(i, j) for i, j in pairs if i < j]
    leaving = []
    ups = [raised.at[i] for i in range(ITERS - 1)] + [last_raised]

    def chunk(q, offset=0):
        return pl.ds(offset + q * rows_of_chunk, rows_of_chunk)

    def block_rows(block):
        return pl.ds(pl.multiple_of(block * 8, 8), 8)

    loads = [
        pltpu.make_async_copy(source, target, input_sems.at[n])
        for n, (source, target) in enumerate((
            (far_modes, first_modes), (far_rows, rows_table), (far_cols, cols_table), (far_amplitudes, amplitudes),
        ))
    ]
    for load in loads:
        load.start()

    wide[0, :, :tiles, :, :width] = field[...]

    @pl.when(jnp.logical_not(place.has_left))
    def _():
        sideways[...] = jnp.zeros_like(sideways)

    @pl.when(jnp.logical_not(place.has_up))
    def _():
        fallen[...] = jnp.zeros_like(fallen)

    for slot, there in ((1, place.has_left), (2, place.has_up), (3, place.has_before)):

        @pl.when(jnp.logical_not(there))
        def _():
            for i in range(ITERS):
                taken[i, slot] = jnp.zeros(taken.shape[2:], jnp.float32)

    orders = stream_orders(scan_count, col_count, units)
    place.greet(orders[0])
    halos = [
        Halo(place, wide.at[i], tiles, width, halo_send.at[i], halo_recv.at[i]) for i in range(ITERS)
    ]
    for q in range(CHUNKS):
        halos[0].begin(q)
    def live(slot):
        return slot < count[0]

    def inside(value, limit):
        return jnp.minimum(jnp.maximum(value, 0), limit - 1)

    corners = [
        (
            inside(positions[g, 0] - place.scan * height, height),
            inside(positions[g, 1] - place.col * width, width),
        )
        for g in range(frames)
    ]

    def turned(piece, row, col):
        return pltpu.roll(pltpu.roll(piece, row, 0), col, 1)

    def hold(plane, slot, piece):
        row, col = corners[slot]
        held[plane, slot] = turned(piece, row, col).reshape(tiles, 8, width)

    lanes = lax.broadcasted_iota(jnp.int32, (8, width), 1)
    sublanes = lax.broadcasted_iota(jnp.int32, (8, width), 0)

    def settle(i):
        def move(n, carry):
            for plane in range(2):
                quarters = [0.0] * 4
                for g in range(frames):
                    row, col = corners[g]
                    value = held[plane, g, n]
                    below, beyond = sublanes + 8 * n < row, lanes < col
                    upper, lower = jnp.where(below, 0.0, value), jnp.where(below, value, 0.0)
                    for at, half in ((0, upper), (2, lower)):
                        quarters[at] += jnp.where(beyond, 0.0, half)
                        quarters[at + 1] += jnp.where(beyond, half, 0.0)
                totals[i, plane, n, :, :width] = quarters[0]
                totals[i, plane, n, :, width:] = quarters[1]
                totals[i, plane, tiles + n, :, :width] = quarters[2]
                totals[i, plane, tiles + n, :, width:] = quarters[3]
            return carry

        lax.fori_loop(0, tiles, move, 0, unroll=4)

    def cut(i, plane, slot):
        row, col = corners[slot]
        picked = []
        for n in range(tiles):
            below, beyond = sublanes + 8 * n < row, lanes < col
            upper, lower = wide[i, plane, n], wide[i, plane, tiles + n]
            left = jnp.where(below, lower[:, :width], upper[:, :width])
            right = jnp.where(below, lower[:, width:], upper[:, width:])
            picked.append(jnp.where(beyond, right, left))
        return turned(
            jnp.concatenate(picked, 0), lax.rem(height - row, height), lax.rem(width - col, width)
        )

    def masked(weights):
        table = [[weights[g:g + 1, k:k + 1] for k in range(mode_count)] for g in range(frames)]
        return [[jnp.where(live(g), w, 0.0) for w in row] for g, row in enumerate(table)]

    def wave(weights, tiles):
        out = []
        for g in range(frames):
            for part in range(2):
                value = weights[g][0] * tiles[part]
                for k in range(1, mode_count):
                    value = value + weights[g][k] * tiles[2 * k + part]
                out.append(value)
        return out

    def fold(value):
        total = value[:, :128]
        for at in range(128, length, 128):
            total = total + value[:, at:at + 128]
        return total

    def whole(value):
        return jnp.sum(jnp.sum(value, 0, keepdims=True), 1, keepdims=True)

    def run_frame(i, g):
        object_real = cut(i, 0, g)
        object_imag = cut(i, 1, g)
        probe_real, probe_imag = probes[g, 0], probes[g, 1]
        exit_real = probe_real * object_real - probe_imag * object_imag
        exit_imag = probe_real * object_imag + probe_imag * object_real
        stacked = jnp.concatenate([exit_real, exit_imag], 0).astype(jnp.bfloat16)
        far_field = apply_transform(stacked, rows_table[...], cols_table[...])
        far_real, far_imag = far_field[:, :length], far_field[:, length:]
        magnitude = jnp.sqrt(far_real * far_real + far_imag * far_imag)
        factor = amplitudes[g].astype(jnp.float32) / jnp.maximum(magnitude, 0.5)
        scaled = jnp.concatenate([far_real * factor, far_imag * factor], 0).astype(jnp.bfloat16)
        back = apply_transform(scaled, cols_table[...], rows_table[...])
        diff_real = back[:, :length] - exit_real
        diff_imag = back[:, length:] - exit_imag
        grads[i, g, 0] = object_real * diff_real + object_imag * diff_imag
        grads[i, g, 1] = object_real * diff_imag - object_imag * diff_real
        hold(0, g, probe_real * diff_real + probe_imag * diff_imag)
        hold(1, g, probe_real * diff_imag - probe_imag * diff_real)

    weights = masked(first_weights)
    mate = place.partner(orders[0][0], 1)

    def tell(i):
        for g in range(frames):
            for k in range(mode_count):
                given[i, g:g + 1, k:k + 1] = weights[g][k]
            for at, value in enumerate(corners[g]):
                given[i, g:g + 1, mode_count + at:mode_count + at + 1] = jnp.full((1, 1), value, jnp.int32).astype(jnp.float32)
        for telling in tellings[i]:
            telling.start()

    def telling_to(i, slot, device, sends, receives):
        at = 3 * CHUNKS + slot
        return Shift(
            reach(device, given.at[i], taken.at[i, slot], side_send.at[i, at], side_recv.at[i, at]), sends, receives
        )

    always = place.col >= 0
    tellings = [
        [
            telling_to(i, 0, mate, always, always),
            telling_to(i, 1, place.right, place.has_right, place.has_left),
            telling_to(i, 2, place.down, place.has_down, place.has_up),
            telling_to(i, 3, place.beyond, place.has_beyond, place.has_before),
        ]
        for i in range(ITERS)
    ]
    tell(0)

    def first_wave(block, carry):
        rows = block_rows(block)
        values = wave(weights, [first_modes[p, rows, :] for p in range(planes)])
        for at, value in enumerate(values):
            probes[at // 2, at % 2, rows, :] = value
        return carry

    loads[0].wait()
    lax.fori_loop(0, blocks, first_wave, 0, unroll=4)
    for load in loads[1:]:
        load.wait()

    for i in range(ITERS):
        again = i < ITERS - 1
        modes = first_modes if i == 0 else middle_modes
        kept_weights = first_weights if i == 0 else middle_weights

        def rightward(at, source, target):
            copy = reach(place.right, source, target, side_send.at[i, at], side_recv.at[i, at])
            return Shift(copy, place.has_right, place.has_left)

        def downward(at, source, target):
            copy = reach(place.down, source, target, side_send.at[i, at], side_recv.at[i, at])
            return Shift(copy, place.has_down, place.has_up)

        pair = pl.ds(0, 2)
        low_rights = [
            rightward(q, totals.at[i, pair, chunk(q, tiles), :, far], sideways.at[i, pair, chunk(q, tiles)])
            for q in range(CHUNKS)
        ]
        top_rights = [
            rightward(CHUNKS + q, totals.at[i, pair, chunk(q), :, far], sideways.at[i, pair, chunk(q)])
            for q in range(CHUNKS)
        ]
        downs = [
            downward(2 * CHUNKS + q, bottom.at[i, pair, chunk(q)], fallen.at[i, pair, chunk(q)])
            for q in range(CHUNKS)
        ]
        leaving += low_rights + top_rights + downs

        if i == 0:
            for q in range(CHUNKS):
                halos[0].turn(q)
        halos[i].end()
        for g in range(frames):
            run_frame(i, g)
        settle(i)
        for q in range(CHUNKS):
            low_rights[q].start()

        stages = len(orders[0])
        share = units // len(orders)
        streams = [
            Stream(
                place, order, t * share, share, terms.at[i], landed.at[i],
                stream_send.at[i, t], stream_recv.at[i, t],
            )
            for t, order in enumerate(orders)
        ]
        leaving += streams

        def term_step(block, carry):
            rows = block_rows(block)
            tiles_ = [ref[i, g, part, rows, :] for ref in (grads, mates) for g in range(frames) for part in range(2)]
            for k in range(mode_count):
                for part in range(2):
                    value = joint[0][k] * tiles_[part]
                    for g in range(1, 2 * frames):
                        value = value + joint[g][k] * tiles_[2 * g + part]
                    terms[i, block * planes + 2 * k + part] = value
            return carry

        half = share // planes // 2
        for t, stream in enumerate(streams):
            stream.offer(grads.at[i], mates.at[i], t * 2 * half, half)
        for q in range(CHUNKS):
            top_rights[q].start()

        for telling in tellings[i]:
            telling.arrive()
        joint = weights + [[taken[i, 0, g:g + 1, k:k + 1] for k in range(mode_count)] for g in range(frames)]
        joint = [[jnp.broadcast_to(w, (8, length)) for w in row] for row in joint]

        def finish_scatter(t, s):
            stream = streams[t]
            if s == 0:
                stream.copies["scatter", 0, 1].wait_recv()
                first = stream.bases[1] // planes
                lax.fori_loop(0, half, lambda n, carry: term_step(first + n, carry), 0, unroll=min(half, 4))
                stream.scatter(1)
                return
            at, value = stream.gathered(s)
            if s < stages - 1:
                terms[i, at] = value
                stream.scatter(s + 1)
                return
            first, target = stream.bases[s + 1], ups[i]
            for n in range(stream.counts[s + 1]):
                unit = first + n
                kept = modes[unit % planes, block_rows(unit // planes), :]
                target[unit] = kept + value[n] / root_total
            stream.spread(s, ups[i])

        sums = [jnp.zeros((8, 128), jnp.float32)] * (len(pairs) + len(strict) + 2 * mode_count * frames)

        def fit_step(block, sums):
            rows = block_rows(block)
            tiles = [ups[i][block * planes + p] for p in range(planes)]
            real, imag = tiles[0::2], tiles[1::2]
            terms_ = [fold(real[a] * real[b] + imag[a] * imag[b]) for a, b in pairs]
            terms_ += [fold(real[a] * imag[b] - imag[a] * real[b]) for a, b in strict]
            for g in range(frames):
                held_real = probes[g, 0, rows, :] + 0.5 * grads[i, g, 0, rows, :]
                held_imag = probes[g, 1, rows, :] + 0.5 * grads[i, g, 1, rows, :]
                for a in range(mode_count):
                    terms_.append(fold(real[a] * held_real + imag[a] * held_imag))
                    terms_.append(fold(real[a] * held_imag - imag[a] * held_real))
            return tuple(a + b for a, b in zip(sums, terms_))

        def finish_gather(t, s):
            nonlocal sums
            streams[t].arrived(s)
            if s > 0:
                streams[t].spread(s - 1, ups[i])
            else:
                per = share // planes
                sums = lax.fori_loop(t * per, (t + 1) * per, fit_step, tuple(sums), unroll=2)

        def drop(q):
            low_rights[q].arrive()
            bottom[i, :2, chunk(q)] = totals[i, :2, chunk(q, tiles), :, near] + sideways[i, :2, chunk(q, tiles)]
            downs[q].start()

        def renew(q):
            top_rights[q].arrive()
            downs[q].arrive()
            update = [
                totals[i, p, chunk(q), :, near] + sideways[i, p, chunk(q)] + fallen[i, p, chunk(q)]
                for p in range(2)
            ]
            scale = 1.0 / (den[chunk(q)] + 1.0)
            for p in range(2):
                value = wide[i, p, chunk(q), :, near] + update[p] * scale
                if again:
                    wide[i + 1, p, chunk(q), :, near] = value
                else:
                    new_object[p, chunk(q)] = value
            if again:
                halos[i + 1].begin(q)

        def weigh():
            near_weights = [
                [
                    [jnp.broadcast_to(taken[i, slot, g:g + 1, k:k + 1], (8, length)) for k in range(mode_count)]
                    for g in range(frames)
                ]
                for slot in range(1, 4)
            ]

            def power_step(block, carry):
                rows = block_rows(block)
                tiles_ = [modes[p, rows, :] for p in range(planes)]
                values = [probes[g, part, rows, :] for g in range(frames) for part in range(2)]
                for weights_ in near_weights:
                    values += wave(weights_, tiles_)
                for n in range(4 * frames):
                    real, imag = values[2 * n], values[2 * n + 1]
                    powers[n // frames, n % frames, rows, :] = real * real + imag * imag
                return carry

            lax.fori_loop(0, blocks, power_step, 0, unroll=2)
            spots = [list(corners)]
            for slot in range(1, 4):
                spots.append([
                    tuple(
                        inside(jnp.sum(taken[i, slot, g:g + 1, at:at + 1]).astype(jnp.int32), limit)
                        for at, limit in ((mode_count, height), (mode_count + 1, width))
                    )
                    for g in range(frames)
                ])
            for slot in range(4):
                for g in range(frames):
                    powers[slot, g] = turned(powers[slot, g], *spots[slot][g])

            def den_step(n, carry):
                rows = block_rows(n)
                total = 0.0
                for slot in range(4):
                    for g in range(frames):
                        row, col = spots[slot][g]
                        below, beyond = sublanes + 8 * n < row, lanes < col
                        if slot < 2:
                            below = jnp.logical_not(below)
                        if slot % 2 == 0:
                            beyond = jnp.logical_not(beyond)
                        total = total + jnp.where(jnp.logical_and(below, beyond), powers[slot, g, rows, :], 0.0)
                den[n] = total
                return carry

            lax.fori_loop(0, tiles, den_step, 0, unroll=2)

        def turn(q):
            if again:
                halos[i + 1].turn(q)

        steps = [functools.partial(finish_scatter, t, s) for s in range(stages) for t in range(len(streams))]
        steps += [
            functools.partial(finish_gather, t, s)
            for s in range(stages - 1, -1, -1) for t in range(len(streams))
        ]
        drops, turns = (4, 4, 5, 5, 6, 6, 7, 7), (18, 19, 20, 21, 22, 23, 24, 27)
        renews = (9, 10, 11, 12, 13, 14, 15, 16) if again else (13, 14, 15, 16, 18, 20, 21, 22)
        marks = [(drop, drops), (renew, renews), (turn, turns)]
        for n, step in enumerate(steps):
            if n == len(steps) * 6 // 32:
                weigh()
            for task, whens in marks:
                for q, when in enumerate(whens):
                    if when * len(steps) // 32 == n:
                        task(q)
            step()

        totals_of = [whole(s) / pixels for s in sums]
        gram_real = dict(zip(pairs, totals_of))
        gram_imag = dict(zip(strict, totals_of[len(pairs):]))
        upper_real, upper_imag = {}, {}
        for b in range(mode_count):
            for a in range(b):
                sum_real, sum_imag = gram_real[a, b], gram_imag[a, b]
                for k in range(a):
                    r, s, u, v = upper_real[k, a], upper_imag[k, a], upper_real[k, b], upper_imag[k, b]
                    sum_real = sum_real - (r * u + s * v)
                    sum_imag = sum_imag - (r * v - s * u)
                upper_real[a, b] = sum_real / upper_real[a, a]
                upper_imag[a, b] = sum_imag / upper_real[a, a]
            diagonal = gram_real[b, b]
            for k in range(b):
                diagonal = diagonal - (upper_real[k, b] * upper_real[k, b] + upper_imag[k, b] * upper_imag[k, b])
            upper_real[b, b] = jnp.sqrt(diagonal)
        inverse = {b: 1.0 / upper_real[b, b] for b in range(mode_count)}

        refit_weights = []
        at = len(pairs) + len(strict)
        for g in range(frames):
            inner = []
            for k in range(mode_count):
                real, imag = totals_of[at], totals_of[at + 1]
                at += 2
                for a in range(k):
                    r, s, u, v = upper_real[a, k], upper_imag[a, k], inner[a][0], inner[a][1]
                    real = real - (r * u + s * v)
                    imag = imag - (r * v - s * u)
                inner.append((real * inverse[k], imag * inverse[k]))
            refit_weights.append([
                jnp.where(live(g), inner[k][0], kept_weights[g:g + 1, k:k + 1]) for k in range(mode_count)
            ])
        target_weights = middle_weights if again else new_weights
        for g in range(frames):
            for k in range(mode_count):
                target_weights[g:g + 1, k:k + 1] = refit_weights[g][k]
        weights = [[jnp.where(live(g), w, 0.0) for w in row] for g, row in enumerate(refit_weights)]
        if again:
            tell(i + 1)

        def spread_out(value):
            return jnp.broadcast_to(value, (8, length))

        upper_real = {p: spread_out(v) for p, v in upper_real.items() if p[0] < p[1]}
        upper_imag = {p: spread_out(v) for p, v in upper_imag.items()}
        inverse = {p: spread_out(v) for p, v in inverse.items()}
        wave_weights = [[spread_out(w) for w in row] for row in weights]

        def basis_step(block, carry):
            rows = block_rows(block)
            basis = []
            for b in range(mode_count):
                real, imag = ups[i][block * planes + 2 * b], ups[i][block * planes + 2 * b + 1]
                for a in range(b):
                    r, s = upper_real[a, b], upper_imag[a, b]
                    u, v = basis[2 * a], basis[2 * a + 1]
                    real = real - (r * u - s * v)
                    imag = imag - (r * v + s * u)
                basis += [real * inverse[b], imag * inverse[b]]
            for p in range(planes):
                middle_modes[p, rows, :] = basis[p]
            for n, value in enumerate(wave(wave_weights, basis)):
                probes[n // 2, n % 2, rows, :] = value
            return carry

        if again:
            lax.fori_loop(0, blocks, basis_step, 0, unroll=4)
        else:
            rows_ = [inverse[b] for b in range(mode_count)]
            rows_ += [upper_real[p] for p in strict] + [upper_imag[p] for p in strict]
            for n, row in enumerate(rows_):
                factors[n] = row

    for item in leaving + halos:
        item.leave()
    for telling in sum(tellings, []):
        telling.leave()


def finish_kernel(mode_count, settled, rotated, factors, kept_weights, new_object, new_modes, new_weights):
    planes = 2 * mode_count
    pairs = [(i, j) for j in range(mode_count) for i in range(j)]
    new_object[...] = settled[...]
    new_weights[...] = kept_weights[...]
    inverse = [factors[b] for b in range(mode_count)]
    upper_real = {p: factors[mode_count + n] for n, p in enumerate(pairs)}
    upper_imag = {p: factors[mode_count + len(pairs) + n] for n, p in enumerate(pairs)}
    for block in range(rotated.shape[0] // planes):
        basis = []
        for b in range(mode_count):
            real, imag = rotated[block * planes + 2 * b], rotated[block * planes + 2 * b + 1]
            for a in range(b):
                r, s = upper_real[a, b], upper_imag[a, b]
                u, v = basis[2 * a], basis[2 * a + 1]
                real = real - (r * u - s * v)
                imag = imag - (r * v + s * u)
            basis += [real * inverse[b], imag * inverse[b]]
        for p in range(planes):
            new_modes[p, block * 8:block * 8 + 8, :] = basis[p]


def shape(*dims):
    return jax.ShapeDtypeStruct(dims, jnp.float32)


def on_device(object_field, amplitudes, positions, frame_count, coefficients, probe_modes):
    frames, length = amplitudes.shape[:2]
    mode_count = probe_modes.shape[0]
    planes = 2 * mode_count
    height, width = object_field.shape[1:]
    scan_count = lax.axis_size("scan")
    col_count = lax.axis_size("col")
    root_total = math.sqrt(frames * scan_count * col_count)
    rows_table, cols_table = make_tables(length)
    tiles, blocks = height // 8, length // 8
    full_width = width + length
    units = planes * blocks
    orders = stream_orders(scan_count, col_count, units)
    partners = 2 * sum((1 << len(group)) - 1 for group in orders[0])

    def vmem(*dims):
        return pltpu.VMEM(dims, jnp.float32)

    stream_sems = pltpu.SemaphoreType.DMA((ITERS, len(orders), partners))
    halo_sems = pltpu.SemaphoreType.DMA((ITERS, 3, CHUNKS))
    side_sems = pltpu.SemaphoreType.DMA((ITERS, 3 * CHUNKS + 4))
    settled, rotated, factors, kept = pl.pallas_call(
        functools.partial(step_kernel, scan_count, col_count, mode_count, root_total),
        name="reconstruct",
        out_shape=(
            shape(2, tiles, 8, width), shape(units, 8, length), shape(mode_count * mode_count, 8, length),
            shape(frames, mode_count),
        ),
        in_specs=[SMEM] * 2 + [VMEM] * 2 + [ANY] * 4,
        out_specs=(VMEM,) * 4,
        scratch_shapes=[
            pltpu.VMEM(amplitudes.shape, amplitudes.dtype),
            vmem(planes, length, length),
            pltpu.VMEM(rows_table.shape, rows_table.dtype),
            pltpu.VMEM(cols_table.shape, cols_table.dtype),
            pltpu.SemaphoreType.DMA((4,)),
            vmem(ITERS, 2, tiles + blocks, 8, full_width),
            vmem(ITERS, 2, tiles + blocks, 8, full_width),
            vmem(2, frames, tiles, 8, width),
            vmem(tiles, 8, width),
            vmem(4, frames, length, length),
            vmem(frames, 2, length, length),
            vmem(ITERS, frames, 2, length, length),
            vmem(ITERS, frames, 2, length, length),
            vmem(ITERS, frames, mode_count + 2),
            vmem(ITERS, 4, frames, mode_count + 2),
            vmem(ITERS, units, 8, length),
            vmem(ITERS, units, 8, length),
            vmem(ITERS - 1, units, 8, length),
            vmem(planes, length, length),
            vmem(frames, mode_count),
            vmem(ITERS, 2, tiles + blocks, 8, width),
            vmem(ITERS, 2, tiles, 8, width),
            vmem(ITERS, 2, tiles, 8, width),
            stream_sems, stream_sems, halo_sems, halo_sems, side_sems, side_sems,
        ],
        compiler_params=pltpu.CompilerParams(
            collective_id=0, has_side_effects=True, vmem_limit_bytes=60 * 2**20
        ),
        cost_estimate=pl.CostEstimate(flops=5 * 10**9, bytes_accessed=10**7, transcendentals=0),
    )(
        frame_count, positions, coefficients, object_field.reshape(2, tiles, 8, width), amplitudes,
        probe_modes.reshape(planes, length, length), rows_table, cols_table,
    )
    parts = 2
    new_object, modes, weights = pl.pallas_call(
        functools.partial(finish_kernel, mode_count),
        name="finish",
        grid=(parts,),
        out_shape=(shape(2, tiles, 8, width), shape(planes, length, length), shape(frames, mode_count)),
        in_specs=[
            pl.BlockSpec((2, tiles // parts, 8, width), lambda n: (0, n, 0, 0)),
            pl.BlockSpec((units // parts, 8, length), lambda n: (n, 0, 0)),
            pl.BlockSpec(factors.shape, lambda n: (0, 0, 0)),
            pl.BlockSpec(kept.shape, lambda n: (0, 0)),
        ],
        out_specs=(
            pl.BlockSpec((2, tiles // parts, 8, width), lambda n: (0, n, 0, 0)),
            pl.BlockSpec((planes, length // parts, length), lambda n: (0, n, 0)),
            pl.BlockSpec(kept.shape, lambda n: (0, 0)),
        ),
    )(settled, rotated, factors, kept)
    return (new_object.reshape(object_field.shape), modes.reshape(probe_modes.shape), weights)


def solution(mesh):
    placed = (
        P(None, "scan", "col"),
        P(("scan", "col"), None, None),
        P(("scan", "col"), None),
        P(("scan", "col")),
        P(("scan", "col"), None),
        P(),
    )
    return jax.shard_map(
        on_device,
        mesh=mesh,
        in_specs=placed,
        out_specs=(P(None, "scan", "col"), P(), P(("scan", "col"), None)),
        check_vma=False,
    )
```

```python
import functools
import math

import jax
import jax.numpy as jnp
import ml_dtypes
import numpy as np
from jax import lax
from jax.experimental import pallas as pl
from jax.experimental.pallas import tpu as pltpu
from jax.sharding import PartitionSpec as P

ITERS = 2
CHUNKS = 8

VMEM = pl.BlockSpec(memory_space=pltpu.VMEM)
SMEM = pl.BlockSpec(memory_space=pltpu.SMEM)
ANY = pl.BlockSpec(memory_space=pl.ANY)


def make_tables(length):
    indices = np.arange(length, dtype=np.int32)
    phases = indices[:, None] * indices[None, :] % length
    angles = phases.astype(np.float32) * np.float32(2.0 * math.pi / length)
    factor = np.float32(1.0 / math.sqrt(length))
    cosine = np.cos(angles) * factor
    sine = np.sin(angles) * factor
    rows_table = np.block([[cosine, sine], [-sine, cosine]])
    cols_table = np.block([[cosine, -sine], [sine, cosine]])
    return (rows_table.astype(ml_dtypes.bfloat16), cols_table.astype(ml_dtypes.bfloat16))


def apply_transform(stacked, first_table, second_table):
    length = stacked.shape[1]
    halfway = jnp.dot(first_table, stacked, preferred_element_type=jnp.float32).astype(jnp.bfloat16)
    beside = jnp.concatenate([halfway[:length], halfway[length:]], 1)
    return jnp.dot(beside, second_table, preferred_element_type=jnp.float32)


def bits_of(axis, count):
    return [(axis, 1 << b) for b in range(count.bit_length() - 1)]


def stream_orders(scan_count, col_count, units):
    scan, col = bits_of("scan", scan_count), bits_of("col", col_count)
    core, y, x, z, w = col[:1], col[1:], scan[:1], scan[1:3], scan[3:]
    orders = [[core, y, z, x, w], [core, z, y, x, w], [core, x, y, z, w], [core, y, x, z, w]]
    shares = units // (scan_count * col_count)
    if shares < len(orders):
        orders = orders[2:]
    elif shares >= 2 * len(orders):
        orders = 2 * orders
    return [[group for group in order if group] for order in orders]


def reach(device, source, target, send_sem, recv_sem):
    return pltpu.make_async_remote_copy(
        src_ref=source,
        dst_ref=target,
        send_sem=send_sem,
        recv_sem=recv_sem,
        device_id=device,
        device_id_type=pl.DeviceIdType.MESH,
    )


class Shift:
    def __init__(self, copy, sends, receives):
        self.copy, self.sends, self.receives = copy, sends, receives

    def start(self):
        pl.when(self.sends)(self.copy.start)

    def arrive(self):
        pl.when(self.receives)(self.copy.wait_recv)

    def leave(self):
        pl.when(self.sends)(self.copy.wait_send)


class Place:
    def __init__(self, scan_count, col_count):
        self.scan, self.col = lax.axis_index("scan"), lax.axis_index("col")
        self.right = (self.scan, lax.rem(self.col + 1, col_count))
        self.left = (self.scan, lax.rem(self.col + col_count - 1, col_count))
        self.down = (lax.rem(self.scan + 1, scan_count), self.col)
        self.up = (lax.rem(self.scan + scan_count - 1, scan_count), self.col)
        self.has_right, self.has_left = self.col < col_count - 1, self.col > 0
        self.has_down, self.has_up = self.scan < scan_count - 1, self.scan > 0
        self.beyond = (self.down[0], self.right[1])
        self.before = (self.up[0], self.left[1])
        self.has_beyond = jnp.logical_and(self.has_down, self.has_right)
        self.has_before = jnp.logical_and(self.has_up, self.has_left)

    def sides(self):
        return (
            (self.right, self.has_right), (self.left, self.has_left),
            (self.down, self.has_down), (self.up, self.has_up),
            (self.beyond, self.has_beyond), (self.before, self.has_before),
        )

    def bit(self, axis, bit):
        at = self.scan if axis == "scan" else self.col
        return at // bit % 2

    def index(self, group, flips):
        total = 0
        for b, (axis, bit) in enumerate(group):
            mine = self.bit(axis, bit)
            total = total + (1 - mine if flips >> b & 1 else mine) * (1 << b)
        return total

    def partner(self, group, flips):
        scan, col = self.scan, self.col
        for b, (axis, bit) in enumerate(group):
            if flips >> b & 1:
                step = bit - 2 * bit * self.bit(axis, bit)
                if axis == "scan":
                    scan = scan + step
                else:
                    col = col + step
        return (scan, col)

    def greet(self, groups):
        barrier = pltpu.get_barrier_semaphore()
        partners = [self.partner(group, flips) for group in groups for flips in range(1, 1 << len(group))]

        def signal(device):
            pl.semaphore_signal(barrier, inc=1, device_id=device, device_id_type=pl.DeviceIdType.MESH)

        for device in partners:
            signal(device)
        for device, there in self.sides():
            pl.when(there)(functools.partial(signal, device))
        present = [there.astype(jnp.int32) for _, there in self.sides()]
        pl.semaphore_wait(barrier, len(partners) + sum(present))


class Stream:
    def __init__(self, place, order, base, count, terms, landed, send_sems, recv_sems):
        self.place, self.order = place, order
        self.terms, self.landed = terms, landed
        self.send_sems, self.recv_sems = send_sems, recv_sems
        self.bases, self.counts, self.slots, self.marks = [base], [count], [], []
        self.copies = {}
        slot, mark = base, 0
        for group in order:
            members = 1 << len(group)
            part = self.counts[-1] // members
            self.bases.append(self.bases[-1] + place.index(group, 0) * part)
            self.counts.append(part)
            self.slots.append(slot)
            self.marks.append(mark)
            slot += part * (members - 1)
            mark += members - 1
        self.total = mark

    def flips(self, s):
        return range(1, 1 << len(self.order[s]))

    def scatter(self, s):
        part = self.counts[s + 1]
        for flips in self.flips(s):
            group = self.order[s]
            source = self.terms.at[pl.ds(self.bases[s] + self.place.index(group, flips) * part, part)]
            target = self.landed.at[pl.ds(self.slots[s] + (flips - 1) * part, part)]
            at = self.marks[s] + flips - 1
            copy = reach(
                self.place.partner(group, flips), source, target, self.send_sems.at[at], self.recv_sems.at[at]
            )
            copy.start()
            self.copies["scatter", s, flips] = copy

    def offer(self, grads, mates, first, half):
        group = self.order[0]
        start = (first + self.place.index(group, 1) * half) * 8
        rows = pl.ds(pl.multiple_of(start, 8), half * 8)
        copy = reach(
            self.place.partner(group, 1), grads.at[:, :, rows, :], mates.at[:, :, rows, :],
            self.send_sems.at[0], self.recv_sems.at[0],
        )
        copy.start()
        self.copies["scatter", 0, 1] = copy

    def gathered(self, s):
        part = self.counts[s + 1]
        at = pl.ds(self.bases[s + 1], part)
        value = self.terms[at]
        for flips in self.flips(s):
            self.copies["scatter", s, flips].wait_recv()
            value = value + self.landed[pl.ds(self.slots[s] + (flips - 1) * part, part)]
        return at, value

    def spread(self, s, raised):
        piece = raised.at[pl.ds(self.bases[s + 1], self.counts[s + 1])]
        for flips in self.flips(s):
            at = self.total + self.marks[s] + flips - 1
            copy = reach(
                self.place.partner(self.order[s], flips), piece, piece,
                self.send_sems.at[at], self.recv_sems.at[at],
            )
            copy.start()
            self.copies["gather", s, flips] = copy

    def arrived(self, s):
        for flips in self.flips(s):
            self.copies["gather", s, flips].wait_recv()

    def leave(self):
        for copy in self.copies.values():
            copy.wait_send()


class Halo:
    def __init__(self, place, wide, tiles, width, send_sems, recv_sems):
        rows = tiles // CHUNKS
        near, far = pl.ds(0, width), pl.ds(width, width)
        self.up, self.side, self.corner = [], [], []
        for q in range(CHUNKS):
            top, low = pl.ds(q * rows, rows), pl.ds(tiles + q * rows, rows)
            self.up.append(Shift(
                reach(place.up, wide.at[:, top, :, near], wide.at[:, low, :, near], send_sems.at[0, q], recv_sems.at[0, q]),
                place.has_up, place.has_down,
            ))
            self.side.append(Shift(
                reach(place.left, wide.at[:, top, :, near], wide.at[:, top, :, far], send_sems.at[1, q], recv_sems.at[1, q]),
                place.has_left, place.has_right,
            ))
            self.corner.append(Shift(
                reach(place.left, wide.at[:, low, :, near], wide.at[:, low, :, far], send_sems.at[2, q], recv_sems.at[2, q]),
                place.has_left, place.has_right,
            ))

    def begin(self, q):
        self.up[q].start()
        self.side[q].start()

    def turn(self, q):
        self.up[q].arrive()
        self.corner[q].start()

    def end(self):
        for shift in self.side + self.corner:
            shift.arrive()

    def leave(self):
        for shift in self.up + self.side + self.corner:
            shift.leave()


def step_kernel(
    scan_count, col_count, mode_count, root_total,
    count, positions, first_weights, field, far_amplitudes, far_modes, far_rows, far_cols,
    new_object, last_raised, factors, new_weights,
    amplitudes, first_modes, rows_table, cols_table, input_sems,
    wide, totals, held, den, powers, probes, grads, mates, given, taken, terms, landed, raised, middle_modes, middle_weights,
    sideways, fallen, bottom,
    stream_send, stream_recv, halo_send, halo_recv, side_send, side_recv,
):
    tiles, _, width = field.shape[1:]
    height = 8 * tiles
    frames, length = amplitudes.shape[:2]
    planes = 2 * mode_count
    blocks = length // 8
    units = blocks * planes
    pixels = float(length * length)
    full_width = width + length
    rows_of_chunk = tiles // CHUNKS
    place = Place(scan_count, col_count)
    near, far = pl.ds(0, width), pl.ds(width, width)
    top, low = pl.ds(0, tiles), pl.ds(tiles, tiles)
    pairs = [(i, j) for j in range(mode_count) for i in range(j + 1)]
    strict = [(i, j) for i, j in pairs if i < j]
    leaving = []
    ups = [raised.at[i] for i in range(ITERS - 1)] + [last_raised]

    def chunk(q, offset=0):
        return pl.ds(offset + q * rows_of_chunk, rows_of_chunk)

    def block_rows(block):
        return pl.ds(pl.multiple_of(block * 8, 8), 8)

    loads = [
        pltpu.make_async_copy(source, target, input_sems.at[n])
        for n, (source, target) in enumerate((
            (far_modes, first_modes), (far_rows, rows_table), (far_cols, cols_table), (far_amplitudes, amplitudes),
        ))
    ]
    for load in loads:
        load.start()

    wide[0, :, :tiles, :, :width] = field[...]

    @pl.when(jnp.logical_not(place.has_left))
    def _():
        sideways[...] = jnp.zeros_like(sideways)

    @pl.when(jnp.logical_not(place.has_up))
    def _():
        fallen[...] = jnp.zeros_like(fallen)

    for slot, there in ((1, place.has_left), (2, place.has_up), (3, place.has_before)):

        @pl.when(jnp.logical_not(there))
        def _():
            for i in range(ITERS):
                taken[i, slot] = jnp.zeros(taken.shape[2:], jnp.float32)

    orders = stream_orders(scan_count, col_count, units)
    place.greet(orders[0])
    halos = [
        Halo(place, wide.at[i], tiles, width, halo_send.at[i], halo_recv.at[i]) for i in range(ITERS)
    ]
    for q in range(CHUNKS):
        halos[0].begin(q)
    def live(slot):
        return slot < count[0]

    def inside(value, limit):
        return jnp.minimum(jnp.maximum(value, 0), limit - 1)

    corners = [
        (
            inside(positions[g, 0] - place.scan * height, height),
            inside(positions[g, 1] - place.col * width, width),
        )
        for g in range(frames)
    ]

    def turned(piece, row, col):
        return pltpu.roll(pltpu.roll(piece, row, 0), col, 1)

    def hold(plane, slot, piece):
        row, col = corners[slot]
        held[plane, slot] = turned(piece, row, col).reshape(tiles, 8, width)

    lanes = lax.broadcasted_iota(jnp.int32, (8, width), 1)
    sublanes = lax.broadcasted_iota(jnp.int32, (8, width), 0)

    def settle(i):
        def move(n, carry):
            for plane in range(2):
                quarters = [0.0] * 4
                for g in range(frames):
                    row, col = corners[g]
                    value = held[plane, g, n]
                    below, beyond = sublanes + 8 * n < row, lanes < col
                    upper, lower = jnp.where(below, 0.0, value), jnp.where(below, value, 0.0)
                    for at, half in ((0, upper), (2, lower)):
                        quarters[at] += jnp.where(beyond, 0.0, half)
                        quarters[at + 1] += jnp.where(beyond, half, 0.0)
                totals[i, plane, n, :, :width] = quarters[0]
                totals[i, plane, n, :, width:] = quarters[1]
                totals[i, plane, tiles + n, :, :width] = quarters[2]
                totals[i, plane, tiles + n, :, width:] = quarters[3]
            return carry

        lax.fori_loop(0, tiles, move, 0, unroll=4)

    def cut(i, plane, slot):
        row, col = corners[slot]
        picked = []
        for n in range(tiles):
            below, beyond = sublanes + 8 * n < row, lanes < col
            upper, lower = wide[i, plane, n], wide[i, plane, tiles + n]
            left = jnp.where(below, lower[:, :width], upper[:, :width])
            right = jnp.where(below, lower[:, width:], upper[:, width:])
            picked.append(jnp.where(beyond, right, left))
        return turned(
            jnp.concatenate(picked, 0), lax.rem(height - row, height), lax.rem(width - col, width)
        )

    def masked(weights):
        table = [[weights[g:g + 1, k:k + 1] for k in range(mode_count)] for g in range(frames)]
        return [[jnp.where(live(g), w, 0.0) for w in row] for g, row in enumerate(table)]

    def wave(weights, tiles):
        out = []
        for g in range(frames):
            for part in range(2):
                value = weights[g][0] * tiles[part]
                for k in range(1, mode_count):
                    value = value + weights[g][k] * tiles[2 * k + part]
                out.append(value)
        return out

    def fold(value):
        total = value[:, :128]
        for at in range(128, length, 128):
            total = total + value[:, at:at + 128]
        return total

    def whole(value):
        return jnp.sum(jnp.sum(value, 0, keepdims=True), 1, keepdims=True)

    def run_frame(i, g):
        object_real = cut(i, 0, g)
        object_imag = cut(i, 1, g)
        probe_real, probe_imag = probes[g, 0], probes[g, 1]
        exit_real = probe_real * object_real - probe_imag * object_imag
        exit_imag = probe_real * object_imag + probe_imag * object_real
        stacked = jnp.concatenate([exit_real, exit_imag], 0).astype(jnp.bfloat16)
        far_field = apply_transform(stacked, rows_table[...], cols_table[...])
        far_real, far_imag = far_field[:, :length], far_field[:, length:]
        magnitude = jnp.sqrt(far_real * far_real + far_imag * far_imag)
        factor = amplitudes[g].astype(jnp.float32) / jnp.maximum(magnitude, 0.5)
        scaled = jnp.concatenate([far_real * factor, far_imag * factor], 0).astype(jnp.bfloat16)
        back = apply_transform(scaled, cols_table[...], rows_table[...])
        diff_real = back[:, :length] - exit_real
        diff_imag = back[:, length:] - exit_imag
        grads[i, g, 0] = object_real * diff_real + object_imag * diff_imag
        grads[i, g, 1] = object_real * diff_imag - object_imag * diff_real
        hold(0, g, probe_real * diff_real + probe_imag * diff_imag)
        hold(1, g, probe_real * diff_imag - probe_imag * diff_real)

    weights = masked(first_weights)
    mate = place.partner(orders[0][0], 1)

    def tell(i):
        for g in range(frames):
            for k in range(mode_count):
                given[i, g:g + 1, k:k + 1] = weights[g][k]
            for at, value in enumerate(corners[g]):
                given[i, g:g + 1, mode_count + at:mode_count + at + 1] = jnp.full((1, 1), value, jnp.int32).astype(jnp.float32)
        for telling in tellings[i]:
            telling.start()

    def telling_to(i, slot, device, sends, receives):
        at = 3 * CHUNKS + slot
        return Shift(
            reach(device, given.at[i], taken.at[i, slot], side_send.at[i, at], side_recv.at[i, at]), sends, receives
        )

    always = place.col >= 0
    tellings = [
        [
            telling_to(i, 0, mate, always, always),
            telling_to(i, 1, place.right, place.has_right, place.has_left),
            telling_to(i, 2, place.down, place.has_down, place.has_up),
            telling_to(i, 3, place.beyond, place.has_beyond, place.has_before),
        ]
        for i in range(ITERS)
    ]
    tell(0)

    def first_wave(block, carry):
        rows = block_rows(block)
        values = wave(weights, [first_modes[p, rows, :] for p in range(planes)])
        for at, value in enumerate(values):
            probes[at // 2, at % 2, rows, :] = value
        return carry

    loads[0].wait()
    lax.fori_loop(0, blocks, first_wave, 0, unroll=4)
    for load in loads[1:]:
        load.wait()

    for i in range(ITERS):
        again = i < ITERS - 1
        modes = first_modes if i == 0 else middle_modes
        kept_weights = first_weights if i == 0 else middle_weights

        def rightward(at, source, target):
            copy = reach(place.right, source, target, side_send.at[i, at], side_recv.at[i, at])
            return Shift(copy, place.has_right, place.has_left)

        def downward(at, source, target):
            copy = reach(place.down, source, target, side_send.at[i, at], side_recv.at[i, at])
            return Shift(copy, place.has_down, place.has_up)

        pair = pl.ds(0, 2)
        low_rights = [
            rightward(q, totals.at[i, pair, chunk(q, tiles), :, far], sideways.at[i, pair, chunk(q, tiles)])
            for q in range(CHUNKS)
        ]
        top_rights = [
            rightward(CHUNKS + q, totals.at[i, pair, chunk(q), :, far], sideways.at[i, pair, chunk(q)])
            for q in range(CHUNKS)
        ]
        downs = [
            downward(2 * CHUNKS + q, bottom.at[i, pair, chunk(q)], fallen.at[i, pair, chunk(q)])
            for q in range(CHUNKS)
        ]
        leaving += low_rights + top_rights + downs

        if i == 0:
            for q in range(CHUNKS):
                halos[0].turn(q)
        halos[i].end()
        for g in range(frames):
            run_frame(i, g)
        settle(i)
        for q in range(CHUNKS):
            low_rights[q].start()

        stages = len(orders[0])
        share = units // len(orders)
        streams = [
            Stream(
                place, order, t * share, share, terms.at[i], landed.at[i],
                stream_send.at[i, t], stream_recv.at[i, t],
            )
            for t, order in enumerate(orders)
        ]
        leaving += streams

        def term_step(block, carry):
            rows = block_rows(block)
            tiles_ = [ref[i, g, part, rows, :] for ref in (grads, mates) for g in range(frames) for part in range(2)]
            for k in range(mode_count):
                for part in range(2):
                    value = joint[0][k] * tiles_[part]
                    for g in range(1, 2 * frames):
                        value = value + joint[g][k] * tiles_[2 * g + part]
                    terms[i, block * planes + 2 * k + part] = value
            return carry

        half = share // planes // 2
        for t, stream in enumerate(streams):
            stream.offer(grads.at[i], mates.at[i], t * 2 * half, half)
        for q in range(CHUNKS):
            top_rights[q].start()

        for telling in tellings[i]:
            telling.arrive()
        joint = weights + [[taken[i, 0, g:g + 1, k:k + 1] for k in range(mode_count)] for g in range(frames)]
        joint = [[jnp.broadcast_to(w, (8, length)) for w in row] for row in joint]

        def finish_scatter(t, s):
            stream = streams[t]
            if s == 0:
                stream.copies["scatter", 0, 1].wait_recv()
                first = stream.bases[1] // planes
                lax.fori_loop(0, half, lambda n, carry: term_step(first + n, carry), 0, unroll=min(half, 4))
                stream.scatter(1)
                return
            at, value = stream.gathered(s)
            if s < stages - 1:
                terms[i, at] = value
                stream.scatter(s + 1)
                return
            first, target = stream.bases[s + 1], ups[i]
            for n in range(stream.counts[s + 1]):
                unit = first + n
                kept = modes[unit % planes, block_rows(unit // planes), :]
                target[unit] = kept + value[n] / root_total
            stream.spread(s, ups[i])

        sums = [jnp.zeros((8, 128), jnp.float32)] * (len(pairs) + len(strict) + 2 * mode_count * frames)

        def fit_step(block, sums):
            rows = block_rows(block)
            tiles = [ups[i][block * planes + p] for p in range(planes)]
            real, imag = tiles[0::2], tiles[1::2]
            terms_ = [fold(real[a] * real[b] + imag[a] * imag[b]) for a, b in pairs]
            terms_ += [fold(real[a] * imag[b] - imag[a] * real[b]) for a, b in strict]
            for g in range(frames):
                held_real = probes[g, 0, rows, :] + 0.5 * grads[i, g, 0, rows, :]
                held_imag = probes[g, 1, rows, :] + 0.5 * grads[i, g, 1, rows, :]
                for a in range(mode_count):
                    terms_.append(fold(real[a] * held_real + imag[a] * held_imag))
                    terms_.append(fold(real[a] * held_imag - imag[a] * held_real))
            return tuple(a + b for a, b in zip(sums, terms_))

        def finish_gather(t, s):
            nonlocal sums
            streams[t].arrived(s)
            if s > 0:
                streams[t].spread(s - 1, ups[i])
            else:
                per = share // planes
                sums = lax.fori_loop(t * per, (t + 1) * per, fit_step, tuple(sums), unroll=4)

        def drop(q):
            low_rights[q].arrive()
            bottom[i, :2, chunk(q)] = totals[i, :2, chunk(q, tiles), :, near] + sideways[i, :2, chunk(q, tiles)]
            downs[q].start()

        def renew(q):
            top_rights[q].arrive()
            downs[q].arrive()
            update = [
                totals[i, p, chunk(q), :, near] + sideways[i, p, chunk(q)] + fallen[i, p, chunk(q)]
                for p in range(2)
            ]
            scale = 1.0 / (den[chunk(q)] + 1.0)
            for p in range(2):
                value = wide[i, p, chunk(q), :, near] + update[p] * scale
                if again:
                    wide[i + 1, p, chunk(q), :, near] = value
                else:
                    new_object[p, chunk(q)] = value
            if again:
                halos[i + 1].begin(q)

        def weigh():
            near_weights = [
                [
                    [jnp.broadcast_to(taken[i, slot, g:g + 1, k:k + 1], (8, length)) for k in range(mode_count)]
                    for g in range(frames)
                ]
                for slot in range(1, 4)
            ]

            def power_step(block, carry):
                rows = block_rows(block)
                tiles_ = [modes[p, rows, :] for p in range(planes)]
                values = [probes[g, part, rows, :] for g in range(frames) for part in range(2)]
                for weights_ in near_weights:
                    values += wave(weights_, tiles_)
                for n in range(4 * frames):
                    real, imag = values[2 * n], values[2 * n + 1]
                    powers[n // frames, n % frames, rows, :] = real * real + imag * imag
                return carry

            lax.fori_loop(0, blocks, power_step, 0, unroll=4)
            spots = [list(corners)]
            for slot in range(1, 4):
                spots.append([
                    tuple(
                        inside(jnp.sum(taken[i, slot, g:g + 1, at:at + 1]).astype(jnp.int32), limit)
                        for at, limit in ((mode_count, height), (mode_count + 1, width))
                    )
                    for g in range(frames)
                ])
            for slot in range(4):
                for g in range(frames):
                    powers[slot, g] = turned(powers[slot, g], *spots[slot][g])

            def den_step(n, carry):
                rows = block_rows(n)
                total = 0.0
                for slot in range(4):
                    for g in range(frames):
                        row, col = spots[slot][g]
                        below, beyond = sublanes + 8 * n < row, lanes < col
                        if slot < 2:
                            below = jnp.logical_not(below)
                        if slot % 2 == 0:
                            beyond = jnp.logical_not(beyond)
                        total = total + jnp.where(jnp.logical_and(below, beyond), powers[slot, g, rows, :], 0.0)
                den[n] = total
                return carry

            lax.fori_loop(0, tiles, den_step, 0, unroll=4)

        def turn(q):
            if again:
                halos[i + 1].turn(q)

        steps = [functools.partial(finish_scatter, t, s) for s in range(stages) for t in range(len(streams))]
        steps += [
            functools.partial(finish_gather, t, s)
            for s in range(stages - 1, -1, -1) for t in range(len(streams))
        ]
        drops, turns = (4, 4, 5, 5, 6, 6, 7, 7), (13, 14, 15, 16, 17, 18, 19, 20)
        renews = (9, 10, 11, 12, 13, 14, 15, 16) if again else (13, 14, 15, 16, 18, 20, 21, 22)
        marks = [(drop, drops), (renew, renews), (turn, turns)]
        for n, step in enumerate(steps):
            if n == len(steps) * 6 // 32:
                weigh()
            for task, whens in marks:
                for q, when in enumerate(whens):
                    if when * len(steps) // 32 == n:
                        task(q)
            step()

        column = jnp.sum(jnp.concatenate([jnp.sum(s, 0, keepdims=True) for s in sums], 0), 1, keepdims=True) / pixels
        totals_of = [column[n:n + 1] for n in range(len(sums))]
        gram_real = dict(zip(pairs, totals_of))
        gram_imag = dict(zip(strict, totals_of[len(pairs):]))
        upper_real, upper_imag = {}, {}
        for b in range(mode_count):
            for a in range(b):
                sum_real, sum_imag = gram_real[a, b], gram_imag[a, b]
                for k in range(a):
                    r, s, u, v = upper_real[k, a], upper_imag[k, a], upper_real[k, b], upper_imag[k, b]
                    sum_real = sum_real - (r * u + s * v)
                    sum_imag = sum_imag - (r * v - s * u)
                upper_real[a, b] = sum_real / upper_real[a, a]
                upper_imag[a, b] = sum_imag / upper_real[a, a]
            diagonal = gram_real[b, b]
            for k in range(b):
                diagonal = diagonal - (upper_real[k, b] * upper_real[k, b] + upper_imag[k, b] * upper_imag[k, b])
            upper_real[b, b] = jnp.sqrt(diagonal)
        inverse = {b: 1.0 / upper_real[b, b] for b in range(mode_count)}

        refit_weights = []
        at = len(pairs) + len(strict)
        for g in range(frames):
            inner = []
            for k in range(mode_count):
                real, imag = totals_of[at], totals_of[at + 1]
                at += 2
                for a in range(k):
                    r, s, u, v = upper_real[a, k], upper_imag[a, k], inner[a][0], inner[a][1]
                    real = real - (r * u + s * v)
                    imag = imag - (r * v - s * u)
                inner.append((real * inverse[k], imag * inverse[k]))
            refit_weights.append([
                jnp.where(live(g), inner[k][0], kept_weights[g:g + 1, k:k + 1]) for k in range(mode_count)
            ])
        target_weights = middle_weights if again else new_weights
        for g in range(frames):
            for k in range(mode_count):
                target_weights[g:g + 1, k:k + 1] = refit_weights[g][k]
        weights = [[jnp.where(live(g), w, 0.0) for w in row] for g, row in enumerate(refit_weights)]
        if again:
            tell(i + 1)

        def spread_out(value):
            return jnp.broadcast_to(value, (8, length))

        upper_real = {p: spread_out(v) for p, v in upper_real.items() if p[0] < p[1]}
        upper_imag = {p: spread_out(v) for p, v in upper_imag.items()}
        inverse = {p: spread_out(v) for p, v in inverse.items()}
        wave_weights = [[spread_out(w) for w in row] for row in weights]

        def basis_step(block, carry):
            rows = block_rows(block)
            basis = []
            for b in range(mode_count):
                real, imag = ups[i][block * planes + 2 * b], ups[i][block * planes + 2 * b + 1]
                for a in range(b):
                    r, s = upper_real[a, b], upper_imag[a, b]
                    u, v = basis[2 * a], basis[2 * a + 1]
                    real = real - (r * u - s * v)
                    imag = imag - (r * v + s * u)
                basis += [real * inverse[b], imag * inverse[b]]
            for p in range(planes):
                middle_modes[p, rows, :] = basis[p]
            for n, value in enumerate(wave(wave_weights, basis)):
                probes[n // 2, n % 2, rows, :] = value
            return carry

        if again:
            lax.fori_loop(0, blocks, basis_step, 0, unroll=4)
        else:
            rows_ = [inverse[b] for b in range(mode_count)]
            rows_ += [upper_real[p] for p in strict] + [upper_imag[p] for p in strict]
            for n, row in enumerate(rows_):
                factors[n] = row

    for item in leaving + halos:
        item.leave()
    for telling in sum(tellings, []):
        telling.leave()


def finish_kernel(mode_count, settled, rotated, factors, kept_weights, new_object, new_modes, new_weights):
    planes = 2 * mode_count
    pairs = [(i, j) for j in range(mode_count) for i in range(j)]
    new_object[...] = settled[...]
    new_weights[...] = kept_weights[...]
    inverse = [factors[b] for b in range(mode_count)]
    upper_real = {p: factors[mode_count + n] for n, p in enumerate(pairs)}
    upper_imag = {p: factors[mode_count + len(pairs) + n] for n, p in enumerate(pairs)}
    for block in range(rotated.shape[0] // planes):
        basis = []
        for b in range(mode_count):
            real, imag = rotated[block * planes + 2 * b], rotated[block * planes + 2 * b + 1]
            for a in range(b):
                r, s = upper_real[a, b], upper_imag[a, b]
                u, v = basis[2 * a], basis[2 * a + 1]
                real = real - (r * u - s * v)
                imag = imag - (r * v + s * u)
            basis += [real * inverse[b], imag * inverse[b]]
        for p in range(planes):
            new_modes[p, block * 8:block * 8 + 8, :] = basis[p]


def shape(*dims):
    return jax.ShapeDtypeStruct(dims, jnp.float32)


def on_device(object_field, amplitudes, positions, frame_count, coefficients, probe_modes):
    frames, length = amplitudes.shape[:2]
    mode_count = probe_modes.shape[0]
    planes = 2 * mode_count
    height, width = object_field.shape[1:]
    scan_count = lax.axis_size("scan")
    col_count = lax.axis_size("col")
    root_total = math.sqrt(frames * scan_count * col_count)
    rows_table, cols_table = make_tables(length)
    tiles, blocks = height // 8, length // 8
    full_width = width + length
    units = planes * blocks
    orders = stream_orders(scan_count, col_count, units)
    partners = 2 * sum((1 << len(group)) - 1 for group in orders[0])

    def vmem(*dims):
        return pltpu.VMEM(dims, jnp.float32)

    stream_sems = pltpu.SemaphoreType.DMA((ITERS, len(orders), partners))
    halo_sems = pltpu.SemaphoreType.DMA((ITERS, 3, CHUNKS))
    side_sems = pltpu.SemaphoreType.DMA((ITERS, 3 * CHUNKS + 4))
    settled, rotated, factors, kept = pl.pallas_call(
        functools.partial(step_kernel, scan_count, col_count, mode_count, root_total),
        name="reconstruct",
        out_shape=(
            shape(2, tiles, 8, width), shape(units, 8, length), shape(mode_count * mode_count, 8, length),
            shape(frames, mode_count),
        ),
        in_specs=[SMEM] * 2 + [VMEM] * 2 + [ANY] * 4,
        out_specs=(VMEM,) * 4,
        scratch_shapes=[
            pltpu.VMEM(amplitudes.shape, amplitudes.dtype),
            vmem(planes, length, length),
            pltpu.VMEM(rows_table.shape, rows_table.dtype),
            pltpu.VMEM(cols_table.shape, cols_table.dtype),
            pltpu.SemaphoreType.DMA((4,)),
            vmem(ITERS, 2, tiles + blocks, 8, full_width),
            vmem(ITERS, 2, tiles + blocks, 8, full_width),
            vmem(2, frames, tiles, 8, width),
            vmem(tiles, 8, width),
            vmem(4, frames, length, length),
            vmem(frames, 2, length, length),
            vmem(ITERS, frames, 2, length, length),
            vmem(ITERS, frames, 2, length, length),
            vmem(ITERS, frames, mode_count + 2),
            vmem(ITERS, 4, frames, mode_count + 2),
            vmem(ITERS, units, 8, length),
            vmem(ITERS, units, 8, length),
            vmem(ITERS - 1, units, 8, length),
            vmem(planes, length, length),
            vmem(frames, mode_count),
            vmem(ITERS, 2, tiles + blocks, 8, width),
            vmem(ITERS, 2, tiles, 8, width),
            vmem(ITERS, 2, tiles, 8, width),
            stream_sems, stream_sems, halo_sems, halo_sems, side_sems, side_sems,
        ],
        compiler_params=pltpu.CompilerParams(
            collective_id=0, has_side_effects=True, vmem_limit_bytes=60 * 2**20
        ),
        cost_estimate=pl.CostEstimate(flops=5 * 10**9, bytes_accessed=10**7, transcendentals=0),
    )(
        frame_count, positions, coefficients, object_field.reshape(2, tiles, 8, width), amplitudes,
        probe_modes.reshape(planes, length, length), rows_table, cols_table,
    )
    parts = 2
    new_object, modes, weights = pl.pallas_call(
        functools.partial(finish_kernel, mode_count),
        name="finish",
        grid=(parts,),
        out_shape=(shape(2, tiles, 8, width), shape(planes, length, length), shape(frames, mode_count)),
        in_specs=[
            pl.BlockSpec((2, tiles // parts, 8, width), lambda n: (0, n, 0, 0)),
            pl.BlockSpec((units // parts, 8, length), lambda n: (n, 0, 0)),
            pl.BlockSpec(factors.shape, lambda n: (0, 0, 0)),
            pl.BlockSpec(kept.shape, lambda n: (0, 0)),
        ],
        out_specs=(
            pl.BlockSpec((2, tiles // parts, 8, width), lambda n: (0, n, 0, 0)),
            pl.BlockSpec((planes, length // parts, length), lambda n: (0, n, 0)),
            pl.BlockSpec(kept.shape, lambda n: (0, 0)),
        ),
    )(settled, rotated, factors, kept)
    return (new_object.reshape(object_field.shape), modes.reshape(probe_modes.shape), weights)


def solution(mesh):
    placed = (
        P(None, "scan", "col"),
        P(("scan", "col"), None, None),
        P(("scan", "col"), None),
        P(("scan", "col")),
        P(("scan", "col"), None),
        P(),
    )
    return jax.shard_map(
        on_device,
        mesh=mesh,
        in_specs=placed,
        out_specs=(P(None, "scan", "col"), P(), P(("scan", "col"), None)),
        check_vma=False,
    )
```

```python
import functools
import math

import jax
import jax.numpy as jnp
import ml_dtypes
import numpy as np
from jax import lax
from jax.experimental import pallas as pl
from jax.experimental.pallas import tpu as pltpu
from jax.sharding import PartitionSpec as P

ITERS = 2
CHUNKS = 8

VMEM = pl.BlockSpec(memory_space=pltpu.VMEM)
SMEM = pl.BlockSpec(memory_space=pltpu.SMEM)
ANY = pl.BlockSpec(memory_space=pl.ANY)


def make_tables(length):
    indices = np.arange(length, dtype=np.int32)
    phases = indices[:, None] * indices[None, :] % length
    angles = phases.astype(np.float32) * np.float32(2.0 * math.pi / length)
    factor = np.float32(1.0 / math.sqrt(length))
    cosine = np.cos(angles) * factor
    sine = np.sin(angles) * factor
    rows_table = np.block([[cosine, sine], [-sine, cosine]])
    cols_table = np.block([[cosine, -sine], [sine, cosine]])
    return (rows_table.astype(ml_dtypes.bfloat16), cols_table.astype(ml_dtypes.bfloat16))


def apply_transform(stacked, first_table, second_table):
    length = stacked.shape[1]
    halfway = jnp.dot(first_table, stacked, preferred_element_type=jnp.float32).astype(jnp.bfloat16)
    beside = jnp.concatenate([halfway[:length], halfway[length:]], 1)
    return jnp.dot(beside, second_table, preferred_element_type=jnp.float32)


def bits_of(axis, count):
    return [(axis, 1 << b) for b in range(count.bit_length() - 1)]


def stream_orders(scan_count, col_count, units):
    scan, col = bits_of("scan", scan_count), bits_of("col", col_count)
    core, y, x, z, w = col[:1], col[1:], scan[:1], scan[1:3], scan[3:]
    orders = [[core, y, z, x, w], [core, z, y, x, w], [core, x, y, z, w], [core, y, x, z, w]]
    shares = units // (scan_count * col_count)
    if shares < len(orders):
        orders = orders[2:]
    elif shares >= 2 * len(orders):
        orders = 2 * orders
    return [[group for group in order if group] for order in orders]


def reach(device, source, target, send_sem, recv_sem):
    return pltpu.make_async_remote_copy(
        src_ref=source,
        dst_ref=target,
        send_sem=send_sem,
        recv_sem=recv_sem,
        device_id=device,
        device_id_type=pl.DeviceIdType.MESH,
    )


class Shift:
    def __init__(self, copy, sends, receives):
        self.copy, self.sends, self.receives = copy, sends, receives

    def start(self):
        pl.when(self.sends)(self.copy.start)

    def arrive(self):
        pl.when(self.receives)(self.copy.wait_recv)

    def leave(self):
        pl.when(self.sends)(self.copy.wait_send)


class Place:
    def __init__(self, scan_count, col_count):
        self.scan, self.col = lax.axis_index("scan"), lax.axis_index("col")
        self.right = (self.scan, lax.rem(self.col + 1, col_count))
        self.left = (self.scan, lax.rem(self.col + col_count - 1, col_count))
        self.down = (lax.rem(self.scan + 1, scan_count), self.col)
        self.up = (lax.rem(self.scan + scan_count - 1, scan_count), self.col)
        self.has_right, self.has_left = self.col < col_count - 1, self.col > 0
        self.has_down, self.has_up = self.scan < scan_count - 1, self.scan > 0
        self.beyond = (self.down[0], self.right[1])
        self.before = (self.up[0], self.left[1])
        self.has_beyond = jnp.logical_and(self.has_down, self.has_right)
        self.has_before = jnp.logical_and(self.has_up, self.has_left)

    def sides(self):
        return (
            (self.right, self.has_right), (self.left, self.has_left),
            (self.down, self.has_down), (self.up, self.has_up),
            (self.beyond, self.has_beyond), (self.before, self.has_before),
        )

    def bit(self, axis, bit):
        at = self.scan if axis == "scan" else self.col
        return at // bit % 2

    def index(self, group, flips):
        total = 0
        for b, (axis, bit) in enumerate(group):
            mine = self.bit(axis, bit)
            total = total + (1 - mine if flips >> b & 1 else mine) * (1 << b)
        return total

    def partner(self, group, flips):
        scan, col = self.scan, self.col
        for b, (axis, bit) in enumerate(group):
            if flips >> b & 1:
                step = bit - 2 * bit * self.bit(axis, bit)
                if axis == "scan":
                    scan = scan + step
                else:
                    col = col + step
        return (scan, col)

    def greet(self, groups):
        barrier = pltpu.get_barrier_semaphore()
        partners = [self.partner(group, flips) for group in groups for flips in range(1, 1 << len(group))]

        def signal(device):
            pl.semaphore_signal(barrier, inc=1, device_id=device, device_id_type=pl.DeviceIdType.MESH)

        for device in partners:
            signal(device)
        for device, there in self.sides():
            pl.when(there)(functools.partial(signal, device))
        present = [there.astype(jnp.int32) for _, there in self.sides()]
        pl.semaphore_wait(barrier, len(partners) + sum(present))


class Stream:
    def __init__(self, place, order, base, count, terms, landed, send_sems, recv_sems):
        self.place, self.order = place, order
        self.terms, self.landed = terms, landed
        self.send_sems, self.recv_sems = send_sems, recv_sems
        self.bases, self.counts, self.slots, self.marks = [base], [count], [], []
        self.copies = {}
        slot, mark = base, 0
        for group in order:
            members = 1 << len(group)
            part = self.counts[-1] // members
            self.bases.append(self.bases[-1] + place.index(group, 0) * part)
            self.counts.append(part)
            self.slots.append(slot)
            self.marks.append(mark)
            slot += part * (members - 1)
            mark += members - 1
        self.total = mark

    def flips(self, s):
        return range(1, 1 << len(self.order[s]))

    def scatter(self, s):
        part = self.counts[s + 1]
        for flips in self.flips(s):
            group = self.order[s]
            source = self.terms.at[pl.ds(self.bases[s] + self.place.index(group, flips) * part, part)]
            target = self.landed.at[pl.ds(self.slots[s] + (flips - 1) * part, part)]
            at = self.marks[s] + flips - 1
            copy = reach(
                self.place.partner(group, flips), source, target, self.send_sems.at[at], self.recv_sems.at[at]
            )
            copy.start()
            self.copies["scatter", s, flips] = copy

    def offer(self, grads, mates, first, half):
        group = self.order[0]
        start = (first + self.place.index(group, 1) * half) * 8
        rows = pl.ds(pl.multiple_of(start, 8), half * 8)
        copy = reach(
            self.place.partner(group, 1), grads.at[:, :, rows, :], mates.at[:, :, rows, :],
            self.send_sems.at[0], self.recv_sems.at[0],
        )
        copy.start()
        self.copies["scatter", 0, 1] = copy

    def gathered(self, s):
        part = self.counts[s + 1]
        at = pl.ds(self.bases[s + 1], part)
        value = self.terms[at]
        for flips in self.flips(s):
            self.copies["scatter", s, flips].wait_recv()
            value = value + self.landed[pl.ds(self.slots[s] + (flips - 1) * part, part)]
        return at, value

    def spread(self, s, raised):
        piece = raised.at[pl.ds(self.bases[s + 1], self.counts[s + 1])]
        for flips in self.flips(s):
            at = self.total + self.marks[s] + flips - 1
            copy = reach(
                self.place.partner(self.order[s], flips), piece, piece,
                self.send_sems.at[at], self.recv_sems.at[at],
            )
            copy.start()
            self.copies["gather", s, flips] = copy

    def arrived(self, s):
        for flips in self.flips(s):
            self.copies["gather", s, flips].wait_recv()

    def leave(self):
        for copy in self.copies.values():
            copy.wait_send()


class Halo:
    def __init__(self, place, wide, tiles, width, send_sems, recv_sems):
        rows = tiles // CHUNKS
        near, far = pl.ds(0, width), pl.ds(width, width)
        self.up, self.side, self.corner = [], [], []
        for q in range(CHUNKS):
            top, low = pl.ds(q * rows, rows), pl.ds(tiles + q * rows, rows)
            self.up.append(Shift(
                reach(place.up, wide.at[:, top, :, near], wide.at[:, low, :, near], send_sems.at[0, q], recv_sems.at[0, q]),
                place.has_up, place.has_down,
            ))
            self.side.append(Shift(
                reach(place.left, wide.at[:, top, :, near], wide.at[:, top, :, far], send_sems.at[1, q], recv_sems.at[1, q]),
                place.has_left, place.has_right,
            ))
            self.corner.append(Shift(
                reach(place.left, wide.at[:, low, :, near], wide.at[:, low, :, far], send_sems.at[2, q], recv_sems.at[2, q]),
                place.has_left, place.has_right,
            ))

    def begin(self, q):
        self.up[q].start()
        self.side[q].start()

    def turn(self, q):
        self.up[q].arrive()
        self.corner[q].start()

    def end(self):
        for shift in self.side + self.corner:
            shift.arrive()

    def leave(self):
        for shift in self.up + self.side + self.corner:
            shift.leave()


def step_kernel(
    scan_count, col_count, mode_count, root_total,
    count, positions, first_weights, field, far_amplitudes, far_modes, far_rows, far_cols,
    new_object, last_raised, factors, new_weights,
    amplitudes, first_modes, rows_table, cols_table, input_sems,
    wide, totals, held, den, powers, probes, grads, mates, given, taken, terms, landed, raised, middle_modes, middle_weights,
    sideways, fallen, bottom,
    stream_send, stream_recv, halo_send, halo_recv, side_send, side_recv,
):
    tiles, _, width = field.shape[1:]
    height = 8 * tiles
    frames, length = amplitudes.shape[:2]
    planes = 2 * mode_count
    blocks = length // 8
    units = blocks * planes
    pixels = float(length * length)
    full_width = width + length
    rows_of_chunk = tiles // CHUNKS
    place = Place(scan_count, col_count)
    near, far = pl.ds(0, width), pl.ds(width, width)
    top, low = pl.ds(0, tiles), pl.ds(tiles, tiles)
    pairs = [(i, j) for j in range(mode_count) for i in range(j + 1)]
    strict = [(i, j) for i, j in pairs if i < j]
    leaving = []
    ups = [raised.at[i] for i in range(ITERS - 1)] + [last_raised]

    def chunk(q, offset=0):
        return pl.ds(offset + q * rows_of_chunk, rows_of_chunk)

    def block_rows(block):
        return pl.ds(pl.multiple_of(block * 8, 8), 8)

    loads = [
        pltpu.make_async_copy(source, target, input_sems.at[n])
        for n, (source, target) in enumerate((
            (far_modes, first_modes), (far_rows, rows_table), (far_cols, cols_table), (far_amplitudes, amplitudes),
        ))
    ]
    for load in loads:
        load.start()

    wide[0, :, :tiles, :, :width] = field[...]

    @pl.when(jnp.logical_not(place.has_left))
    def _():
        sideways[...] = jnp.zeros_like(sideways)

    @pl.when(jnp.logical_not(place.has_up))
    def _():
        fallen[...] = jnp.zeros_like(fallen)

    for slot, there in ((1, place.has_left), (2, place.has_up), (3, place.has_before)):

        @pl.when(jnp.logical_not(there))
        def _():
            for i in range(ITERS):
                taken[i, slot] = jnp.zeros(taken.shape[2:], jnp.float32)

    orders = stream_orders(scan_count, col_count, units)
    place.greet(orders[0])
    halos = [
        Halo(place, wide.at[i], tiles, width, halo_send.at[i], halo_recv.at[i]) for i in range(ITERS)
    ]
    for q in range(CHUNKS):
        halos[0].begin(q)
    def live(slot):
        return slot < count[0]

    def inside(value, limit):
        return jnp.minimum(jnp.maximum(value, 0), limit - 1)

    corners = [
        (
            inside(positions[g, 0] - place.scan * height, height),
            inside(positions[g, 1] - place.col * width, width),
        )
        for g in range(frames)
    ]

    def turned(piece, row, col):
        return pltpu.roll(pltpu.roll(piece, row, 0), col, 1)

    def hold(plane, slot, piece):
        row, col = corners[slot]
        held[plane, slot] = turned(piece, row, col).reshape(tiles, 8, width)

    lanes = lax.broadcasted_iota(jnp.int32, (8, width), 1)
    sublanes = lax.broadcasted_iota(jnp.int32, (8, width), 0)

    def settle(i):
        def move(n, carry):
            for plane in range(2):
                quarters = [0.0] * 4
                for g in range(frames):
                    row, col = corners[g]
                    value = held[plane, g, n]
                    below, beyond = sublanes + 8 * n < row, lanes < col
                    upper, lower = jnp.where(below, 0.0, value), jnp.where(below, value, 0.0)
                    for at, half in ((0, upper), (2, lower)):
                        quarters[at] += jnp.where(beyond, 0.0, half)
                        quarters[at + 1] += jnp.where(beyond, half, 0.0)
                totals[i, plane, n, :, :width] = quarters[0]
                totals[i, plane, n, :, width:] = quarters[1]
                totals[i, plane, tiles + n, :, :width] = quarters[2]
                totals[i, plane, tiles + n, :, width:] = quarters[3]
            return carry

        lax.fori_loop(0, tiles, move, 0, unroll=4)

    def cut(i, plane, slot):
        row, col = corners[slot]
        picked = []
        for n in range(tiles):
            below, beyond = sublanes + 8 * n < row, lanes < col
            upper, lower = wide[i, plane, n], wide[i, plane, tiles + n]
            left = jnp.where(below, lower[:, :width], upper[:, :width])
            right = jnp.where(below, lower[:, width:], upper[:, width:])
            picked.append(jnp.where(beyond, right, left))
        return turned(
            jnp.concatenate(picked, 0), lax.rem(height - row, height), lax.rem(width - col, width)
        )

    def masked(weights):
        table = [[weights[g:g + 1, k:k + 1] for k in range(mode_count)] for g in range(frames)]
        return [[jnp.where(live(g), w, 0.0) for w in row] for g, row in enumerate(table)]

    def wave(weights, tiles):
        out = []
        for g in range(frames):
            for part in range(2):
                value = weights[g][0] * tiles[part]
                for k in range(1, mode_count):
                    value = value + weights[g][k] * tiles[2 * k + part]
                out.append(value)
        return out

    def fold(value):
        total = value[:, :128]
        for at in range(128, length, 128):
            total = total + value[:, at:at + 128]
        return total

    def whole(value):
        return jnp.sum(jnp.sum(value, 0, keepdims=True), 1, keepdims=True)

    def run_frame(i, g):
        object_real = cut(i, 0, g)
        object_imag = cut(i, 1, g)
        probe_real, probe_imag = probes[g, 0], probes[g, 1]
        exit_real = probe_real * object_real - probe_imag * object_imag
        exit_imag = probe_real * object_imag + probe_imag * object_real
        stacked = jnp.concatenate([exit_real, exit_imag], 0).astype(jnp.bfloat16)
        far_field = apply_transform(stacked, rows_table[...], cols_table[...])
        far_real, far_imag = far_field[:, :length], far_field[:, length:]
        inverse_size = lax.rsqrt(far_real * far_real + far_imag * far_imag)
        factor = amplitudes[g].astype(jnp.float32) * jnp.minimum(inverse_size, 2.0)
        scaled = jnp.concatenate([far_real * factor, far_imag * factor], 0).astype(jnp.bfloat16)
        back = apply_transform(scaled, cols_table[...], rows_table[...])
        diff_real = back[:, :length] - exit_real
        diff_imag = back[:, length:] - exit_imag
        grads[i, g, 0] = object_real * diff_real + object_imag * diff_imag
        grads[i, g, 1] = object_real * diff_imag - object_imag * diff_real
        hold(0, g, probe_real * diff_real + probe_imag * diff_imag)
        hold(1, g, probe_real * diff_imag - probe_imag * diff_real)

    weights = masked(first_weights)
    mate = place.partner(orders[0][0], 1)

    def tell(i):
        for g in range(frames):
            for k in range(mode_count):
                given[i, g:g + 1, k:k + 1] = weights[g][k]
            for at, value in enumerate(corners[g]):
                given[i, g:g + 1, mode_count + at:mode_count + at + 1] = jnp.full((1, 1), value, jnp.int32).astype(jnp.float32)
        for telling in tellings[i]:
            telling.start()

    def telling_to(i, slot, device, sends, receives):
        at = 3 * CHUNKS + slot
        return Shift(
            reach(device, given.at[i], taken.at[i, slot], side_send.at[i, at], side_recv.at[i, at]), sends, receives
        )

    always = place.col >= 0
    tellings = [
        [
            telling_to(i, 0, mate, always, always),
            telling_to(i, 1, place.right, place.has_right, place.has_left),
            telling_to(i, 2, place.down, place.has_down, place.has_up),
            telling_to(i, 3, place.beyond, place.has_beyond, place.has_before),
        ]
        for i in range(ITERS)
    ]
    tell(0)

    def first_wave(block, carry):
        rows = block_rows(block)
        values = wave(weights, [first_modes[p, rows, :] for p in range(planes)])
        for at, value in enumerate(values):
            probes[at // 2, at % 2, rows, :] = value
        return carry

    loads[0].wait()
    lax.fori_loop(0, blocks, first_wave, 0, unroll=4)
    for load in loads[1:]:
        load.wait()

    for i in range(ITERS):
        again = i < ITERS - 1
        modes = first_modes if i == 0 else middle_modes
        kept_weights = first_weights if i == 0 else middle_weights

        def rightward(at, source, target):
            copy = reach(place.right, source, target, side_send.at[i, at], side_recv.at[i, at])
            return Shift(copy, place.has_right, place.has_left)

        def downward(at, source, target):
            copy = reach(place.down, source, target, side_send.at[i, at], side_recv.at[i, at])
            return Shift(copy, place.has_down, place.has_up)

        pair = pl.ds(0, 2)
        low_rights = [
            rightward(q, totals.at[i, pair, chunk(q, tiles), :, far], sideways.at[i, pair, chunk(q, tiles)])
            for q in range(CHUNKS)
        ]
        top_rights = [
            rightward(CHUNKS + q, totals.at[i, pair, chunk(q), :, far], sideways.at[i, pair, chunk(q)])
            for q in range(CHUNKS)
        ]
        downs = [
            downward(2 * CHUNKS + q, bottom.at[i, pair, chunk(q)], fallen.at[i, pair, chunk(q)])
            for q in range(CHUNKS)
        ]
        leaving += low_rights + top_rights + downs

        if i == 0:
            for q in range(CHUNKS):
                halos[0].turn(q)
        halos[i].end()
        for g in range(frames):
            run_frame(i, g)
        settle(i)
        for q in range(CHUNKS):
            low_rights[q].start()

        stages = len(orders[0])
        share = units // len(orders)
        streams = [
            Stream(
                place, order, t * share, share, terms.at[i], landed.at[i],
                stream_send.at[i, t], stream_recv.at[i, t],
            )
            for t, order in enumerate(orders)
        ]
        leaving += streams

        def term_step(block, carry):
            rows = block_rows(block)
            tiles_ = [ref[i, g, part, rows, :] for ref in (grads, mates) for g in range(frames) for part in range(2)]
            for k in range(mode_count):
                for part in range(2):
                    value = joint[0][k] * tiles_[part]
                    for g in range(1, 2 * frames):
                        value = value + joint[g][k] * tiles_[2 * g + part]
                    terms[i, block * planes + 2 * k + part] = value
            return carry

        half = share // planes // 2
        for t, stream in enumerate(streams):
            stream.offer(grads.at[i], mates.at[i], t * 2 * half, half)
        for q in range(CHUNKS):
            top_rights[q].start()

        for telling in tellings[i]:
            telling.arrive()
        joint = weights + [[taken[i, 0, g:g + 1, k:k + 1] for k in range(mode_count)] for g in range(frames)]
        joint = [[jnp.broadcast_to(w, (8, length)) for w in row] for row in joint]

        def finish_scatter(t, s):
            stream = streams[t]
            if s == 0:
                stream.copies["scatter", 0, 1].wait_recv()
                first = stream.bases[1] // planes
                lax.fori_loop(0, half, lambda n, carry: term_step(first + n, carry), 0, unroll=min(half, 4))
                stream.scatter(1)
                return
            at, value = stream.gathered(s)
            if s < stages - 1:
                terms[i, at] = value
                stream.scatter(s + 1)
                return
            first, target = stream.bases[s + 1], ups[i]
            for n in range(stream.counts[s + 1]):
                unit = first + n
                kept = modes[unit % planes, block_rows(unit // planes), :]
                target[unit] = kept + value[n] / root_total
            stream.spread(s, ups[i])

        sums = [jnp.zeros((8, 128), jnp.float32)] * (len(pairs) + len(strict) + 2 * mode_count * frames)

        def fit_step(block, sums):
            rows = block_rows(block)
            tiles = [ups[i][block * planes + p] for p in range(planes)]
            real, imag = tiles[0::2], tiles[1::2]
            terms_ = [fold(real[a] * real[b] + imag[a] * imag[b]) for a, b in pairs]
            terms_ += [fold(real[a] * imag[b] - imag[a] * real[b]) for a, b in strict]
            for g in range(frames):
                held_real = probes[g, 0, rows, :] + 0.5 * grads[i, g, 0, rows, :]
                held_imag = probes[g, 1, rows, :] + 0.5 * grads[i, g, 1, rows, :]
                for a in range(mode_count):
                    terms_.append(fold(real[a] * held_real + imag[a] * held_imag))
                    terms_.append(fold(real[a] * held_imag - imag[a] * held_real))
            return tuple(a + b for a, b in zip(sums, terms_))

        def finish_gather(t, s):
            nonlocal sums
            streams[t].arrived(s)
            if s > 0:
                streams[t].spread(s - 1, ups[i])
            else:
                per = share // planes
                sums = lax.fori_loop(t * per, (t + 1) * per, fit_step, tuple(sums), unroll=4)

        def drop(q):
            low_rights[q].arrive()
            bottom[i, :2, chunk(q)] = totals[i, :2, chunk(q, tiles), :, near] + sideways[i, :2, chunk(q, tiles)]
            downs[q].start()

        def renew(q):
            top_rights[q].arrive()
            downs[q].arrive()
            update = [
                totals[i, p, chunk(q), :, near] + sideways[i, p, chunk(q)] + fallen[i, p, chunk(q)]
                for p in range(2)
            ]
            scale = 1.0 / (den[chunk(q)] + 1.0)
            for p in range(2):
                value = wide[i, p, chunk(q), :, near] + update[p] * scale
                if again:
                    wide[i + 1, p, chunk(q), :, near] = value
                else:
                    new_object[p, chunk(q)] = value
            if again:
                halos[i + 1].begin(q)

        def weigh():
            near_weights = [
                [
                    [jnp.broadcast_to(taken[i, slot, g:g + 1, k:k + 1], (8, length)) for k in range(mode_count)]
                    for g in range(frames)
                ]
                for slot in range(1, 4)
            ]

            def power_step(block, carry):
                rows = block_rows(block)
                tiles_ = [modes[p, rows, :] for p in range(planes)]
                values = [probes[g, part, rows, :] for g in range(frames) for part in range(2)]
                for weights_ in near_weights:
                    values += wave(weights_, tiles_)
                for n in range(4 * frames):
                    real, imag = values[2 * n], values[2 * n + 1]
                    powers[n // frames, n % frames, rows, :] = real * real + imag * imag
                return carry

            lax.fori_loop(0, blocks, power_step, 0, unroll=4)
            spots = [list(corners)]
            for slot in range(1, 4):
                spots.append([
                    tuple(
                        inside(jnp.sum(taken[i, slot, g:g + 1, at:at + 1]).astype(jnp.int32), limit)
                        for at, limit in ((mode_count, height), (mode_count + 1, width))
                    )
                    for g in range(frames)
                ])
            for slot in range(4):
                for g in range(frames):
                    powers[slot, g] = turned(powers[slot, g], *spots[slot][g])

            def den_step(n, carry):
                rows = block_rows(n)
                total = 0.0
                for slot in range(4):
                    for g in range(frames):
                        row, col = spots[slot][g]
                        below, beyond = sublanes + 8 * n < row, lanes < col
                        if slot < 2:
                            below = jnp.logical_not(below)
                        if slot % 2 == 0:
                            beyond = jnp.logical_not(beyond)
                        total = total + jnp.where(jnp.logical_and(below, beyond), powers[slot, g, rows, :], 0.0)
                den[n] = total
                return carry

            lax.fori_loop(0, tiles, den_step, 0, unroll=4)

        def turn(q):
            if again:
                halos[i + 1].turn(q)

        steps = [functools.partial(finish_scatter, t, s) for s in range(stages) for t in range(len(streams))]
        steps += [
            functools.partial(finish_gather, t, s)
            for s in range(stages - 1, -1, -1) for t in range(len(streams))
        ]
        drops, turns = (4, 4, 5, 5, 6, 6, 7, 7), (13, 14, 15, 16, 17, 18, 19, 20)
        renews = (9, 10, 11, 12, 13, 14, 15, 16) if again else (13, 14, 15, 16, 18, 20, 21, 22)
        marks = [(drop, drops), (renew, renews), (turn, turns)]
        for n, step in enumerate(steps):
            if n == len(steps) * 6 // 32:
                weigh()
            for task, whens in marks:
                for q, when in enumerate(whens):
                    if when * len(steps) // 32 == n:
                        task(q)
            step()

        column = jnp.sum(jnp.concatenate([jnp.sum(s, 0, keepdims=True) for s in sums], 0), 1, keepdims=True) / pixels
        totals_of = [column[n:n + 1] for n in range(len(sums))]
        gram_real = dict(zip(pairs, totals_of))
        gram_imag = dict(zip(strict, totals_of[len(pairs):]))
        upper_real, upper_imag = {}, {}
        for b in range(mode_count):
            for a in range(b):
                sum_real, sum_imag = gram_real[a, b], gram_imag[a, b]
                for k in range(a):
                    r, s, u, v = upper_real[k, a], upper_imag[k, a], upper_real[k, b], upper_imag[k, b]
                    sum_real = sum_real - (r * u + s * v)
                    sum_imag = sum_imag - (r * v - s * u)
                upper_real[a, b] = sum_real / upper_real[a, a]
                upper_imag[a, b] = sum_imag / upper_real[a, a]
            diagonal = gram_real[b, b]
            for k in range(b):
                diagonal = diagonal - (upper_real[k, b] * upper_real[k, b] + upper_imag[k, b] * upper_imag[k, b])
            upper_real[b, b] = jnp.sqrt(diagonal)
        inverse = {b: 1.0 / upper_real[b, b] for b in range(mode_count)}

        refit_weights = []
        at = len(pairs) + len(strict)
        for g in range(frames):
            inner = []
            for k in range(mode_count):
                real, imag = totals_of[at], totals_of[at + 1]
                at += 2
                for a in range(k):
                    r, s, u, v = upper_real[a, k], upper_imag[a, k], inner[a][0], inner[a][1]
                    real = real - (r * u + s * v)
                    imag = imag - (r * v - s * u)
                inner.append((real * inverse[k], imag * inverse[k]))
            refit_weights.append([
                jnp.where(live(g), inner[k][0], kept_weights[g:g + 1, k:k + 1]) for k in range(mode_count)
            ])
        target_weights = middle_weights if again else new_weights
        for g in range(frames):
            for k in range(mode_count):
                target_weights[g:g + 1, k:k + 1] = refit_weights[g][k]
        weights = [[jnp.where(live(g), w, 0.0) for w in row] for g, row in enumerate(refit_weights)]
        if again:
            tell(i + 1)

        def spread_out(value):
            return jnp.broadcast_to(value, (8, length))

        upper_real = {p: spread_out(v) for p, v in upper_real.items() if p[0] < p[1]}
        upper_imag = {p: spread_out(v) for p, v in upper_imag.items()}
        inverse = {p: spread_out(v) for p, v in inverse.items()}
        wave_weights = [[spread_out(w) for w in row] for row in weights]

        def basis_step(block, carry):
            rows = block_rows(block)
            basis = []
            for b in range(mode_count):
                real, imag = ups[i][block * planes + 2 * b], ups[i][block * planes + 2 * b + 1]
                for a in range(b):
                    r, s = upper_real[a, b], upper_imag[a, b]
                    u, v = basis[2 * a], basis[2 * a + 1]
                    real = real - (r * u - s * v)
                    imag = imag - (r * v + s * u)
                basis += [real * inverse[b], imag * inverse[b]]
            for p in range(planes):
                middle_modes[p, rows, :] = basis[p]
            for n, value in enumerate(wave(wave_weights, basis)):
                probes[n // 2, n % 2, rows, :] = value
            return carry

        if again:
            lax.fori_loop(0, blocks, basis_step, 0, unroll=4)
        else:
            rows_ = [inverse[b] for b in range(mode_count)]
            rows_ += [upper_real[p] for p in strict] + [upper_imag[p] for p in strict]
            for n, row in enumerate(rows_):
                factors[n] = row

    for item in leaving + halos:
        item.leave()
    for telling in sum(tellings, []):
        telling.leave()


def finish_kernel(mode_count, settled, rotated, factors, kept_weights, new_object, new_modes, new_weights):
    planes = 2 * mode_count
    pairs = [(i, j) for j in range(mode_count) for i in range(j)]
    new_object[...] = settled[...]
    new_weights[...] = kept_weights[...]
    inverse = [factors[b] for b in range(mode_count)]
    upper_real = {p: factors[mode_count + n] for n, p in enumerate(pairs)}
    upper_imag = {p: factors[mode_count + len(pairs) + n] for n, p in enumerate(pairs)}
    for block in range(rotated.shape[0] // planes):
        basis = []
        for b in range(mode_count):
            real, imag = rotated[block * planes + 2 * b], rotated[block * planes + 2 * b + 1]
            for a in range(b):
                r, s = upper_real[a, b], upper_imag[a, b]
                u, v = basis[2 * a], basis[2 * a + 1]
                real = real - (r * u - s * v)
                imag = imag - (r * v + s * u)
            basis += [real * inverse[b], imag * inverse[b]]
        for p in range(planes):
            new_modes[p, block * 8:block * 8 + 8, :] = basis[p]


def shape(*dims):
    return jax.ShapeDtypeStruct(dims, jnp.float32)


def on_device(object_field, amplitudes, positions, frame_count, coefficients, probe_modes):
    frames, length = amplitudes.shape[:2]
    mode_count = probe_modes.shape[0]
    planes = 2 * mode_count
    height, width = object_field.shape[1:]
    scan_count = lax.axis_size("scan")
    col_count = lax.axis_size("col")
    root_total = math.sqrt(frames * scan_count * col_count)
    rows_table, cols_table = make_tables(length)
    tiles, blocks = height // 8, length // 8
    full_width = width + length
    units = planes * blocks
    orders = stream_orders(scan_count, col_count, units)
    partners = 2 * sum((1 << len(group)) - 1 for group in orders[0])

    def vmem(*dims):
        return pltpu.VMEM(dims, jnp.float32)

    stream_sems = pltpu.SemaphoreType.DMA((ITERS, len(orders), partners))
    halo_sems = pltpu.SemaphoreType.DMA((ITERS, 3, CHUNKS))
    side_sems = pltpu.SemaphoreType.DMA((ITERS, 3 * CHUNKS + 4))
    settled, rotated, factors, kept = pl.pallas_call(
        functools.partial(step_kernel, scan_count, col_count, mode_count, root_total),
        name="reconstruct",
        out_shape=(
            shape(2, tiles, 8, width), shape(units, 8, length), shape(mode_count * mode_count, 8, length),
            shape(frames, mode_count),
        ),
        in_specs=[SMEM] * 2 + [VMEM] * 2 + [ANY] * 4,
        out_specs=(VMEM,) * 4,
        scratch_shapes=[
            pltpu.VMEM(amplitudes.shape, amplitudes.dtype),
            vmem(planes, length, length),
            pltpu.VMEM(rows_table.shape, rows_table.dtype),
            pltpu.VMEM(cols_table.shape, cols_table.dtype),
            pltpu.SemaphoreType.DMA((4,)),
            vmem(ITERS, 2, tiles + blocks, 8, full_width),
            vmem(ITERS, 2, tiles + blocks, 8, full_width),
            vmem(2, frames, tiles, 8, width),
            vmem(tiles, 8, width),
            vmem(4, frames, length, length),
            vmem(frames, 2, length, length),
            vmem(ITERS, frames, 2, length, length),
            vmem(ITERS, frames, 2, length, length),
            vmem(ITERS, frames, mode_count + 2),
            vmem(ITERS, 4, frames, mode_count + 2),
            vmem(ITERS, units, 8, length),
            vmem(ITERS, units, 8, length),
            vmem(ITERS - 1, units, 8, length),
            vmem(planes, length, length),
            vmem(frames, mode_count),
            vmem(ITERS, 2, tiles + blocks, 8, width),
            vmem(ITERS, 2, tiles, 8, width),
            vmem(ITERS, 2, tiles, 8, width),
            stream_sems, stream_sems, halo_sems, halo_sems, side_sems, side_sems,
        ],
        compiler_params=pltpu.CompilerParams(
            collective_id=0, has_side_effects=True, vmem_limit_bytes=60 * 2**20
        ),
        cost_estimate=pl.CostEstimate(flops=5 * 10**9, bytes_accessed=10**7, transcendentals=0),
    )(
        frame_count, positions, coefficients, object_field.reshape(2, tiles, 8, width), amplitudes,
        probe_modes.reshape(planes, length, length), rows_table, cols_table,
    )
    parts = 2
    new_object, modes, weights = pl.pallas_call(
        functools.partial(finish_kernel, mode_count),
        name="finish",
        grid=(parts,),
        out_shape=(shape(2, tiles, 8, width), shape(planes, length, length), shape(frames, mode_count)),
        in_specs=[
            pl.BlockSpec((2, tiles // parts, 8, width), lambda n: (0, n, 0, 0)),
            pl.BlockSpec((units // parts, 8, length), lambda n: (n, 0, 0)),
            pl.BlockSpec(factors.shape, lambda n: (0, 0, 0)),
            pl.BlockSpec(kept.shape, lambda n: (0, 0)),
        ],
        out_specs=(
            pl.BlockSpec((2, tiles // parts, 8, width), lambda n: (0, n, 0, 0)),
            pl.BlockSpec((planes, length // parts, length), lambda n: (0, n, 0)),
            pl.BlockSpec(kept.shape, lambda n: (0, 0)),
        ),
    )(settled, rotated, factors, kept)
    return (new_object.reshape(object_field.shape), modes.reshape(probe_modes.shape), weights)


def solution(mesh):
    placed = (
        P(None, "scan", "col"),
        P(("scan", "col"), None, None),
        P(("scan", "col"), None),
        P(("scan", "col")),
        P(("scan", "col"), None),
        P(),
    )
    return jax.shard_map(
        on_device,
        mesh=mesh,
        in_specs=placed,
        out_specs=(P(None, "scan", "col"), P(), P(("scan", "col"), None)),
        check_vma=False,
    )
```

```python
import functools
import math

import jax
import jax.numpy as jnp
import ml_dtypes
import numpy as np
from jax import lax
from jax.experimental import pallas as pl
from jax.experimental.pallas import tpu as pltpu
from jax.sharding import PartitionSpec as P

ITERS = 2
CHUNKS = 8

VMEM = pl.BlockSpec(memory_space=pltpu.VMEM)
SMEM = pl.BlockSpec(memory_space=pltpu.SMEM)
ANY = pl.BlockSpec(memory_space=pl.ANY)


def make_tables(length):
    indices = np.arange(length, dtype=np.int32)
    phases = indices[:, None] * indices[None, :] % length
    angles = phases.astype(np.float32) * np.float32(2.0 * math.pi / length)
    factor = np.float32(1.0 / math.sqrt(length))
    cosine = np.cos(angles) * factor
    sine = np.sin(angles) * factor
    rows_table = np.block([[cosine, sine], [-sine, cosine]])
    cols_table = np.block([[cosine, -sine], [sine, cosine]])
    return (rows_table.astype(ml_dtypes.bfloat16), cols_table.astype(ml_dtypes.bfloat16))


def apply_transform(stacked, first_table, second_table):
    length = stacked.shape[1]
    halfway = jnp.dot(first_table, stacked, preferred_element_type=jnp.float32).astype(jnp.bfloat16)
    beside = jnp.concatenate([halfway[:length], halfway[length:]], 1)
    return jnp.dot(beside, second_table, preferred_element_type=jnp.float32)


def bits_of(axis, count):
    return [(axis, 1 << b) for b in range(count.bit_length() - 1)]


def stream_orders(scan_count, col_count, units):
    scan, col = bits_of("scan", scan_count), bits_of("col", col_count)
    core, y, x, z, w = col[:1], col[1:], scan[:1], scan[1:3], scan[3:]
    orders = [[core, y, z, x, w], [core, z, y, x, w], [core, x, y, z, w], [core, y, x, z, w]]
    shares = units // (scan_count * col_count)
    if shares < len(orders):
        orders = orders[2:]
    elif shares >= 2 * len(orders):
        orders = 2 * orders
    return [[group for group in order if group] for order in orders]


def reach(device, source, target, send_sem, recv_sem):
    return pltpu.make_async_remote_copy(
        src_ref=source,
        dst_ref=target,
        send_sem=send_sem,
        recv_sem=recv_sem,
        device_id=device,
        device_id_type=pl.DeviceIdType.MESH,
    )


class Shift:
    def __init__(self, copy, sends, receives):
        self.copy, self.sends, self.receives = copy, sends, receives

    def start(self):
        pl.when(self.sends)(self.copy.start)

    def arrive(self):
        pl.when(self.receives)(self.copy.wait_recv)

    def leave(self):
        pl.when(self.sends)(self.copy.wait_send)


class Place:
    def __init__(self, scan_count, col_count):
        self.scan, self.col = lax.axis_index("scan"), lax.axis_index("col")
        self.right = (self.scan, lax.rem(self.col + 1, col_count))
        self.left = (self.scan, lax.rem(self.col + col_count - 1, col_count))
        self.down = (lax.rem(self.scan + 1, scan_count), self.col)
        self.up = (lax.rem(self.scan + scan_count - 1, scan_count), self.col)
        self.has_right, self.has_left = self.col < col_count - 1, self.col > 0
        self.has_down, self.has_up = self.scan < scan_count - 1, self.scan > 0
        self.beyond = (self.down[0], self.right[1])
        self.before = (self.up[0], self.left[1])
        self.has_beyond = jnp.logical_and(self.has_down, self.has_right)
        self.has_before = jnp.logical_and(self.has_up, self.has_left)

    def sides(self):
        return (
            (self.right, self.has_right), (self.left, self.has_left),
            (self.down, self.has_down), (self.up, self.has_up),
            (self.beyond, self.has_beyond), (self.before, self.has_before),
        )

    def bit(self, axis, bit):
        at = self.scan if axis == "scan" else self.col
        return at // bit % 2

    def index(self, group, flips):
        total = 0
        for b, (axis, bit) in enumerate(group):
            mine = self.bit(axis, bit)
            total = total + (1 - mine if flips >> b & 1 else mine) * (1 << b)
        return total

    def partner(self, group, flips):
        scan, col = self.scan, self.col
        for b, (axis, bit) in enumerate(group):
            if flips >> b & 1:
                step = bit - 2 * bit * self.bit(axis, bit)
                if axis == "scan":
                    scan = scan + step
                else:
                    col = col + step
        return (scan, col)

    def greet(self, groups):
        barrier = pltpu.get_barrier_semaphore()
        partners = [self.partner(group, flips) for group in groups for flips in range(1, 1 << len(group))]

        def signal(device):
            pl.semaphore_signal(barrier, inc=1, device_id=device, device_id_type=pl.DeviceIdType.MESH)

        for device in partners:
            signal(device)
        for device, there in self.sides():
            pl.when(there)(functools.partial(signal, device))
        present = [there.astype(jnp.int32) for _, there in self.sides()]
        pl.semaphore_wait(barrier, len(partners) + sum(present))


class Stream:
    def __init__(self, place, order, base, count, terms, landed, send_sems, recv_sems):
        self.place, self.order = place, order
        self.terms, self.landed = terms, landed
        self.send_sems, self.recv_sems = send_sems, recv_sems
        self.bases, self.counts, self.slots, self.marks = [base], [count], [], []
        self.copies = {}
        slot, mark = base, 0
        for group in order:
            members = 1 << len(group)
            part = self.counts[-1] // members
            self.bases.append(self.bases[-1] + place.index(group, 0) * part)
            self.counts.append(part)
            self.slots.append(slot)
            self.marks.append(mark)
            slot += part * (members - 1)
            mark += members - 1
        self.total = mark

    def flips(self, s):
        return range(1, 1 << len(self.order[s]))

    def scatter(self, s):
        part = self.counts[s + 1]
        for flips in self.flips(s):
            group = self.order[s]
            source = self.terms.at[pl.ds(self.bases[s] + self.place.index(group, flips) * part, part)]
            target = self.landed.at[pl.ds(self.slots[s] + (flips - 1) * part, part)]
            at = self.marks[s] + flips - 1
            copy = reach(
                self.place.partner(group, flips), source, target, self.send_sems.at[at], self.recv_sems.at[at]
            )
            copy.start()
            self.copies["scatter", s, flips] = copy

    def offer(self, grads, mates, first, half):
        group = self.order[0]
        start = (first + self.place.index(group, 1) * half) * 8
        rows = pl.ds(pl.multiple_of(start, 8), half * 8)
        copy = reach(
            self.place.partner(group, 1), grads.at[:, :, rows, :], mates.at[:, :, rows, :],
            self.send_sems.at[0], self.recv_sems.at[0],
        )
        copy.start()
        self.copies["scatter", 0, 1] = copy

    def gathered(self, s):
        part = self.counts[s + 1]
        at = pl.ds(self.bases[s + 1], part)
        value = self.terms[at]
        for flips in self.flips(s):
            self.copies["scatter", s, flips].wait_recv()
            value = value + self.landed[pl.ds(self.slots[s] + (flips - 1) * part, part)]
        return at, value

    def spread(self, s, raised):
        piece = raised.at[pl.ds(self.bases[s + 1], self.counts[s + 1])]
        for flips in self.flips(s):
            at = self.total + self.marks[s] + flips - 1
            copy = reach(
                self.place.partner(self.order[s], flips), piece, piece,
                self.send_sems.at[at], self.recv_sems.at[at],
            )
            copy.start()
            self.copies["gather", s, flips] = copy

    def arrived(self, s):
        for flips in self.flips(s):
            self.copies["gather", s, flips].wait_recv()

    def leave(self):
        for copy in self.copies.values():
            copy.wait_send()


class Halo:
    def __init__(self, place, wide, tiles, width, send_sems, recv_sems):
        rows = tiles // CHUNKS
        near, far = pl.ds(0, width), pl.ds(width, width)
        self.up, self.side, self.corner = [], [], []
        for q in range(CHUNKS):
            top, low = pl.ds(q * rows, rows), pl.ds(tiles + q * rows, rows)
            self.up.append(Shift(
                reach(place.up, wide.at[:, top, :, near], wide.at[:, low, :, near], send_sems.at[0, q], recv_sems.at[0, q]),
                place.has_up, place.has_down,
            ))
            self.side.append(Shift(
                reach(place.left, wide.at[:, top, :, near], wide.at[:, top, :, far], send_sems.at[1, q], recv_sems.at[1, q]),
                place.has_left, place.has_right,
            ))
            self.corner.append(Shift(
                reach(place.left, wide.at[:, low, :, near], wide.at[:, low, :, far], send_sems.at[2, q], recv_sems.at[2, q]),
                place.has_left, place.has_right,
            ))

    def begin(self, q):
        self.up[q].start()
        self.side[q].start()

    def turn(self, q):
        self.up[q].arrive()
        self.corner[q].start()

    def end(self):
        for shift in self.side + self.corner:
            shift.arrive()

    def leave(self):
        for shift in self.up + self.side + self.corner:
            shift.leave()


def step_kernel(
    scan_count, col_count, mode_count, root_total,
    count, positions, first_weights, field, far_amplitudes, far_modes, far_rows, far_cols,
    new_object, last_raised, factors, new_weights,
    amplitudes, first_modes, rows_table, cols_table, input_sems,
    wide, totals, held, den, powers, probes, grads, mates, given, taken, terms, landed, raised, middle_modes, middle_weights,
    sideways, fallen, bottom,
    stream_send, stream_recv, halo_send, halo_recv, side_send, side_recv,
):
    tiles, _, width = field.shape[1:]
    height = 8 * tiles
    frames, length = amplitudes.shape[:2]
    planes = 2 * mode_count
    blocks = length // 8
    units = blocks * planes
    pixels = float(length * length)
    full_width = width + length
    rows_of_chunk = tiles // CHUNKS
    place = Place(scan_count, col_count)
    near, far = pl.ds(0, width), pl.ds(width, width)
    top, low = pl.ds(0, tiles), pl.ds(tiles, tiles)
    pairs = [(i, j) for j in range(mode_count) for i in range(j + 1)]
    strict = [(i, j) for i, j in pairs if i < j]
    leaving = []
    ups = [raised.at[i] for i in range(ITERS - 1)] + [last_raised]

    def chunk(q, offset=0):
        return pl.ds(offset + q * rows_of_chunk, rows_of_chunk)

    def block_rows(block):
        return pl.ds(pl.multiple_of(block * 8, 8), 8)

    loads = [
        pltpu.make_async_copy(source, target, input_sems.at[n])
        for n, (source, target) in enumerate((
            (far_modes, first_modes), (far_rows, rows_table), (far_cols, cols_table), (far_amplitudes, amplitudes),
        ))
    ]
    for load in loads:
        load.start()

    wide[0, :, :tiles, :, :width] = field[...]

    @pl.when(jnp.logical_not(place.has_left))
    def _():
        sideways[...] = jnp.zeros_like(sideways)

    @pl.when(jnp.logical_not(place.has_up))
    def _():
        fallen[...] = jnp.zeros_like(fallen)

    for slot, there in ((1, place.has_left), (2, place.has_up), (3, place.has_before)):

        @pl.when(jnp.logical_not(there))
        def _():
            for i in range(ITERS):
                taken[i, slot] = jnp.zeros(taken.shape[2:], jnp.float32)

    orders = stream_orders(scan_count, col_count, units)
    place.greet(orders[0])
    halos = [
        Halo(place, wide.at[i], tiles, width, halo_send.at[i], halo_recv.at[i]) for i in range(ITERS)
    ]
    for q in range(CHUNKS):
        halos[0].begin(q)
    def live(slot):
        return slot < count[0]

    def inside(value, limit):
        return jnp.minimum(jnp.maximum(value, 0), limit - 1)

    corners = [
        (
            inside(positions[g, 0] - place.scan * height, height),
            inside(positions[g, 1] - place.col * width, width),
        )
        for g in range(frames)
    ]

    def turned(piece, row, col):
        return pltpu.roll(pltpu.roll(piece, row, 0), col, 1)

    def hold(plane, slot, piece):
        row, col = corners[slot]
        held[plane, slot] = turned(piece, row, col).reshape(tiles, 8, width)

    lanes = lax.broadcasted_iota(jnp.int32, (8, width), 1)
    sublanes = lax.broadcasted_iota(jnp.int32, (8, width), 0)

    def settle(i):
        def move(n, carry):
            for plane in range(2):
                quarters = [0.0] * 4
                for g in range(frames):
                    row, col = corners[g]
                    value = held[plane, g, n]
                    below, beyond = sublanes + 8 * n < row, lanes < col
                    upper, lower = jnp.where(below, 0.0, value), jnp.where(below, value, 0.0)
                    for at, half in ((0, upper), (2, lower)):
                        quarters[at] += jnp.where(beyond, 0.0, half)
                        quarters[at + 1] += jnp.where(beyond, half, 0.0)
                totals[i, plane, n, :, :width] = quarters[0]
                totals[i, plane, n, :, width:] = quarters[1]
                totals[i, plane, tiles + n, :, :width] = quarters[2]
                totals[i, plane, tiles + n, :, width:] = quarters[3]
            return carry

        lax.fori_loop(0, tiles, move, 0, unroll=8)

    def cut(i, plane, slot):
        row, col = corners[slot]
        picked = []
        for n in range(tiles):
            below, beyond = sublanes + 8 * n < row, lanes < col
            upper, lower = wide[i, plane, n], wide[i, plane, tiles + n]
            left = jnp.where(below, lower[:, :width], upper[:, :width])
            right = jnp.where(below, lower[:, width:], upper[:, width:])
            picked.append(jnp.where(beyond, right, left))
        return turned(
            jnp.concatenate(picked, 0), lax.rem(height - row, height), lax.rem(width - col, width)
        )

    def masked(weights):
        table = [[weights[g:g + 1, k:k + 1] for k in range(mode_count)] for g in range(frames)]
        return [[jnp.where(live(g), w, 0.0) for w in row] for g, row in enumerate(table)]

    def wave(weights, tiles):
        out = []
        for g in range(frames):
            for part in range(2):
                value = weights[g][0] * tiles[part]
                for k in range(1, mode_count):
                    value = value + weights[g][k] * tiles[2 * k + part]
                out.append(value)
        return out

    def fold(value):
        total = value[:, :128]
        for at in range(128, length, 128):
            total = total + value[:, at:at + 128]
        return total

    def whole(value):
        return jnp.sum(jnp.sum(value, 0, keepdims=True), 1, keepdims=True)

    def run_frame(i, g):
        object_real = cut(i, 0, g)
        object_imag = cut(i, 1, g)
        probe_real, probe_imag = probes[g, 0], probes[g, 1]
        exit_real = probe_real * object_real - probe_imag * object_imag
        exit_imag = probe_real * object_imag + probe_imag * object_real
        stacked = jnp.concatenate([exit_real, exit_imag], 0).astype(jnp.bfloat16)
        far_field = apply_transform(stacked, rows_table[...], cols_table[...])
        far_real, far_imag = far_field[:, :length], far_field[:, length:]
        inverse_size = lax.rsqrt(far_real * far_real + far_imag * far_imag)
        factor = amplitudes[g].astype(jnp.float32) * jnp.minimum(inverse_size, 2.0)
        scaled = jnp.concatenate([far_real * factor, far_imag * factor], 0).astype(jnp.bfloat16)
        back = apply_transform(scaled, cols_table[...], rows_table[...])
        diff_real = back[:, :length] - exit_real
        diff_imag = back[:, length:] - exit_imag
        grads[i, g, 0] = object_real * diff_real + object_imag * diff_imag
        grads[i, g, 1] = object_real * diff_imag - object_imag * diff_real
        hold(0, g, probe_real * diff_real + probe_imag * diff_imag)
        hold(1, g, probe_real * diff_imag - probe_imag * diff_real)

    weights = masked(first_weights)
    mate = place.partner(orders[0][0], 1)

    def tell(i):
        for g in range(frames):
            for k in range(mode_count):
                given[i, g:g + 1, k:k + 1] = weights[g][k]
            for at, value in enumerate(corners[g]):
                given[i, g:g + 1, mode_count + at:mode_count + at + 1] = jnp.full((1, 1), value, jnp.int32).astype(jnp.float32)
        for telling in tellings[i]:
            telling.start()

    def telling_to(i, slot, device, sends, receives):
        at = 3 * CHUNKS + slot
        return Shift(
            reach(device, given.at[i], taken.at[i, slot], side_send.at[i, at], side_recv.at[i, at]), sends, receives
        )

    always = place.col >= 0
    tellings = [
        [
            telling_to(i, 0, mate, always, always),
            telling_to(i, 1, place.right, place.has_right, place.has_left),
            telling_to(i, 2, place.down, place.has_down, place.has_up),
            telling_to(i, 3, place.beyond, place.has_beyond, place.has_before),
        ]
        for i in range(ITERS)
    ]
    tell(0)

    def first_wave(block, carry):
        rows = block_rows(block)
        values = wave(weights, [first_modes[p, rows, :] for p in range(planes)])
        for at, value in enumerate(values):
            probes[at // 2, at % 2, rows, :] = value
        return carry

    loads[0].wait()
    lax.fori_loop(0, blocks, first_wave, 0, unroll=4)
    for load in loads[1:]:
        load.wait()

    for i in range(ITERS):
        again = i < ITERS - 1
        modes = first_modes if i == 0 else middle_modes
        kept_weights = first_weights if i == 0 else middle_weights

        def rightward(at, source, target):
            copy = reach(place.right, source, target, side_send.at[i, at], side_recv.at[i, at])
            return Shift(copy, place.has_right, place.has_left)

        def downward(at, source, target):
            copy = reach(place.down, source, target, side_send.at[i, at], side_recv.at[i, at])
            return Shift(copy, place.has_down, place.has_up)

        pair = pl.ds(0, 2)
        low_rights = [
            rightward(q, totals.at[i, pair, chunk(q, tiles), :, far], sideways.at[i, pair, chunk(q, tiles)])
            for q in range(CHUNKS)
        ]
        top_rights = [
            rightward(CHUNKS + q, totals.at[i, pair, chunk(q), :, far], sideways.at[i, pair, chunk(q)])
            for q in range(CHUNKS)
        ]
        downs = [
            downward(2 * CHUNKS + q, bottom.at[i, pair, chunk(q)], fallen.at[i, pair, chunk(q)])
            for q in range(CHUNKS)
        ]
        leaving += low_rights + top_rights + downs

        if i == 0:
            for q in range(CHUNKS):
                halos[0].turn(q)
        halos[i].end()
        for g in range(frames):
            run_frame(i, g)
        settle(i)
        for q in range(CHUNKS):
            low_rights[q].start()

        stages = len(orders[0])
        share = units // len(orders)
        streams = [
            Stream(
                place, order, t * share, share, terms.at[i], landed.at[i],
                stream_send.at[i, t], stream_recv.at[i, t],
            )
            for t, order in enumerate(orders)
        ]
        leaving += streams

        def term_step(block, carry):
            rows = block_rows(block)
            tiles_ = [ref[i, g, part, rows, :] for ref in (grads, mates) for g in range(frames) for part in range(2)]
            for k in range(mode_count):
                for part in range(2):
                    value = joint[0][k] * tiles_[part]
                    for g in range(1, 2 * frames):
                        value = value + joint[g][k] * tiles_[2 * g + part]
                    terms[i, block * planes + 2 * k + part] = value
            return carry

        half = share // planes // 2
        for t, stream in enumerate(streams):
            stream.offer(grads.at[i], mates.at[i], t * 2 * half, half)
        for q in range(CHUNKS):
            top_rights[q].start()

        for telling in tellings[i]:
            telling.arrive()
        joint = weights + [[taken[i, 0, g:g + 1, k:k + 1] for k in range(mode_count)] for g in range(frames)]
        joint = [[jnp.broadcast_to(w, (8, length)) for w in row] for row in joint]

        def finish_scatter(t, s):
            stream = streams[t]
            if s == 0:
                stream.copies["scatter", 0, 1].wait_recv()
                first = stream.bases[1] // planes
                lax.fori_loop(0, half, lambda n, carry: term_step(first + n, carry), 0, unroll=min(half, 4))
                stream.scatter(1)
                return
            at, value = stream.gathered(s)
            if s < stages - 1:
                terms[i, at] = value
                stream.scatter(s + 1)
                return
            first, target = stream.bases[s + 1], ups[i]
            for n in range(stream.counts[s + 1]):
                unit = first + n
                kept = modes[unit % planes, block_rows(unit // planes), :]
                target[unit] = kept + value[n] / root_total
            stream.spread(s, ups[i])

        sums = [jnp.zeros((8, 128), jnp.float32)] * (len(pairs) + len(strict) + 2 * mode_count * frames)

        def fit_step(block, sums):
            rows = block_rows(block)
            tiles = [ups[i][block * planes + p] for p in range(planes)]
            real, imag = tiles[0::2], tiles[1::2]
            terms_ = [fold(real[a] * real[b] + imag[a] * imag[b]) for a, b in pairs]
            terms_ += [fold(real[a] * imag[b] - imag[a] * real[b]) for a, b in strict]
            for g in range(frames):
                held_real = probes[g, 0, rows, :] + 0.5 * grads[i, g, 0, rows, :]
                held_imag = probes[g, 1, rows, :] + 0.5 * grads[i, g, 1, rows, :]
                for a in range(mode_count):
                    terms_.append(fold(real[a] * held_real + imag[a] * held_imag))
                    terms_.append(fold(real[a] * held_imag - imag[a] * held_real))
            return tuple(a + b for a, b in zip(sums, terms_))

        def finish_gather(t, s):
            nonlocal sums
            streams[t].arrived(s)
            if s > 0:
                streams[t].spread(s - 1, ups[i])
            else:
                per = share // planes
                sums = lax.fori_loop(t * per, (t + 1) * per, fit_step, tuple(sums), unroll=4)

        def drop(q):
            low_rights[q].arrive()
            bottom[i, :2, chunk(q)] = totals[i, :2, chunk(q, tiles), :, near] + sideways[i, :2, chunk(q, tiles)]
            downs[q].start()

        def renew(q):
            top_rights[q].arrive()
            downs[q].arrive()
            update = [
                totals[i, p, chunk(q), :, near] + sideways[i, p, chunk(q)] + fallen[i, p, chunk(q)]
                for p in range(2)
            ]
            scale = 1.0 / (den[chunk(q)] + 1.0)
            for p in range(2):
                value = wide[i, p, chunk(q), :, near] + update[p] * scale
                if again:
                    wide[i + 1, p, chunk(q), :, near] = value
                else:
                    new_object[p, chunk(q)] = value
            if again:
                halos[i + 1].begin(q)

        def weigh():
            near_weights = [
                [
                    [jnp.broadcast_to(taken[i, slot, g:g + 1, k:k + 1], (8, length)) for k in range(mode_count)]
                    for g in range(frames)
                ]
                for slot in range(1, 4)
            ]

            def power_step(block, carry):
                rows = block_rows(block)
                tiles_ = [modes[p, rows, :] for p in range(planes)]
                values = [probes[g, part, rows, :] for g in range(frames) for part in range(2)]
                for weights_ in near_weights:
                    values += wave(weights_, tiles_)
                for n in range(4 * frames):
                    real, imag = values[2 * n], values[2 * n + 1]
                    powers[n // frames, n % frames, rows, :] = real * real + imag * imag
                return carry

            lax.fori_loop(0, blocks, power_step, 0, unroll=4)
            spots = [list(corners)]
            for slot in range(1, 4):
                spots.append([
                    tuple(
                        inside(jnp.sum(taken[i, slot, g:g + 1, at:at + 1]).astype(jnp.int32), limit)
                        for at, limit in ((mode_count, height), (mode_count + 1, width))
                    )
                    for g in range(frames)
                ])
            for slot in range(4):
                for g in range(frames):
                    powers[slot, g] = turned(powers[slot, g], *spots[slot][g])

            def den_step(n, carry):
                rows = block_rows(n)
                total = 0.0
                for slot in range(4):
                    for g in range(frames):
                        row, col = spots[slot][g]
                        below, beyond = sublanes + 8 * n < row, lanes < col
                        if slot < 2:
                            below = jnp.logical_not(below)
                        if slot % 2 == 0:
                            beyond = jnp.logical_not(beyond)
                        total = total + jnp.where(jnp.logical_and(below, beyond), powers[slot, g, rows, :], 0.0)
                den[n] = total
                return carry

            lax.fori_loop(0, tiles, den_step, 0, unroll=4)

        def turn(q):
            if again:
                halos[i + 1].turn(q)

        steps = [functools.partial(finish_scatter, t, s) for s in range(stages) for t in range(len(streams))]
        steps += [
            functools.partial(finish_gather, t, s)
            for s in range(stages - 1, -1, -1) for t in range(len(streams))
        ]
        drops, turns = (4, 4, 5, 5, 6, 6, 7, 7), (13, 14, 15, 16, 17, 18, 19, 20)
        renews = (9, 10, 11, 12, 13, 14, 15, 16) if again else (13, 14, 15, 16, 18, 20, 21, 22)
        marks = [(drop, drops), (renew, renews), (turn, turns)]
        for n, step in enumerate(steps):
            if n == len(steps) * 6 // 32:
                weigh()
            for task, whens in marks:
                for q, when in enumerate(whens):
                    if when * len(steps) // 32 == n:
                        task(q)
            step()

        column = jnp.sum(jnp.concatenate([jnp.sum(s, 0, keepdims=True) for s in sums], 0), 1, keepdims=True) / pixels
        totals_of = [column[n:n + 1] for n in range(len(sums))]
        gram_real = dict(zip(pairs, totals_of))
        gram_imag = dict(zip(strict, totals_of[len(pairs):]))
        upper_real, upper_imag = {}, {}
        for b in range(mode_count):
            for a in range(b):
                sum_real, sum_imag = gram_real[a, b], gram_imag[a, b]
                for k in range(a):
                    r, s, u, v = upper_real[k, a], upper_imag[k, a], upper_real[k, b], upper_imag[k, b]
                    sum_real = sum_real - (r * u + s * v)
                    sum_imag = sum_imag - (r * v - s * u)
                upper_real[a, b] = sum_real / upper_real[a, a]
                upper_imag[a, b] = sum_imag / upper_real[a, a]
            diagonal = gram_real[b, b]
            for k in range(b):
                diagonal = diagonal - (upper_real[k, b] * upper_real[k, b] + upper_imag[k, b] * upper_imag[k, b])
            upper_real[b, b] = jnp.sqrt(diagonal)
        inverse = {b: 1.0 / upper_real[b, b] for b in range(mode_count)}

        refit_weights = []
        at = len(pairs) + len(strict)
        for g in range(frames):
            inner = []
            for k in range(mode_count):
                real, imag = totals_of[at], totals_of[at + 1]
                at += 2
                for a in range(k):
                    r, s, u, v = upper_real[a, k], upper_imag[a, k], inner[a][0], inner[a][1]
                    real = real - (r * u + s * v)
                    imag = imag - (r * v - s * u)
                inner.append((real * inverse[k], imag * inverse[k]))
            refit_weights.append([
                jnp.where(live(g), inner[k][0], kept_weights[g:g + 1, k:k + 1]) for k in range(mode_count)
            ])
        target_weights = middle_weights if again else new_weights
        for g in range(frames):
            for k in range(mode_count):
                target_weights[g:g + 1, k:k + 1] = refit_weights[g][k]
        weights = [[jnp.where(live(g), w, 0.0) for w in row] for g, row in enumerate(refit_weights)]
        if again:
            tell(i + 1)

        def spread_out(value):
            return jnp.broadcast_to(value, (8, length))

        upper_real = {p: spread_out(v) for p, v in upper_real.items() if p[0] < p[1]}
        upper_imag = {p: spread_out(v) for p, v in upper_imag.items()}
        inverse = {p: spread_out(v) for p, v in inverse.items()}
        wave_weights = [[spread_out(w) for w in row] for row in weights]

        def basis_step(block, carry):
            rows = block_rows(block)
            basis = []
            for b in range(mode_count):
                real, imag = ups[i][block * planes + 2 * b], ups[i][block * planes + 2 * b + 1]
                for a in range(b):
                    r, s = upper_real[a, b], upper_imag[a, b]
                    u, v = basis[2 * a], basis[2 * a + 1]
                    real = real - (r * u - s * v)
                    imag = imag - (r * v + s * u)
                basis += [real * inverse[b], imag * inverse[b]]
            for p in range(planes):
                middle_modes[p, rows, :] = basis[p]
            for n, value in enumerate(wave(wave_weights, basis)):
                probes[n // 2, n % 2, rows, :] = value
            return carry

        if again:
            lax.fori_loop(0, blocks, basis_step, 0, unroll=8)
        else:
            rows_ = [inverse[b] for b in range(mode_count)]
            rows_ += [upper_real[p] for p in strict] + [upper_imag[p] for p in strict]
            for n, row in enumerate(rows_):
                factors[n] = row

    for item in leaving + halos:
        item.leave()
    for telling in sum(tellings, []):
        telling.leave()


def finish_kernel(mode_count, settled, rotated, factors, kept_weights, new_object, new_modes, new_weights):
    planes = 2 * mode_count
    pairs = [(i, j) for j in range(mode_count) for i in range(j)]
    new_object[...] = settled[...]
    new_weights[...] = kept_weights[...]
    inverse = [factors[b] for b in range(mode_count)]
    upper_real = {p: factors[mode_count + n] for n, p in enumerate(pairs)}
    upper_imag = {p: factors[mode_count + len(pairs) + n] for n, p in enumerate(pairs)}
    for block in range(rotated.shape[0] // planes):
        basis = []
        for b in range(mode_count):
            real, imag = rotated[block * planes + 2 * b], rotated[block * planes + 2 * b + 1]
            for a in range(b):
                r, s = upper_real[a, b], upper_imag[a, b]
                u, v = basis[2 * a], basis[2 * a + 1]
                real = real - (r * u - s * v)
                imag = imag - (r * v + s * u)
            basis += [real * inverse[b], imag * inverse[b]]
        for p in range(planes):
            new_modes[p, block * 8:block * 8 + 8, :] = basis[p]


def shape(*dims):
    return jax.ShapeDtypeStruct(dims, jnp.float32)


def on_device(object_field, amplitudes, positions, frame_count, coefficients, probe_modes):
    frames, length = amplitudes.shape[:2]
    mode_count = probe_modes.shape[0]
    planes = 2 * mode_count
    height, width = object_field.shape[1:]
    scan_count = lax.axis_size("scan")
    col_count = lax.axis_size("col")
    root_total = math.sqrt(frames * scan_count * col_count)
    rows_table, cols_table = make_tables(length)
    tiles, blocks = height // 8, length // 8
    full_width = width + length
    units = planes * blocks
    orders = stream_orders(scan_count, col_count, units)
    partners = 2 * sum((1 << len(group)) - 1 for group in orders[0])

    def vmem(*dims):
        return pltpu.VMEM(dims, jnp.float32)

    stream_sems = pltpu.SemaphoreType.DMA((ITERS, len(orders), partners))
    halo_sems = pltpu.SemaphoreType.DMA((ITERS, 3, CHUNKS))
    side_sems = pltpu.SemaphoreType.DMA((ITERS, 3 * CHUNKS + 4))
    settled, rotated, factors, kept = pl.pallas_call(
        functools.partial(step_kernel, scan_count, col_count, mode_count, root_total),
        name="reconstruct",
        out_shape=(
            shape(2, tiles, 8, width), shape(units, 8, length), shape(mode_count * mode_count, 8, length),
            shape(frames, mode_count),
        ),
        in_specs=[SMEM] * 2 + [VMEM] * 2 + [ANY] * 4,
        out_specs=(VMEM,) * 4,
        scratch_shapes=[
            pltpu.VMEM(amplitudes.shape, amplitudes.dtype),
            vmem(planes, length, length),
            pltpu.VMEM(rows_table.shape, rows_table.dtype),
            pltpu.VMEM(cols_table.shape, cols_table.dtype),
            pltpu.SemaphoreType.DMA((4,)),
            vmem(ITERS, 2, tiles + blocks, 8, full_width),
            vmem(ITERS, 2, tiles + blocks, 8, full_width),
            vmem(2, frames, tiles, 8, width),
            vmem(tiles, 8, width),
            vmem(4, frames, length, length),
            vmem(frames, 2, length, length),
            vmem(ITERS, frames, 2, length, length),
            vmem(ITERS, frames, 2, length, length),
            vmem(ITERS, frames, mode_count + 2),
            vmem(ITERS, 4, frames, mode_count + 2),
            vmem(ITERS, units, 8, length),
            vmem(ITERS, units, 8, length),
            vmem(ITERS - 1, units, 8, length),
            vmem(planes, length, length),
            vmem(frames, mode_count),
            vmem(ITERS, 2, tiles + blocks, 8, width),
            vmem(ITERS, 2, tiles, 8, width),
            vmem(ITERS, 2, tiles, 8, width),
            stream_sems, stream_sems, halo_sems, halo_sems, side_sems, side_sems,
        ],
        compiler_params=pltpu.CompilerParams(
            collective_id=0, has_side_effects=True, vmem_limit_bytes=60 * 2**20
        ),
        cost_estimate=pl.CostEstimate(flops=5 * 10**9, bytes_accessed=10**7, transcendentals=0),
    )(
        frame_count, positions, coefficients, object_field.reshape(2, tiles, 8, width), amplitudes,
        probe_modes.reshape(planes, length, length), rows_table, cols_table,
    )
    parts = 2
    new_object, modes, weights = pl.pallas_call(
        functools.partial(finish_kernel, mode_count),
        name="finish",
        grid=(parts,),
        out_shape=(shape(2, tiles, 8, width), shape(planes, length, length), shape(frames, mode_count)),
        in_specs=[
            pl.BlockSpec((2, tiles // parts, 8, width), lambda n: (0, n, 0, 0)),
            pl.BlockSpec((units // parts, 8, length), lambda n: (n, 0, 0)),
            pl.BlockSpec(factors.shape, lambda n: (0, 0, 0)),
            pl.BlockSpec(kept.shape, lambda n: (0, 0)),
        ],
        out_specs=(
            pl.BlockSpec((2, tiles // parts, 8, width), lambda n: (0, n, 0, 0)),
            pl.BlockSpec((planes, length // parts, length), lambda n: (0, n, 0)),
            pl.BlockSpec(kept.shape, lambda n: (0, 0)),
        ),
    )(settled, rotated, factors, kept)
    return (new_object.reshape(object_field.shape), modes.reshape(probe_modes.shape), weights)


def solution(mesh):
    placed = (
        P(None, "scan", "col"),
        P(("scan", "col"), None, None),
        P(("scan", "col"), None),
        P(("scan", "col")),
        P(("scan", "col"), None),
        P(),
    )
    return jax.shard_map(
        on_device,
        mesh=mesh,
        in_specs=placed,
        out_specs=(P(None, "scan", "col"), P(), P(("scan", "col"), None)),
        check_vma=False,
    )
```
